128 devices in a mesh: gz: 16 (over x, y), gy: 8 (over z, core).
Axes of the slice: x: 4, y: 4, z: 4, core: 2. Of those that a mesh axis runs over, the one named last changes fastest.
Arguments:
- applied_load: float32 [3, 128, 64, 512], P(None, 'gz', 'gy'), may hold values from -12 to 12
- start_field: float32 [3, 128, 64, 512], P(None, 'gz', 'gy'), may hold values from -2 to 2
- bone_mask: int32 [128, 64, 512], P('gz', 'gy'), may hold values 0 or 1
- element_stiffness: bfloat16 [24, 24], replicated, may hold values from -1.5 to 2, as said below
Outputs:
- corrected: float32 [3, 128, 64, 512], P(None, 'gz', 'gy')
The draws below stay inside these ranges and needn't reach their ends.
Inputs may be any that keep to these rules, and one draw needn't show every extreme that they name: element_stiffness is symmetric and positive definite, and each of its diagonal entries is at least 0.125.
All inputs are finite; a program needn't handle non-finite values. No bound on the sum of `bone_mask` on one device may be relied on, other than what follows from the above.
Results may differ from the reference program's by a relative error of at most 0.0059.
Values may be sent and summed in bfloat16 or wider, within the bound.
No kernel may reach another device: no remote copies, remote signals or barrier semaphores. Data moves between devices by JAX's collectives and lax.ppermute only.
A program may use at most 64 MiB of HBM per device.

```python
import math
import jax
import jax.numpy as jnp
from jax import lax

DOF = 3
EDOF = 24
CHEB = 3
NX = 512
NZ = 128
NY = 64


def draw_element_stiffness(key, part):
    first_key = jax.random.fold_in(key, 0)
    third_key = jax.random.fold_in(key, 2)
    factors = jax.random.truncated_normal(first_key, -3.0, 3.0, (EDOF, EDOF), jnp.float32)
    shared = jax.random.uniform(third_key, (EDOF,), jnp.float32, 0.4, 1.0)
    gram = jnp.dot(factors, factors.T, precision=lax.Precision.HIGHEST) / (8.0 * EDOF)
    gram = 0.5 * (gram + gram.T)
    matrix = gram + 0.5 * shared[:, None] * shared[None, :] + 0.125 * jnp.eye(EDOF, dtype=jnp.float32)
    return matrix.astype(jnp.bfloat16)


def draw_start_field(key, part):
    freq_key, phase_key, amp_key, noise_key = jax.random.split(key, 4)
    freqs = jax.random.uniform(freq_key, (DOF, 3), jnp.float32, 0.5, 2.0)
    phases = jax.random.uniform(phase_key, (DOF, 3), jnp.float32, 0.0, 1.0)
    depth = jnp.arange(NZ, dtype=jnp.float32) / NZ
    rows = jnp.arange(NY, dtype=jnp.float32) / NY
    cols = jnp.arange(NX, dtype=jnp.float32) / NX
    wave_z = jnp.cos(2.0 * math.pi * (freqs[:, 0:1] * depth[None, :] + phases[:, 0:1]))
    wave_y = jnp.cos(2.0 * math.pi * (freqs[:, 1:2] * rows[None, :] + phases[:, 1:2]))
    wave_x = jnp.cos(2.0 * math.pi * (freqs[:, 2:3] * cols[None, :] + phases[:, 2:3]))
    smooth = 0.6 + 0.4 * wave_z[:, :, None, None] * wave_y[:, None, :, None] * wave_x[:, None, None, :]
    signs = jnp.where(jnp.arange(DOF) % 2 == 1, -1.0, 1.0).astype(jnp.float32)
    amps = jax.random.uniform(amp_key, (DOF,), jnp.float32, 0.5, 1.0)
    noise = 0.35 * jax.random.truncated_normal(noise_key, -2.8, 2.8, (DOF, NZ, NY, NX), jnp.float32)
    values = (signs * amps)[:, None, None, None] * smooth + noise
    return values.astype(jnp.float32)


def set_ends(array, rng, least, largest):
    index_at = [jax.random.randint(jax.random.fold_in(rng, axis), (), 0, length) for axis, length in enumerate(array.shape)]
    main_axis = array.shape.index(max(array.shape))
    neighbour = index_at[:main_axis] + [(index_at[main_axis] + 1) % array.shape[main_axis]] + index_at[main_axis + 1:]
    return array.at[tuple(index_at)].set(least).at[tuple(neighbour)].set(largest)


def levels(key, dims, cuts, smallest, high):
    def one(position, blocks):
        heights = jax.random.uniform(jax.random.fold_in(jax.random.fold_in(key, 6), position), (blocks,), jnp.float32, smallest / len(cuts), high / len(cuts))
        return jnp.repeat(jnp.exp(heights), dims[position] // blocks).reshape((-1,) + (1,) * (len(dims) - position - 1))

    gain = one(*cuts[0])
    for cut in cuts[1:]:
        gain = gain * one(*cut)
    return gain


def bell_draw(key, dims, scale, limit, shards=(), kind=jnp.bfloat16):
    values = scale * jax.random.normal(key, dims, jnp.float32)
    if shards:
        values = values * levels(key, dims, shards, -0.22, 0.18)
    return jnp.clip(values, -limit, limit).astype(kind)


def setup_inputs(seed: int = 0) -> dict:
    splits = jax.random.split(jax.random.key(seed), 5)
    applied_load = bell_draw(splits[0], (DOF, NZ, NY, NX), 2.0, 12.0, ((1, 16), (2, 8)), jnp.float32)
    start_field = draw_start_field(jax.random.fold_in(splits[4], 71), 0)
    bone_mask = set_ends((jax.random.randint(splits[2], (NZ, NY, NX), 0, 4) < 3).astype(jnp.int32), jax.random.fold_in(splits[2], 1), 0, 1)
    element_stiffness = draw_element_stiffness(jax.random.fold_in(splits[4], 71), 0)
    return dict(applied_load=applied_load, start_field=start_field, bone_mask=bone_mask, element_stiffness=element_stiffness)


corner_offsets = [(0, 0, 0), (0, 0, 1), (0, 1, 0), (0, 1, 1), (1, 0, 0), (1, 0, 1), (1, 1, 0), (1, 1, 1)]
low_ratio = 0.1


def scatter_full(terms):
    summed = None
    for offset, piece in zip(corner_offsets, terms):
        padded = jnp.pad(piece, ((0, 0), (offset[0], 1 - offset[0]), (offset[1], 1 - offset[1]), (offset[2], 1 - offset[2])))
        summed = padded if summed is None else summed + padded
    return summed


def element_global(values_bf, elem_scale, element_stiffness):
    depth_n, rows_n, cols_n = elem_scale.shape
    padded = lax.optimization_barrier(jnp.pad(values_bf, ((0, 0), (0, 1), (0, 1), (0, 1))))
    stiff_wide = element_stiffness.astype(jnp.float32)

    def one_layer(carried, layer_index):
        pair = lax.dynamic_slice_in_dim(padded, layer_index, 2, 1).astype(jnp.float32)
        layer_scale = lax.dynamic_slice_in_dim(elem_scale, layer_index, 1, 0)
        pieces = [pair[:, offset[0]:offset[0] + 1, offset[1]:offset[1] + rows_n, offset[2]:offset[2] + cols_n] for offset in corner_offsets]
        gathered = jnp.concatenate(pieces, axis=0)
        products = jnp.einsum("ij,jzyx->izyx", stiff_wide, gathered) * layer_scale
        summed = scatter_full([products[DOF * corner:DOF * corner + DOF] for corner in range(8)])
        summed = summed.at[:, 0].add(carried)
        return summed[:, 1], summed[:, 0]

    start_carry = jnp.zeros((DOF, rows_n + 1, cols_n + 1), jnp.float32)
    leftover, planes = lax.scan(one_layer, start_carry, jnp.arange(depth_n, dtype=jnp.int32))
    planes = jnp.transpose(planes, (1, 0, 2, 3))
    return planes[:, :, :rows_n, :cols_n]


def diagonal_global(elem_scale, stiff_diag):
    depth_n, rows_n, cols_n = elem_scale.shape
    summed = scatter_full([stiff_diag[corner][:, None, None, None] * elem_scale[None] for corner in range(8)])
    return summed[:, :depth_n, :rows_n, :cols_n]


def prepare_level(elem_scale, element_stiffness, stiff_diag):
    diagonal = diagonal_global(elem_scale, stiff_diag)
    inactive = (diagonal == 0.0).astype(jnp.float32)
    inverse = 1.0 / (diagonal + inactive)

    def operator(values_in):
        return element_global(values_in.astype(jnp.bfloat16), elem_scale, element_stiffness) + inactive * values_in

    return operator, inverse


def chebyshev(operator, rhs_vals, start_vals, inverse, mid_value, half_width):
    ratio_value = (1.0 + low_ratio) / (1.0 - low_ratio)
    rho_prev = 1.0 / ratio_value
    if start_vals is None:
        update = inverse * rhs_vals / mid_value
        current = update
    else:
        update = inverse * (rhs_vals - operator(start_vals)) / mid_value
        current = start_vals + update
    for sweep in range(CHEB - 1):
        rho_next = 1.0 / (2.0 * ratio_value - rho_prev)
        resid_now = rhs_vals - operator(current)
        update = (rho_next * rho_prev) * update + (2.0 * rho_next / half_width) * inverse * resid_now
        current = current + update
        rho_prev = rho_next
    return current


def halve_axis(values_in, axis_pos):
    length = values_in.shape[axis_pos]
    half_len = length // 2
    widths = [(0, 0)] * values_in.ndim
    widths[axis_pos] = (0, 2 * (half_len + 1) - length)
    padded = jnp.pad(values_in, widths)
    shape_new = values_in.shape[:axis_pos] + (half_len + 1, 2) + values_in.shape[axis_pos + 1:]
    pairs = padded.reshape(shape_new)
    even_part = lax.index_in_dim(pairs, 0, axis_pos + 1, keepdims=False)
    odd_part = lax.index_in_dim(pairs, 1, axis_pos + 1, keepdims=False)
    before = jnp.concatenate([jnp.zeros_like(lax.slice_in_dim(odd_part, 0, 1, axis=axis_pos)), lax.slice_in_dim(odd_part, 0, half_len, axis=axis_pos)], axis=axis_pos)
    return even_part + 0.5 * odd_part + 0.5 * before


def double_axis(values_in, axis_pos):
    coarse_len = values_in.shape[axis_pos] - 1
    lower_part = lax.slice_in_dim(values_in, 0, coarse_len, axis=axis_pos)
    upper_part = lax.slice_in_dim(values_in, 1, coarse_len + 1, axis=axis_pos)
    middle = 0.5 * (lower_part + upper_part)
    stacked = jnp.stack([lower_part, middle], axis=axis_pos + 1)
    shape_new = values_in.shape[:axis_pos] + (2 * coarse_len,) + values_in.shape[axis_pos + 1:]
    return stacked.reshape(shape_new)


def reference(applied_load, start_field, bone_mask, element_stiffness):
    stiff_wide = element_stiffness.astype(jnp.float32)
    upper_bound = jnp.max(jnp.sum(jnp.abs(stiff_wide), axis=1) / jnp.diagonal(stiff_wide))
    mid_value = 0.5 * (1.0 + low_ratio) * upper_bound
    half_width = 0.5 * (1.0 - low_ratio) * upper_bound
    stiff_diag = jnp.diagonal(stiff_wide).reshape(8, DOF)
    fine_scale = bone_mask.astype(jnp.float32)
    depth_n, rows_n, cols_n = bone_mask.shape
    coarse_scale = 0.25 * fine_scale.reshape(depth_n // 2, 2, rows_n // 2, 2, cols_n // 2, 2).sum(axis=(1, 3, 5))
    fine_op, fine_inverse = prepare_level(fine_scale, element_stiffness, stiff_diag)
    smoothed = chebyshev(fine_op, applied_load, start_field, fine_inverse, mid_value, half_width)
    residual = applied_load - fine_op(smoothed)
    coarse_rhs = halve_axis(halve_axis(halve_axis(residual, 1), 2), 3)[:, :-1, :-1, :-1]
    coarse_op, coarse_inverse = prepare_level(coarse_scale, element_stiffness, stiff_diag)
    correction = chebyshev(coarse_op, coarse_rhs, None, coarse_inverse, mid_value, half_width).astype(jnp.bfloat16)
    widened = lax.optimization_barrier(jnp.pad(correction, ((0, 0), (0, 1), (0, 1), (0, 1)))).astype(jnp.float32)
    return smoothed + double_axis(double_axis(double_axis(widened, 1), 2), 3)
```

```python
import jax
import jax.numpy as jnp
from jax import lax
from jax.sharding import PartitionSpec as P
from jax.experimental import pallas as pl
from jax.experimental.pallas import tpu as pltpu

F32 = jnp.float32
BF16 = jnp.bfloat16
CHEB = 3
LOW = 0.1
MID = 0.5 * (1.0 + LOW)
HALF = 0.5 * (1.0 - LOW)
RATIO = (1.0 + LOW) / (1.0 - LOW)
ROWS = 16
BAND = 3 * ROWS
DEEP = 4


def iota(shape, dim):
    return lax.broadcasted_iota(jnp.int32, shape, dim)


def build_matrices(stiff):
    m = 4 * BAND
    row_m = iota((m, 24), 0)
    base_row = 12 * (row_m // (2 * BAND)) + 3 * ((row_m // BAND) % 2) + (row_m // ROWS) % 3
    col_e = iota((m, 24), 1)
    row_k = iota((24, m), 0)
    col_k = iota((24, m), 1)
    base_col = 6 * (col_k // (2 * BAND)) + 3 * ((col_k // BAND) % 2) + (col_k // ROWS) % 3
    mm = iota((m, m), 0)
    kk = iota((m, m), 1)
    gap = (mm % ROWS) - (kk % ROWS) + kk // (2 * BAND)
    blocks = []
    left = []
    for cy in range(2):
        pick = (col_e == base_row + 6 * cy).astype(BF16)
        left.append(jnp.dot(pick, stiff, preferred_element_type=F32).astype(BF16))
    for p in range(2):
        pick = (row_k == base_col + 12 * p).astype(BF16)
        block = jnp.zeros((m, m), F32)
        for cy in range(2):
            full = jnp.dot(left[cy], pick, preferred_element_type=F32)
            block = jnp.where(gap == cy, full, block)
        blocks.append(block.astype(BF16))
    md = iota((m, 2 * ROWS), 0)
    kd = iota((m, 2 * ROWS), 1)
    diag = jnp.zeros((m, 2 * ROWS), F32)
    for cy in range(2):
        own = jnp.sum(
            jnp.where(col_e == base_row + 6 * cy, left[cy].astype(F32), 0.0), axis=1, keepdims=True
        )
        diag = jnp.where((kd // ROWS == cy) & (kd % ROWS == md % ROWS), own, diag)
    return jnp.concatenate(blocks, axis=1), diag.astype(BF16)


def spectral_bound(stiff):
    wide = stiff.astype(F32)
    eye = iota((24, 24), 0) == iota((24, 24), 1)
    own = jnp.sum(jnp.where(eye, wide, 0.0), axis=1, keepdims=True)
    total = jnp.sum(jnp.abs(wide), axis=1, keepdims=True)
    return jnp.max(total / own, axis=0, keepdims=True)


def shift_up(values, width):
    rolled = pltpu.roll(values, width - 1, 1)
    return jnp.where(iota(values.shape, 1) == width - 1, 0.0, rolled)


def shift_down(values):
    rolled = pltpu.roll(values, 1, 1)
    return jnp.where(iota(values.shape, 1) == 0, 0.0, rolled)


def put_nodes(v_ref, z, values, width):
    v_ref[z, 0:BAND] = values.astype(BF16)
    v_ref[z, BAND : 2 * BAND] = shift_up(values, width).astype(BF16)


def put_scale(s_ref, layer, scale):
    s_ref[layer, 0:ROWS] = scale.astype(BF16)
    down = pltpu.roll(scale, 1, 0)
    down = jnp.where(iota(scale.shape, 0) == 0, 0.0, down)
    s_ref[layer, ROWS : 2 * ROWS] = down.astype(BF16)


def masked_nodes(v_ref, s_ref, layer, p, width):
    nodes = v_ref[layer + p].reshape(6, ROWS, width)
    parts = [
        (nodes * s_ref[layer, cy * ROWS : (cy + 1) * ROWS][None]).reshape(2 * BAND, width)
        for cy in range(2)
    ]
    return jnp.concatenate(parts, axis=0)


def layer_product(w_ref, v_ref, s_ref, layer, width):
    operand = jnp.concatenate(
        [masked_nodes(v_ref, s_ref, layer, p, width) for p in range(2)], axis=0
    )
    return jnp.dot(w_ref[...], operand, preferred_element_type=F32)


def gather_plane(first, carry_ref, width):
    both = first[0 : 2 * BAND] + carry_ref[...]
    return both[0:BAND] + shift_down(both[BAND : 2 * BAND])


def plane_loop(lo, hi, product, carry_ref, width, use):
    carry_ref[...] = product(lo - 1)[2 * BAND : 4 * BAND]

    def step(z, token):
        both = product(z)
        plane = gather_plane(both, carry_ref, width)
        carry_ref[...] = both[2 * BAND : 4 * BAND]
        use(z, plane)
        return token

    lax.fori_loop(lo, hi + 1, step, 0)


def invert_diagonal(
    lo, hi, wd_ref, s_ref, carry_ref, inv_ref, idle_ref, bound, width, past_z, past_y, first_z, first_y
):
    def product(layer):
        return jnp.dot(wd_ref[...], s_ref[layer], preferred_element_type=F32)

    rows = iota((BAND, width), 0) % ROWS
    keep_y = jnp.where((rows >= first_y) & (past_y == 1), 0.0, 1.0)

    def use(z, diag):
        idle = (diag == 0.0).astype(F32)
        keep_z = jnp.where((z >= first_z) & (past_z == 1), 0.0, 1.0)
        inv_ref[z] = keep_y * keep_z / ((diag + idle) * bound)
        idle_ref[z] = idle[0:ROWS]

    plane_loop(lo, hi, product, carry_ref, width, use)


def tile3(values):
    return jnp.concatenate([values, values, values], axis=0)


def sweep(lo, hi, refs, width, previous, current):
    w_ref, v_ref, s_ref, carry_ref, b_ref, x_ref, u_ref, inv_ref, idle_ref = refs

    def product(layer):
        return layer_product(w_ref, v_ref, s_ref, layer, width)

    def use(z, plane):
        x = x_ref[z]
        r = b_ref[z] - plane - tile3(idle_ref[z]) * x
        update = current * (inv_ref[z] * r)
        if previous is not None:
            update = previous * u_ref[z] + update
        x = x + update
        u_ref[z] = update
        x_ref[z] = x
        put_nodes(v_ref, z, x, width)

    plane_loop(lo, hi, product, carry_ref, width, use)


def chebyshev_factors():
    factors = []
    rho = 1.0 / RATIO
    for _ in range(CHEB - 1):
        nxt = 1.0 / (2.0 * RATIO - rho)
        factors.append((nxt * rho, 2.0 * nxt / HALF))
        rho = nxt
    return factors


def pack_z_kernel(place, x_ref, b_ref, m_ref, q0_ref, q1_ref):
    even = 1 - place[0]
    for out, up in ((q0_ref, even), (q1_ref, 1 - even)):
        for d in range(3):
            out[4 * d : 4 * d + 4] = x_ref[d, pl.ds(4 * up, 4)].astype(BF16)
            out[12 + 3 * d : 15 + 3 * d] = b_ref[d, pl.ds(5 * up, 3)].astype(BF16)
        out[21:25] = m_ref[pl.ds(4 * up, 4)].astype(F32).astype(BF16)


def z_planes(place, x_ref, b_ref, m_ref, r0_ref, r1_ref):
    odd = place[0] == 1

    def low(i):
        return jnp.where(odd, r0_ref[i].astype(F32), r1_ref[i].astype(F32))

    def high(i):
        return jnp.where(odd, r1_ref[i].astype(F32), r0_ref[i].astype(F32))

    def x_at(d, w):
        if w < 4:
            return low(4 * d + w)
        if w >= 12:
            return high(4 * d + w - 12)
        return x_ref[d, w - 4]

    def b_at(d, w):
        if w < 4:
            return low(12 + 3 * d + w - 1)
        if w >= 12:
            return high(12 + 3 * d + w - 12)
        return b_ref[d, w - 4]

    def m_at(w):
        if w < 4:
            return low(21 + w)
        if w >= 12:
            return high(21 + w - 12)
        return m_ref[w - 4].astype(F32)

    return x_at, b_at, m_at


def flip(values):
    return pltpu.roll(values, 4, 0)


def y_fields(x_at, b_at, m_at):
    fields = []
    for d in range(3):
        fields += [(x_at, (d,), w) for w in range(0, 16, 2)]
    for d in range(3):
        fields += [(b_at, (d,), w) for w in range(1, 15, 2)]
    fields += [(m_at, (), w) for w in range(0, 16, 2)]
    return fields


def pack_y_kernel(place, x_ref, b_ref, m_ref, r0_ref, r1_ref, q0_ref, q1_ref):
    even = place[1] == 0
    x_at, b_at, m_at = z_planes(place, x_ref, b_ref, m_ref, r0_ref, r1_ref)
    for index, (at, lead, w) in enumerate(y_fields(x_at, b_at, m_at)):
        a, b = at(*lead, w), at(*lead, w + 1)
        head = iota(a.shape, 0) < 4
        up = jnp.where(head, flip(a), b)
        down = jnp.where(head, a, flip(b))
        q0_ref[index] = jnp.where(even, up, down).astype(BF16)
        q1_ref[index] = jnp.where(even, down, up).astype(BF16)


def restrict_rows():
    out = iota((BAND, BAND), 0)
    src = iota((BAND, BAND), 1)
    gap = jnp.abs((src % ROWS) - 4 - 2 * ((out % ROWS) - 3))
    own = ((src % ROWS) >= 4) & ((src % ROWS) < 12) & (out // ROWS == src // ROWS)
    weight = jnp.where(gap == 0, 1.0, jnp.where(gap == 1, 0.5, 0.0))
    return jnp.where(own, weight, 0.0).astype(BF16)


def halve_rows():
    out = iota((ROWS, ROWS), 0)
    src = iota((ROWS, ROWS), 1)
    own = (src >= 4) & (src < 12) & ((src - 4) // 2 == out - 3)
    return own.astype(F32).astype(BF16)


def split(values):
    high = values.astype(BF16)
    return high, (values - high.astype(F32)).astype(BF16)


def fine_kernel(
    place, e_ref, x_in, b_in, m_in, r0_ref, r1_ref, y0_ref, y1_ref,
    out_ref, rhs_ref, sc_ref, q0_ref, q1_ref,
    w_ref, wd_ref, v_ref, s_ref, carry_ref, b_ref, x_ref, u_ref, inv_ref, idle_ref,
):
    width = x_in.shape[-1]
    stiff = e_ref[...]
    w_ref[...], wd_ref[...] = build_matrices(stiff)
    bound = spectral_bound(stiff)
    odd = place[1] == 1
    x_at, b_at, m_at = z_planes(place, x_in, b_in, m_in, r0_ref, r1_ref)
    head = iota((8, width), 0) < 4

    def windows(at, lead, w, index):
        low = jnp.where(odd, y0_ref[index].astype(F32), y1_ref[index].astype(F32))
        high = jnp.where(odd, y1_ref[index].astype(F32), y0_ref[index].astype(F32))
        both = []
        for k in range(2):
            own = flip(at(*lead, w + k))
            below = low if k == 0 else flip(low)
            above = flip(high) if k == 0 else high
            both.append(
                jnp.concatenate([jnp.where(head, below, own), jnp.where(head, own, above)], axis=0)
            )
        return both

    for index, (at, lead, w) in enumerate(y_fields(x_at, b_at, m_at)):
        for k, block in enumerate(windows(at, lead, w, index)):
            if at is m_at:
                put_scale(s_ref, w + k, block)
            elif at is b_at:
                b_ref[w + k, ROWS * lead[0] : ROWS * (lead[0] + 1)] = block
            else:
                x_ref[w + k, ROWS * lead[0] : ROWS * (lead[0] + 1)] = block

    def spread(z, token):
        put_nodes(v_ref, z, x_ref[z], width)
        return token

    lax.fori_loop(0, 16, spread, 0)
    invert_diagonal(
        1, 14, wd_ref, s_ref, carry_ref, inv_ref, idle_ref, bound, width, place[2], place[3], 12, 12
    )
    refs = (w_ref, v_ref, s_ref, carry_ref, b_ref, x_ref, u_ref, inv_ref, idle_ref)
    (p1, c1), (p2, c2) = chebyshev_factors()
    sweep(1, 14, refs, width, None, 1.0 / MID)
    sweep(2, 13, refs, width, p1, c1)
    sweep(3, 12, refs, width, p2, c2)

    def use(z, plane):
        u_ref[z] = b_ref[z] - plane - tile3(idle_ref[z]) * x_ref[z]

    plane_loop(
        4, 11, lambda layer: layer_product(w_ref, v_ref, s_ref, layer, width), carry_ref, width, use
    )
    for z in range(8):
        for d in range(3):
            a = x_ref[4 + z, ROWS * d : ROWS * d + 8]
            b = x_ref[4 + z, ROWS * d + 8 : ROWS * d + 16]
            out_ref[d, z] = flip(jnp.where(head, b, a))

    half = width // 2
    fine_x = iota((width, half), 0)
    coarse_x = iota((width, half), 1)
    gap = jnp.abs(fine_x - 2 * coarse_x)
    rx = jnp.where(gap == 0, 1.0, jnp.where(gap == 1, 0.5, 0.0)).astype(BF16)
    pair = (fine_x // 2 == coarse_x).astype(F32).astype(BF16)
    ry = restrict_rows()
    sums = []
    for k in range(5):
        total = 0.0
        if k > 0:
            total = 0.5 * u_ref[4 + 2 * k - 1]
        if k < 4:
            total = total + u_ref[4 + 2 * k] + 0.5 * u_ref[4 + 2 * k + 1]
        high, low = split(total)
        rows = jnp.dot(ry, high, preferred_element_type=F32) + jnp.dot(
            ry, low, preferred_element_type=F32
        )
        sums += [rows[ROWS * d : ROWS * d + 8] for d in range(3)]
    high, low = split(jnp.concatenate(sums, axis=0))
    rhs_ref[...] = (
        jnp.dot(high, rx, preferred_element_type=F32) + jnp.dot(low, rx, preferred_element_type=F32)
    ).reshape(15, 8, half)
    hy = halve_rows()
    counts = []
    for k in range(4):
        both = s_ref[4 + 2 * k, 0:ROWS] + s_ref[5 + 2 * k, 0:ROWS]
        counts.append(jnp.dot(hy, both, preferred_element_type=F32)[0:8])
    counts = jnp.concatenate(counts, axis=0).astype(BF16)
    sc_ref[...] = (0.25 * jnp.dot(counts, pair, preferred_element_type=F32)).reshape(4, 8, half)
    even = 1 - place[0]
    for out, up in ((q0_ref, even), (q1_ref, 1 - even)):
        out[0:9] = rhs_ref[pl.ds(6 * up, 9)].astype(BF16)
        out[9:12] = sc_ref[pl.ds(up, 3)].astype(BF16)


def pack_coarse_kernel(place, rhs_ref, sc_ref, r0_ref, r1_ref, full_ref, q_ref):
    odd = place[0] == 1

    def low(i):
        return jnp.where(odd, r0_ref[i].astype(F32), r1_ref[i].astype(F32))

    def high(i):
        return jnp.where(odd, r1_ref[i].astype(F32), r0_ref[i].astype(F32))

    for z in range(10):
        c = z - 3
        for d in range(4):
            value = jnp.zeros(rhs_ref.shape[1:], F32)
            if d < 3:
                if -2 <= c <= 0:
                    value = value + low(3 * (c + 2) + d)
                if 4 <= c <= 6:
                    value = value + high(3 * (c - 4) + d)
                if 0 <= c <= 4:
                    value = value + rhs_ref[3 * c + d]
            else:
                if c <= -1:
                    value = low(9 + c + 3)
                elif c >= 4:
                    value = high(9 + c - 4)
                else:
                    value = sc_ref[c]
            full_ref[4 * z + d] = value
            q_ref[4 * z + d] = value.astype(BF16)


def coarse_kernel(
    place, e_ref, full_ref, y0_ref, y1_ref, smooth_ref, out_ref,
    w_ref, wd_ref, v_ref, s_ref, carry_ref, b_ref, x_ref, u_ref, inv_ref, idle_ref,
):
    half = full_ref.shape[-1]
    width = 2 * half
    stiff = e_ref[...]
    w_ref[...], wd_ref[...] = build_matrices(stiff)
    bound = spectral_bound(stiff)
    odd = place[1] == 1
    rows8 = iota((8, half), 0)
    for z in range(10):
        for d in range(4):
            i = 4 * z + d
            low = jnp.where(odd, y0_ref[i].astype(F32), y1_ref[i].astype(F32))
            high = jnp.where(odd, y1_ref[i].astype(F32), y0_ref[i].astype(F32))
            low, high = flip(low), flip(high)
            first = (
                full_ref[i] + jnp.where(rows8 < 4, low, 0.0) + jnp.where(rows8 == 7, high, 0.0)
            )
            block = jnp.concatenate([first, jnp.where(rows8 < 4, high, 0.0)], axis=0)
            if d < 3:
                b_ref[z, ROWS * d : ROWS * (d + 1)] = block
            else:
                put_scale(s_ref, z, block)
    invert_diagonal(
        1, 9, wd_ref, s_ref, carry_ref, inv_ref, idle_ref, bound, half, place[2], place[3], 7, 7
    )

    def first_step(z, token):
        update = (1.0 / MID) * (inv_ref[z] * b_ref[z])
        u_ref[z] = update
        x_ref[z] = update
        put_nodes(v_ref, z, update, half)
        return token

    lax.fori_loop(1, 10, first_step, 0)
    refs = (w_ref, v_ref, s_ref, carry_ref, b_ref, x_ref, u_ref, inv_ref, idle_ref)
    (p1, c1), (p2, c2) = chebyshev_factors()
    sweep(2, 8, refs, half, p1, c1)
    sweep(3, 7, refs, half, p2, c2)

    coarse_x = iota((half, width), 0)
    fine_x = iota((half, width), 1)
    gap = jnp.abs(fine_x - 2 * coarse_x)
    px = jnp.where(gap == 0, 1.0, jnp.where(gap == 1, 0.5, 0.0)).astype(BF16)
    out_r = iota((24, BAND), 0)
    src_r = iota((24, BAND), 1)
    gap_y = jnp.abs((out_r % 8) - 2 * ((src_r % ROWS) - 3))
    py = jnp.where(gap_y == 0, 1.0, jnp.where(gap_y == 1, 0.5, 0.0))
    py = jnp.where(out_r // 8 == src_r // ROWS, py, 0.0).astype(BF16)
    for k in range(5):
        u_wide = jnp.dot(v_ref[3 + k, 0:BAND], px, preferred_element_type=F32)
        if k > 0:
            pieces = ((2 * k - 2, before), (2 * k - 1, 0.5 * (before + u_wide)))
            for z, plane in pieces:
                high, low = split(plane)
                fine = jnp.dot(py, high, preferred_element_type=F32) + jnp.dot(
                    py, low, preferred_element_type=F32
                )
                for d in range(3):
                    out_ref[d, z] = smooth_ref[d, z] + fine[8 * d : 8 * d + 8]
        before = u_wide


def swap(array, axis, offset):
    length = lax.axis_size(axis)
    pairs = []
    for i in range(offset, length - 1, 2):
        pairs += [(i, i + 1), (i + 1, i)]
    return lax.ppermute(array, axis, pairs)


def level_scratch(planes, width):
    return [
        pltpu.VMEM((4 * BAND, 8 * BAND), BF16),
        pltpu.VMEM((4 * BAND, 2 * ROWS), BF16),
        pltpu.VMEM((planes, 2 * BAND, width), BF16),
        pltpu.VMEM((planes, 2 * ROWS, width), BF16),
        pltpu.VMEM((2 * BAND, width), F32),
        pltpu.VMEM((planes, BAND, width), F32),
        pltpu.VMEM((planes, BAND, width), F32),
        pltpu.VMEM((planes, BAND, width), F32),
        pltpu.VMEM((planes, BAND, width), F32),
        pltpu.VMEM((planes, ROWS, width), F32),
    ]


def call(body, out_shape, n_in, scratch=(), name=None):
    vmem = pl.BlockSpec(memory_space=pltpu.VMEM)
    single = not isinstance(out_shape, (tuple, list))
    return pl.pallas_call(
        body,
        out_shape=out_shape,
        in_specs=[pl.BlockSpec(memory_space=pltpu.SMEM)] + [vmem] * n_in,
        out_specs=vmem if single else [vmem] * len(out_shape),
        scratch_shapes=list(scratch),
        compiler_params=pltpu.CompilerParams(vmem_limit_bytes=48 << 20),
        name=name,
    )


def body(applied_load, start_field, bone_mask, element_stiffness):
    width = applied_load.shape[-1]
    half = width // 2
    gz, gy = lax.axis_index("gz"), lax.axis_index("gy")
    place = jnp.stack(
        [
            gz % 2,
            gy % 2,
            (gz == lax.axis_size("gz") - 1).astype(jnp.int32),
            (gy == lax.axis_size("gy") - 1).astype(jnp.int32),
        ]
    ).astype(jnp.int32)
    shape = jax.ShapeDtypeStruct
    packet = shape((25, 8, width), BF16)
    q0, q1 = call(pack_z_kernel, [packet, packet], 3, name="pack_z")(
        place, start_field, applied_load, bone_mask
    )
    r1 = swap(q1, "gz", 1)
    r0 = swap(q0, "gz", 0)
    packet = shape((53, 8, width), BF16)
    q0, q1 = call(pack_y_kernel, [packet, packet], 5, name="pack_y")(
        place, start_field, applied_load, bone_mask, r0, r1
    )
    y1 = swap(q1, "gy", 1)
    y0 = swap(q0, "gy", 0)
    packet = shape((12, 8, half), BF16)
    smoothed, rhs, scale, q0, q1 = call(
        fine_kernel,
        [
            shape(start_field.shape, F32),
            shape((15, 8, half), F32),
            shape((4, 8, half), F32),
            packet,
            packet,
        ],
        8,
        level_scratch(16, width),
        name="fine",
    )(place, element_stiffness, start_field, applied_load, bone_mask, r0, r1, y0, y1)
    r1 = swap(q1, "gz", 1)
    r0 = swap(q0, "gz", 0)
    full, q = call(
        pack_coarse_kernel,
        [shape((40, 8, half), F32), shape((40, 8, half), BF16)],
        4,
        name="pack_coarse",
    )(place, rhs, scale, r0, r1)
    y1 = swap(q, "gy", 1)
    y0 = swap(q, "gy", 0)
    return call(
        coarse_kernel, shape(start_field.shape, F32), 5, level_scratch(11, half), name="coarse"
    )(place, element_stiffness, full, y0, y1, smoothed)


def solution(mesh):
    in_specs = (P(None, "gz", "gy", None), P(None, "gz", "gy", None), P("gz", "gy", None), P())
    out_specs = P(None, "gz", "gy", None)
    return jax.shard_map(body, mesh=mesh, in_specs=in_specs, out_specs=out_specs, check_vma=False)
```

```python
import jax
import jax.numpy as jnp
from jax import lax
from jax.sharding import PartitionSpec as P
from jax.experimental import pallas as pl
from jax.experimental.pallas import tpu as pltpu

F32 = jnp.float32
BF16 = jnp.bfloat16
CHEB = 3
LOW = 0.1
MID = 0.5 * (1.0 + LOW)
HALF = 0.5 * (1.0 - LOW)
RATIO = (1.0 + LOW) / (1.0 - LOW)
ROWS = 16
BAND = 3 * ROWS
DEEP = 4


def iota(shape, dim):
    return lax.broadcasted_iota(jnp.int32, shape, dim)


def build_matrices(stiff):
    m = 4 * BAND
    row_m = iota((m, 24), 0)
    base_row = 12 * (row_m // (2 * BAND)) + 3 * ((row_m // BAND) % 2) + (row_m // ROWS) % 3
    col_e = iota((m, 24), 1)
    row_k = iota((24, m), 0)
    col_k = iota((24, m), 1)
    base_col = 6 * (col_k // (2 * BAND)) + 3 * ((col_k // BAND) % 2) + (col_k // ROWS) % 3
    mm = iota((m, m), 0)
    kk = iota((m, m), 1)
    gap = (mm % ROWS) - (kk % ROWS) + kk // (2 * BAND)
    blocks = []
    left = []
    for cy in range(2):
        pick = (col_e == base_row + 6 * cy).astype(BF16)
        left.append(jnp.dot(pick, stiff, preferred_element_type=F32).astype(BF16))
    for p in range(2):
        pick = (row_k == base_col + 12 * p).astype(BF16)
        block = jnp.zeros((m, m), F32)
        for cy in range(2):
            full = jnp.dot(left[cy], pick, preferred_element_type=F32)
            block = jnp.where(gap == cy, full, block)
        blocks.append(block.astype(BF16))
    md = iota((m, 2 * ROWS), 0)
    kd = iota((m, 2 * ROWS), 1)
    diag = jnp.zeros((m, 2 * ROWS), F32)
    for cy in range(2):
        own = jnp.sum(
            jnp.where(col_e == base_row + 6 * cy, left[cy].astype(F32), 0.0), axis=1, keepdims=True
        )
        diag = jnp.where((kd // ROWS == cy) & (kd % ROWS == md % ROWS), own, diag)
    return jnp.concatenate(blocks, axis=1), diag.astype(BF16)


def spectral_bound(stiff):
    wide = stiff.astype(F32)
    eye = iota((24, 24), 0) == iota((24, 24), 1)
    own = jnp.sum(jnp.where(eye, wide, 0.0), axis=1, keepdims=True)
    total = jnp.sum(jnp.abs(wide), axis=1, keepdims=True)
    return jnp.max(total / own, axis=0, keepdims=True)


def shift_up(values, width):
    rolled = pltpu.roll(values, width - 1, 1)
    return jnp.where(iota(values.shape, 1) == width - 1, 0.0, rolled)


def shift_down(values):
    rolled = pltpu.roll(values, 1, 1)
    return jnp.where(iota(values.shape, 1) == 0, 0.0, rolled)


def put_nodes(v_ref, z, values, width):
    v_ref[z, 0:BAND] = values.astype(BF16)
    v_ref[z, BAND : 2 * BAND] = shift_up(values, width).astype(BF16)


def put_scale(s_ref, layer, scale):
    s_ref[layer, 0:ROWS] = scale.astype(BF16)
    down = pltpu.roll(scale, 1, 0)
    down = jnp.where(iota(scale.shape, 0) == 0, 0.0, down)
    s_ref[layer, ROWS : 2 * ROWS] = down.astype(BF16)


def masked_nodes(v_ref, s_ref, layer, p, width):
    nodes = v_ref[layer + p].reshape(6, ROWS, width)
    parts = [
        (nodes * s_ref[layer, cy * ROWS : (cy + 1) * ROWS][None]).reshape(2 * BAND, width)
        for cy in range(2)
    ]
    return jnp.concatenate(parts, axis=0)


def layer_product(w_ref, v_ref, s_ref, layer, width):
    operand = jnp.concatenate(
        [masked_nodes(v_ref, s_ref, layer, p, width) for p in range(2)], axis=0
    )
    return jnp.dot(w_ref[...], operand, preferred_element_type=F32)


def gather_plane(first, carry_ref, width):
    both = first[0 : 2 * BAND] + carry_ref[...]
    return both[0:BAND] + shift_down(both[BAND : 2 * BAND])


def plane_loop(lo, hi, product, carry_ref, width, use):
    carry_ref[...] = product(lo - 1)[2 * BAND : 4 * BAND]

    def step(z, token):
        both = product(z)
        plane = gather_plane(both, carry_ref, width)
        carry_ref[...] = both[2 * BAND : 4 * BAND]
        use(z, plane)
        return token

    lax.fori_loop(lo, hi + 1, step, 0, unroll=True)


def invert_diagonal(
    lo, hi, wd_ref, s_ref, carry_ref, inv_ref, idle_ref, bound, width, past_z, past_y, first_z, first_y
):
    def product(layer):
        return jnp.dot(wd_ref[...], s_ref[layer], preferred_element_type=F32)

    rows = iota((BAND, width), 0) % ROWS
    keep_y = jnp.where((rows >= first_y) & (past_y == 1), 0.0, 1.0)

    def use(z, diag):
        idle = (diag == 0.0).astype(F32)
        keep_z = jnp.where((z >= first_z) & (past_z == 1), 0.0, 1.0)
        inv_ref[z] = keep_y * keep_z / ((diag + idle) * bound)
        idle_ref[z] = idle[0:ROWS]

    plane_loop(lo, hi, product, carry_ref, width, use)


def tile3(values):
    return jnp.concatenate([values, values, values], axis=0)


def sweep(lo, hi, refs, width, previous, current):
    w_ref, v_ref, s_ref, carry_ref, b_ref, x_ref, u_ref, inv_ref, idle_ref = refs

    def product(layer):
        return layer_product(w_ref, v_ref, s_ref, layer, width)

    def use(z, plane):
        x = x_ref[z]
        r = b_ref[z] - plane - tile3(idle_ref[z]) * x
        update = current * (inv_ref[z] * r)
        if previous is not None:
            update = previous * u_ref[z] + update
        x = x + update
        u_ref[z] = update
        x_ref[z] = x
        put_nodes(v_ref, z, x, width)

    plane_loop(lo, hi, product, carry_ref, width, use)


def chebyshev_factors():
    factors = []
    rho = 1.0 / RATIO
    for _ in range(CHEB - 1):
        nxt = 1.0 / (2.0 * RATIO - rho)
        factors.append((nxt * rho, 2.0 * nxt / HALF))
        rho = nxt
    return factors


def matrices_kernel(e_ref, token_ref, w_ref, wd_ref, bound_ref):
    stiff = e_ref[...]
    w_ref[...], wd_ref[...] = build_matrices(stiff)
    bound_ref[...] = jnp.broadcast_to(spectral_bound(stiff), (8, 128))


def pack_z_kernel(place, x_hbm, b_hbm, m_hbm, q0_ref, q1_ref, token_ref, x_ref, b_ref, m_ref, sem):
    even = 1 - place[0]
    copies = [
        pltpu.make_async_copy(src, dst, sem.at[i])
        for i, (src, dst) in enumerate(((x_hbm, x_ref), (b_hbm, b_ref), (m_hbm, m_ref)))
    ]
    for copy in copies:
        copy.start()
    token_ref[...] = jnp.zeros(token_ref.shape, F32)
    for copy in copies:
        copy.wait()
    for out, up in ((q0_ref, even), (q1_ref, 1 - even)):
        for d in range(3):
            out[4 * d : 4 * d + 4] = x_ref[d, pl.ds(4 * up, 4)].astype(BF16)
            out[12 + 3 * d : 15 + 3 * d] = b_ref[d, pl.ds(5 * up, 3)].astype(BF16)
        out[21:25] = m_ref[pl.ds(4 * up, 4)].astype(F32).astype(BF16)


def z_planes(place, x_ref, b_ref, m_ref, r0_ref, r1_ref):
    odd = place[0] == 1

    def low(i):
        return jnp.where(odd, r0_ref[i].astype(F32), r1_ref[i].astype(F32))

    def high(i):
        return jnp.where(odd, r1_ref[i].astype(F32), r0_ref[i].astype(F32))

    def x_at(d, w):
        if w < 4:
            return low(4 * d + w)
        if w >= 12:
            return high(4 * d + w - 12)
        return x_ref[d, w - 4]

    def b_at(d, w):
        if w < 4:
            return low(12 + 3 * d + w - 1)
        if w >= 12:
            return high(12 + 3 * d + w - 12)
        return b_ref[d, w - 4]

    def m_at(w):
        if w < 4:
            return low(21 + w)
        if w >= 12:
            return high(21 + w - 12)
        return m_ref[w - 4].astype(F32)

    return x_at, b_at, m_at


def flip(values):
    return pltpu.roll(values, 4, 0)


def y_fields(x_at, b_at, m_at):
    fields = []
    for d in range(3):
        fields += [(x_at, (d,), w) for w in range(0, 16, 2)]
    for d in range(3):
        fields += [(b_at, (d,), w) for w in range(1, 15, 2)]
    fields += [(m_at, (), w) for w in range(0, 16, 2)]
    return fields


def pack_y_kernel(place, x_ref, b_ref, m_ref, r0_ref, r1_ref, q0_ref, q1_ref):
    even = place[1] == 0
    x_at, b_at, m_at = z_planes(place, x_ref, b_ref, m_ref, r0_ref, r1_ref)
    for index, (at, lead, w) in enumerate(y_fields(x_at, b_at, m_at)):
        a, b = at(*lead, w), at(*lead, w + 1)
        head = iota(a.shape, 0) < 4
        up = jnp.where(head, flip(a), b)
        down = jnp.where(head, a, flip(b))
        q0_ref[index] = jnp.where(even, up, down).astype(BF16)
        q1_ref[index] = jnp.where(even, down, up).astype(BF16)


def restrict_rows():
    out = iota((BAND, BAND), 0)
    src = iota((BAND, BAND), 1)
    gap = jnp.abs((src % ROWS) - 4 - 2 * ((out % ROWS) - 3))
    own = ((src % ROWS) >= 4) & ((src % ROWS) < 12) & (out // ROWS == src // ROWS)
    weight = jnp.where(gap == 0, 1.0, jnp.where(gap == 1, 0.5, 0.0))
    return jnp.where(own, weight, 0.0).astype(BF16)


def halve_rows():
    out = iota((ROWS, ROWS), 0)
    src = iota((ROWS, ROWS), 1)
    own = (src >= 4) & (src < 12) & ((src - 4) // 2 == out - 3)
    return own.astype(F32).astype(BF16)


def split(values):
    high = values.astype(BF16)
    return high, (values - high.astype(F32)).astype(BF16)


def fine_kernel(
    place, w_ref, wd_ref, bound_ref, x_in, b_in, m_in, r0_ref, r1_ref, y0_ref, y1_ref,
    out_ref, rhs_ref, sc_ref, q0_ref, q1_ref,
    v_ref, s_ref, carry_ref, b_ref, x_ref, u_ref, inv_ref, idle_ref,
):
    width = x_in.shape[-1]
    bound = bound_ref[0:1, 0:1]
    odd = place[1] == 1
    x_at, b_at, m_at = z_planes(place, x_in, b_in, m_in, r0_ref, r1_ref)
    head = iota((8, width), 0) < 4

    def windows(at, lead, w, index):
        low = jnp.where(odd, y0_ref[index].astype(F32), y1_ref[index].astype(F32))
        high = jnp.where(odd, y1_ref[index].astype(F32), y0_ref[index].astype(F32))
        both = []
        for k in range(2):
            own = flip(at(*lead, w + k))
            below = low if k == 0 else flip(low)
            above = flip(high) if k == 0 else high
            both.append(
                jnp.concatenate([jnp.where(head, below, own), jnp.where(head, own, above)], axis=0)
            )
        return both

    for index, (at, lead, w) in enumerate(y_fields(x_at, b_at, m_at)):
        for k, block in enumerate(windows(at, lead, w, index)):
            if at is m_at:
                put_scale(s_ref, w + k, block)
            elif at is b_at:
                b_ref[w + k, ROWS * lead[0] : ROWS * (lead[0] + 1)] = block
            else:
                x_ref[w + k, ROWS * lead[0] : ROWS * (lead[0] + 1)] = block

    def spread(z, token):
        put_nodes(v_ref, z, x_ref[z], width)
        return token

    lax.fori_loop(0, 16, spread, 0, unroll=True)
    invert_diagonal(
        1, 14, wd_ref, s_ref, carry_ref, inv_ref, idle_ref, bound, width, place[2], place[3], 12, 12
    )
    refs = (w_ref, v_ref, s_ref, carry_ref, b_ref, x_ref, u_ref, inv_ref, idle_ref)
    (p1, c1), (p2, c2) = chebyshev_factors()
    sweep(1, 14, refs, width, None, 1.0 / MID)
    sweep(2, 13, refs, width, p1, c1)
    sweep(3, 12, refs, width, p2, c2)

    def use(z, plane):
        u_ref[z] = b_ref[z] - plane - tile3(idle_ref[z]) * x_ref[z]

    plane_loop(
        4, 11, lambda layer: layer_product(w_ref, v_ref, s_ref, layer, width), carry_ref, width, use
    )
    for z in range(8):
        for d in range(3):
            a = x_ref[4 + z, ROWS * d : ROWS * d + 8]
            b = x_ref[4 + z, ROWS * d + 8 : ROWS * d + 16]
            out_ref[d, z] = flip(jnp.where(head, b, a))

    half = width // 2
    fine_x = iota((width, half), 0)
    coarse_x = iota((width, half), 1)
    gap = jnp.abs(fine_x - 2 * coarse_x)
    rx = jnp.where(gap == 0, 1.0, jnp.where(gap == 1, 0.5, 0.0)).astype(BF16)
    pair = (fine_x // 2 == coarse_x).astype(F32).astype(BF16)
    ry = restrict_rows()
    sums = []
    for k in range(5):
        total = 0.0
        if k > 0:
            total = 0.5 * u_ref[4 + 2 * k - 1]
        if k < 4:
            total = total + u_ref[4 + 2 * k] + 0.5 * u_ref[4 + 2 * k + 1]
        high, low = split(total)
        rows = jnp.dot(ry, high, preferred_element_type=F32) + jnp.dot(
            ry, low, preferred_element_type=F32
        )
        sums += [rows[ROWS * d : ROWS * d + 8] for d in range(3)]
    high, low = split(jnp.concatenate(sums, axis=0))
    rhs_ref[...] = (
        jnp.dot(high, rx, preferred_element_type=F32) + jnp.dot(low, rx, preferred_element_type=F32)
    ).reshape(15, 8, half)
    hy = halve_rows()
    counts = []
    for k in range(4):
        both = s_ref[4 + 2 * k, 0:ROWS] + s_ref[5 + 2 * k, 0:ROWS]
        counts.append(jnp.dot(hy, both, preferred_element_type=F32)[0:8])
    counts = jnp.concatenate(counts, axis=0).astype(BF16)
    sc_ref[...] = (0.25 * jnp.dot(counts, pair, preferred_element_type=F32)).reshape(4, 8, half)
    even = 1 - place[0]
    for out, up in ((q0_ref, even), (q1_ref, 1 - even)):
        out[0:9] = rhs_ref[pl.ds(6 * up, 9)].astype(BF16)
        out[9:12] = sc_ref[pl.ds(up, 3)].astype(BF16)


def pack_coarse_kernel(place, rhs_ref, sc_ref, r0_ref, r1_ref, full_ref, q0_ref, q1_ref):
    odd = place[0] == 1
    even_y = place[1] == 0
    head = iota(rhs_ref.shape[1:], 0) < 4
    kept = []

    def low(i):
        return jnp.where(odd, r0_ref[i].astype(F32), r1_ref[i].astype(F32))

    def high(i):
        return jnp.where(odd, r1_ref[i].astype(F32), r0_ref[i].astype(F32))

    for z in range(10):
        c = z - 3
        for d in range(4):
            value = jnp.zeros(rhs_ref.shape[1:], F32)
            if d < 3:
                if -2 <= c <= 0:
                    value = value + low(3 * (c + 2) + d)
                if 4 <= c <= 6:
                    value = value + high(3 * (c - 4) + d)
                if 0 <= c <= 4:
                    value = value + rhs_ref[3 * c + d]
            else:
                if c <= -1:
                    value = low(9 + c + 3)
                elif c >= 4:
                    value = high(9 + c - 4)
                else:
                    value = sc_ref[c]
            full_ref[4 * z + d] = value
            kept.append(value)
    for i in range(20):
        a, b = kept[2 * i], kept[2 * i + 1]
        up = jnp.where(head, flip(a), b)
        down = jnp.where(head, pltpu.roll(a, 5, 0), pltpu.roll(b, 1, 0))
        q0_ref[i] = jnp.where(even_y, up, down).astype(BF16)
        q1_ref[i] = jnp.where(even_y, down, up).astype(BF16)


def coarse_kernel(
    place, w_ref, wd_ref, bound_ref, full_ref, y0_ref, y1_ref, smooth_ref, out_ref,
    v_ref, s_ref, carry_ref, b_ref, x_ref, u_ref, inv_ref, idle_ref,
):
    half = full_ref.shape[-1]
    width = 2 * half
    bound = bound_ref[0:1, 0:1]
    odd = place[1] == 1
    rows8 = iota((8, half), 0)
    for z in range(10):
        for d in range(4):
            i = 4 * z + d
            low = jnp.where(odd, y0_ref[i // 2].astype(F32), y1_ref[i // 2].astype(F32))
            high = jnp.where(odd, y1_ref[i // 2].astype(F32), y0_ref[i // 2].astype(F32))
            if i % 2:
                low = flip(low)
            high = pltpu.roll(high, 3 if i % 2 else 7, 0)
            first = (
                full_ref[i] + jnp.where(rows8 < 4, low, 0.0) + jnp.where(rows8 == 7, high, 0.0)
            )
            block = jnp.concatenate([first, jnp.where(rows8 < 3, high, 0.0)], axis=0)
            if d < 3:
                b_ref[z, ROWS * d : ROWS * (d + 1)] = block
            else:
                put_scale(s_ref, z, block)
    invert_diagonal(
        1, 9, wd_ref, s_ref, carry_ref, inv_ref, idle_ref, bound, half, place[2], place[3], 7, 7
    )

    def first_step(z, token):
        update = (1.0 / MID) * (inv_ref[z] * b_ref[z])
        u_ref[z] = update
        x_ref[z] = update
        put_nodes(v_ref, z, update, half)
        return token

    lax.fori_loop(1, 10, first_step, 0, unroll=True)
    refs = (w_ref, v_ref, s_ref, carry_ref, b_ref, x_ref, u_ref, inv_ref, idle_ref)
    (p1, c1), (p2, c2) = chebyshev_factors()
    sweep(2, 8, refs, half, p1, c1)
    sweep(3, 7, refs, half, p2, c2)

    coarse_x = iota((half, width), 0)
    fine_x = iota((half, width), 1)
    gap = jnp.abs(fine_x - 2 * coarse_x)
    px = jnp.where(gap == 0, 1.0, jnp.where(gap == 1, 0.5, 0.0)).astype(BF16)
    out_r = iota((24, BAND), 0)
    src_r = iota((24, BAND), 1)
    gap_y = jnp.abs((out_r % 8) - 2 * ((src_r % ROWS) - 3))
    py = jnp.where(gap_y == 0, 1.0, jnp.where(gap_y == 1, 0.5, 0.0))
    py = jnp.where(out_r // 8 == src_r // ROWS, py, 0.0).astype(BF16)
    for k in range(5):
        u_wide = jnp.dot(v_ref[3 + k, 0:BAND], px, preferred_element_type=F32)
        if k > 0:
            pieces = ((2 * k - 2, before), (2 * k - 1, 0.5 * (before + u_wide)))
            for z, plane in pieces:
                high, low = split(plane)
                fine = jnp.dot(py, high, preferred_element_type=F32) + jnp.dot(
                    py, low, preferred_element_type=F32
                )
                for d in range(3):
                    out_ref[d, z] = smooth_ref[d, z] + fine[8 * d : 8 * d + 8]
        before = u_wide


def swap(array, axis, offset):
    length = lax.axis_size(axis)
    pairs = []
    for i in range(offset, length - 1, 2):
        pairs += [(i, i + 1), (i + 1, i)]
    return lax.ppermute(array, axis, pairs)


def level_scratch(planes, width):
    return [
        pltpu.VMEM((planes, 2 * BAND, width), BF16),
        pltpu.VMEM((planes, 2 * ROWS, width), BF16),
        pltpu.VMEM((2 * BAND, width), F32),
        pltpu.VMEM((planes, BAND, width), F32),
        pltpu.VMEM((planes, BAND, width), F32),
        pltpu.VMEM((planes, BAND, width), F32),
        pltpu.VMEM((planes, BAND, width), F32),
        pltpu.VMEM((planes, ROWS, width), F32),
    ]


def call(body, out_shape, n_in, scratch=(), name=None, place=True, space=pltpu.VMEM):
    vmem = pl.BlockSpec(memory_space=pltpu.VMEM)
    single = not isinstance(out_shape, (tuple, list))
    lead = [pl.BlockSpec(memory_space=pltpu.SMEM)] if place else []
    return pl.pallas_call(
        body,
        out_shape=out_shape,
        in_specs=lead + [pl.BlockSpec(memory_space=space)] * n_in,
        out_specs=vmem if single else [vmem] * len(out_shape),
        scratch_shapes=list(scratch),
        compiler_params=pltpu.CompilerParams(vmem_limit_bytes=48 << 20),
        name=name,
    )


def body(applied_load, start_field, bone_mask, element_stiffness):
    width = applied_load.shape[-1]
    half = width // 2
    gz, gy = lax.axis_index("gz"), lax.axis_index("gy")
    place = jnp.stack(
        [
            gz % 2,
            gy % 2,
            (gz == lax.axis_size("gz") - 1).astype(jnp.int32),
            (gy == lax.axis_size("gy") - 1).astype(jnp.int32),
        ]
    ).astype(jnp.int32)
    shape = jax.ShapeDtypeStruct
    packet = shape((25, 8, width), BF16)
    q0, q1, token = call(
        pack_z_kernel,
        [packet, packet, shape((8, 128), F32)],
        3,
        [
            pltpu.VMEM(start_field.shape, F32),
            pltpu.VMEM(applied_load.shape, F32),
            pltpu.VMEM(bone_mask.shape, jnp.int32),
            pltpu.SemaphoreType.DMA((3,)),
        ],
        name="pack_z",
        space=pltpu.HBM,
    )(place, *[pltpu.with_memory_space_constraint(a, pltpu.HBM) for a in (start_field, applied_load, bone_mask)])
    r1 = swap(q1, "gz", 1)
    r0 = swap(q0, "gz", 0)
    matrices = call(
        matrices_kernel,
        [
            shape((4 * BAND, 8 * BAND), BF16),
            shape((4 * BAND, 2 * ROWS), BF16),
            shape((8, 128), F32),
        ],
        2,
        name="matrices",
        place=False,
    )(element_stiffness, token)
    packet = shape((53, 8, width), BF16)
    q0, q1 = call(pack_y_kernel, [packet, packet], 5, name="pack_y")(
        place, start_field, applied_load, bone_mask, r0, r1
    )
    y1 = swap(q1, "gy", 1)
    y0 = swap(q0, "gy", 0)
    packet = shape((12, 8, half), BF16)
    smoothed, rhs, scale, q0, q1 = call(
        fine_kernel,
        [
            shape(start_field.shape, F32),
            shape((15, 8, half), F32),
            shape((4, 8, half), F32),
            packet,
            packet,
        ],
        10,
        level_scratch(16, width),
        name="fine",
    )(place, *matrices, start_field, applied_load, bone_mask, r0, r1, y0, y1)
    r1 = swap(q1, "gz", 1)
    r0 = swap(q0, "gz", 0)
    packet = shape((20, 8, half), BF16)
    full, q0, q1 = call(
        pack_coarse_kernel,
        [shape((40, 8, half), F32), packet, packet],
        4,
        name="pack_coarse",
    )(place, rhs, scale, r0, r1)
    y1 = swap(q1, "gy", 1)
    y0 = swap(q0, "gy", 0)
    return call(
        coarse_kernel, shape(start_field.shape, F32), 7, level_scratch(11, half), name="coarse"
    )(place, *matrices, full, y0, y1, smoothed)


def solution(mesh):
    in_specs = (P(None, "gz", "gy", None), P(None, "gz", "gy", None), P("gz", "gy", None), P())
    out_specs = P(None, "gz", "gy", None)
    return jax.shard_map(body, mesh=mesh, in_specs=in_specs, out_specs=out_specs, check_vma=False)
```

```python
import jax
import jax.numpy as jnp
from jax import lax
from jax.sharding import PartitionSpec as P
from jax.experimental import pallas as pl
from jax.experimental.pallas import tpu as pltpu

F32 = jnp.float32
BF16 = jnp.bfloat16
CHEB = 3
LOW = 0.1
MID = 0.5 * (1.0 + LOW)
HALF = 0.5 * (1.0 - LOW)
RATIO = (1.0 + LOW) / (1.0 - LOW)
ROWS = 16
BAND = 3 * ROWS
DEEP = 4


def iota(shape, dim):
    return lax.broadcasted_iota(jnp.int32, shape, dim)


def build_matrices(stiff):
    m = 4 * BAND
    row_m = iota((m, 24), 0)
    base_row = 12 * (row_m // (2 * BAND)) + 3 * ((row_m // BAND) % 2) + (row_m // ROWS) % 3
    col_e = iota((m, 24), 1)
    row_k = iota((24, m), 0)
    col_k = iota((24, m), 1)
    base_col = 6 * (col_k // (2 * BAND)) + 3 * ((col_k // BAND) % 2) + (col_k // ROWS) % 3
    mm = iota((m, m), 0)
    kk = iota((m, m), 1)
    gap = (mm % ROWS) - (kk % ROWS) + kk // (2 * BAND)
    blocks = []
    left = []
    for cy in range(2):
        pick = (col_e == base_row + 6 * cy).astype(BF16)
        left.append(jnp.dot(pick, stiff, preferred_element_type=F32).astype(BF16))
    for p in range(2):
        pick = (row_k == base_col + 12 * p).astype(BF16)
        block = jnp.zeros((m, m), F32)
        for cy in range(2):
            full = jnp.dot(left[cy], pick, preferred_element_type=F32)
            block = jnp.where(gap == cy, full, block)
        blocks.append(block.astype(BF16))
    md = iota((m, 2 * ROWS), 0)
    kd = iota((m, 2 * ROWS), 1)
    diag = jnp.zeros((m, 2 * ROWS), F32)
    for cy in range(2):
        own = jnp.sum(
            jnp.where(col_e == base_row + 6 * cy, left[cy].astype(F32), 0.0), axis=1, keepdims=True
        )
        diag = jnp.where((kd // ROWS == cy) & (kd % ROWS == md % ROWS), own, diag)
    return jnp.concatenate(blocks, axis=1), diag.astype(BF16)


def spectral_bound(stiff):
    wide = stiff.astype(F32)
    eye = iota((24, 24), 0) == iota((24, 24), 1)
    own = jnp.sum(jnp.where(eye, wide, 0.0), axis=1, keepdims=True)
    total = jnp.sum(jnp.abs(wide), axis=1, keepdims=True)
    return jnp.max(total / own, axis=0, keepdims=True)


def shift_up(values, width):
    rolled = pltpu.roll(values, width - 1, 1)
    return jnp.where(iota(values.shape, 1) == width - 1, 0.0, rolled)


def shift_down(values):
    rolled = pltpu.roll(values, 1, 1)
    return jnp.where(iota(values.shape, 1) == 0, 0.0, rolled)


def put_nodes(v_ref, z, values, width):
    v_ref[z, 0:BAND] = values.astype(BF16)
    v_ref[z, BAND : 2 * BAND] = shift_up(values, width).astype(BF16)


def put_scale(s_ref, layer, scale):
    s_ref[layer, 0:ROWS] = scale.astype(BF16)
    down = pltpu.roll(scale, 1, 0)
    down = jnp.where(iota(scale.shape, 0) == 0, 0.0, down)
    s_ref[layer, ROWS : 2 * ROWS] = down.astype(BF16)


def masked_nodes(v_ref, s_ref, layer, p, width):
    nodes = v_ref[layer + p].reshape(6, ROWS, width)
    parts = [
        (nodes * s_ref[layer, cy * ROWS : (cy + 1) * ROWS][None]).reshape(2 * BAND, width)
        for cy in range(2)
    ]
    return jnp.concatenate(parts, axis=0)


def layer_product(w_ref, v_ref, s_ref, layer, width):
    operand = jnp.concatenate(
        [masked_nodes(v_ref, s_ref, layer, p, width) for p in range(2)], axis=0
    )
    return jnp.dot(w_ref[...], operand, preferred_element_type=F32)


def gather_plane(first, carry_ref, width):
    both = first[0 : 2 * BAND] + carry_ref[...]
    return both[0:BAND] + shift_down(both[BAND : 2 * BAND])


def plane_loop(lo, hi, product, carry_ref, width, use):
    carry_ref[...] = product(lo - 1)[2 * BAND : 4 * BAND]

    def step(z, token):
        both = product(z)
        plane = gather_plane(both, carry_ref, width)
        carry_ref[...] = both[2 * BAND : 4 * BAND]
        use(z, plane)
        return token

    lax.fori_loop(lo, hi + 1, step, 0, unroll=True)


def invert_diagonal(
    lo, hi, wd_ref, s_ref, carry_ref, inv_ref, idle_ref, bound, width, past_z, past_y, first_z, first_y
):
    def product(layer):
        return jnp.dot(wd_ref[...], s_ref[layer], preferred_element_type=F32)

    rows = iota((BAND, width), 0) % ROWS
    keep_y = jnp.where((rows >= first_y) & (past_y == 1), 0.0, 1.0)

    def use(z, diag):
        idle = (diag == 0.0).astype(F32)
        keep_z = jnp.where((z >= first_z) & (past_z == 1), 0.0, 1.0)
        inv_ref[z] = keep_y * keep_z / ((diag + idle) * bound)
        idle_ref[z] = idle[0:ROWS]

    plane_loop(lo, hi, product, carry_ref, width, use)


def tile3(values):
    return jnp.concatenate([values, values, values], axis=0)


def sweep(lo, hi, refs, width, previous, current):
    w_ref, v_ref, s_ref, carry_ref, b_ref, x_ref, u_ref, inv_ref, idle_ref = refs

    def product(layer):
        return layer_product(w_ref, v_ref, s_ref, layer, width)

    def use(z, plane):
        x = x_ref[z]
        r = b_ref[z] - plane - tile3(idle_ref[z]) * x
        update = current * (inv_ref[z] * r)
        if previous is not None:
            update = previous * u_ref[z] + update
        x = x + update
        u_ref[z] = update
        x_ref[z] = x
        put_nodes(v_ref, z, x, width)

    plane_loop(lo, hi, product, carry_ref, width, use)


def chebyshev_factors():
    factors = []
    rho = 1.0 / RATIO
    for _ in range(CHEB - 1):
        nxt = 1.0 / (2.0 * RATIO - rho)
        factors.append((nxt * rho, 2.0 * nxt / HALF))
        rho = nxt
    return factors


def weights(gap, where):
    value = jnp.where(gap == 0, 1.0, jnp.where(gap == 1, 0.5, 0.0))
    return jnp.where(where, value, 0.0)


def own_rows(w_ref):
    groups = [w_ref[ROWS * g : ROWS * (g + 1)].astype(F32)[4:12] for g in range(12)]
    return jnp.concatenate(groups, axis=0).astype(BF16)


def restrict_planes():
    out, src = iota((120, 192), 0), iota((120, 192), 1)
    gap_z = jnp.abs(src // 24 - 2 * (out // 24))
    gap_y = jnp.abs(src % 8 - 2 * (out % 8 - 3))
    same = (src // 8) % 3 == (out // 8) % 3
    return (weights(gap_z, same) * weights(gap_y, same)).astype(BF16)


def halve_planes():
    out, src = iota((32, 64), 0), iota((32, 64), 1)
    same = (src // 16 == out // 8) & ((src % 8) // 2 == out % 8 - 3)
    return same.astype(F32).astype(BF16)


def prolong_rows():
    out, src = iota((120, 240), 0), iota((120, 240), 1)
    gap = jnp.abs(out % 8 - 2 * (src % ROWS - 3))
    same = (out // 24 == src // BAND) & ((out // 8) % 3 == (src // ROWS) % 3)
    return weights(gap, same).astype(BF16)


def matrices_kernel(
    e_ref, token_ref, w_ref, wd_ref, bound_ref, wr_ref, rzy_ref, hzy_ref, py_ref, rx_ref, px_ref, pair_ref
):
    stiff = e_ref[...]
    w_ref[...], wd_ref[...] = build_matrices(stiff)
    bound_ref[...] = jnp.broadcast_to(spectral_bound(stiff), (8, 128))
    wr_ref[...] = own_rows(w_ref)
    rzy_ref[...] = restrict_planes()
    hzy_ref[...] = halve_planes()
    py_ref[...] = prolong_rows()
    fine, coarse = iota(rx_ref.shape, 0), iota(rx_ref.shape, 1)
    rx_ref[...] = weights(jnp.abs(fine - 2 * coarse), fine >= 0).astype(BF16)
    pair_ref[...] = (fine // 2 == coarse).astype(F32).astype(BF16)
    coarse, fine = iota(px_ref.shape, 0), iota(px_ref.shape, 1)
    px_ref[...] = weights(jnp.abs(fine - 2 * coarse), fine >= 0).astype(BF16)


def pack_z_kernel(place, x_hbm, b_hbm, m_hbm, q0_ref, q1_ref, token_ref, x_ref, b_ref, m_ref, sem):
    even = 1 - place[0]
    pairs = [(m_hbm, m_ref)]
    for d in range(3):
        pairs += [(x_hbm.at[d], x_ref.at[d]), (b_hbm.at[d], b_ref.at[d])]
    copies = [pltpu.make_async_copy(src, dst, sem.at[i]) for i, (src, dst) in enumerate(pairs)]
    for copy in copies:
        copy.start()
    token_ref[...] = jnp.zeros(token_ref.shape, F32)
    for copy in copies:
        copy.wait()
    for out, up in ((q0_ref, even), (q1_ref, 1 - even)):
        for d in range(3):
            out[4 * d : 4 * d + 4] = x_ref[d, pl.ds(4 * up, 4)].astype(BF16)
            out[12 + 3 * d : 15 + 3 * d] = b_ref[d, pl.ds(5 * up, 3)].astype(BF16)
        out[21:25] = m_ref[pl.ds(4 * up, 4)].astype(F32).astype(BF16)


def z_planes(place, x_ref, b_ref, m_ref, r0_ref, r1_ref):
    odd = place[0] == 1

    def low(i):
        return jnp.where(odd, r0_ref[i].astype(F32), r1_ref[i].astype(F32))

    def high(i):
        return jnp.where(odd, r1_ref[i].astype(F32), r0_ref[i].astype(F32))

    def x_at(d, w):
        if w < 4:
            return low(4 * d + w)
        if w >= 12:
            return high(4 * d + w - 12)
        return x_ref[d, w - 4]

    def b_at(d, w):
        if w < 4:
            return low(12 + 3 * d + w - 1)
        if w >= 12:
            return high(12 + 3 * d + w - 12)
        return b_ref[d, w - 4]

    def m_at(w):
        if w < 4:
            return low(21 + w)
        if w >= 12:
            return high(21 + w - 12)
        return m_ref[w - 4].astype(F32)

    return x_at, b_at, m_at


def flip(values):
    return pltpu.roll(values, 4, 0)


def node_fields(x_at, m_at):
    fields = [(x_at, (d,), w) for d in range(3) for w in range(0, 16, 2)]
    return fields + [(m_at, (), w) for w in range(0, 16, 2)]


def load_fields(b_at):
    return [(b_at, (d,), w) for d in range(3) for w in range(1, 15, 2)]


def pack_rows(place, fields, q0_ref, q1_ref):
    even = place[1] == 0
    for index, (at, lead, w) in enumerate(fields):
        a, b = at(*lead, w), at(*lead, w + 1)
        head = iota(a.shape, 0) < 4
        up = jnp.where(head, flip(a), b)
        down = jnp.where(head, a, flip(b))
        q0_ref[index] = jnp.where(even, up, down).astype(BF16)
        q1_ref[index] = jnp.where(even, down, up).astype(BF16)


def pack_nodes_kernel(place, after_ref, x_ref, m_ref, r0_ref, r1_ref, q0_ref, q1_ref):
    x_at, _, m_at = z_planes(place, x_ref, None, m_ref, r0_ref, r1_ref)
    pack_rows(place, node_fields(x_at, m_at), q0_ref, q1_ref)


def pack_load_kernel(place, b_ref, r0_ref, r1_ref, q0_ref, q1_ref):
    _, b_at, _ = z_planes(place, None, b_ref, None, r0_ref, r1_ref)
    pack_rows(place, load_fields(b_at), q0_ref, q1_ref)


def window_maker(place, y0_ref, y1_ref, width):
    odd = place[1] == 1
    head = iota((8, width), 0) < 4

    def windows(at, lead, w, index):
        low = jnp.where(odd, y0_ref[index].astype(F32), y1_ref[index].astype(F32))
        high = jnp.where(odd, y1_ref[index].astype(F32), y0_ref[index].astype(F32))
        both = []
        for k in range(2):
            own = flip(at(*lead, w + k))
            below = low if k == 0 else flip(low)
            above = flip(high) if k == 0 else high
            both.append(
                jnp.concatenate([jnp.where(head, below, own), jnp.where(head, own, above)], axis=0)
            )
        return both

    return windows


def split(values):
    high = values.astype(BF16)
    return high, (values - high.astype(F32)).astype(BF16)


def fine_start_kernel(
    place, w_ref, wd_ref, bound_ref, hzy_ref, pair_ref, x_in, m_in, r0_ref, r1_ref, y0_ref, y1_ref,
    x_ref, s_ref, inv_ref, idle_ref, first_ref, sc_ref,
    v_ref, carry_ref,
):
    width = x_in.shape[-1]
    x_at, _, m_at = z_planes(place, x_in, None, m_in, r0_ref, r1_ref)
    windows = window_maker(place, y0_ref, y1_ref, width)
    for index, (at, lead, w) in enumerate(node_fields(x_at, m_at)):
        for k, block in enumerate(windows(at, lead, w, index)):
            if at is m_at:
                put_scale(s_ref, w + k, block)
            else:
                x_ref[w + k, ROWS * lead[0] : ROWS * (lead[0] + 1)] = block
    for z in range(16):
        put_nodes(v_ref, z, x_ref[z], width)
    invert_diagonal(
        1, 14, wd_ref, s_ref, carry_ref, inv_ref, idle_ref, bound_ref[0:1, 0:1], width,
        place[2], place[3], 12, 12,
    )

    def use(z, plane):
        first_ref[z] = plane + tile3(idle_ref[z]) * x_ref[z]

    plane_loop(
        1, 14, lambda layer: layer_product(w_ref, v_ref, s_ref, layer, width), carry_ref, width, use
    )
    counts = jnp.dot(
        hzy_ref[...], m_in[...].astype(F32).astype(BF16).reshape(64, width), preferred_element_type=F32
    )
    counts = jnp.dot(counts.astype(BF16), pair_ref[...], preferred_element_type=F32)
    sc_ref[...] = (0.25 * counts).reshape(sc_ref.shape)


def own_part(ref, z, d, head):
    a = ref[z, ROWS * d : ROWS * d + 8]
    b = ref[z, ROWS * d + 8 : ROWS * d + 16]
    return flip(jnp.where(head, b, a))


def fine_kernel(
    place, w_ref, wr_ref, rzy_ref, rx_ref, x0_ref, s_ref, inv_ref, idle_ref, first_ref, sc_ref,
    b_in, r0_ref, r1_ref, y0_ref, y1_ref,
    out_ref, rhs_ref, q0_ref, q1_ref,
    v_ref, carry_ref, b_ref, x_ref, u_ref,
):
    width = b_in.shape[-1]
    _, b_at, _ = z_planes(place, None, b_in, None, r0_ref, r1_ref)
    windows = window_maker(place, y0_ref, y1_ref, width)
    for index, (at, lead, w) in enumerate(load_fields(b_at)):
        for k, block in enumerate(windows(at, lead, w, index)):
            b_ref[w + k, ROWS * lead[0] : ROWS * (lead[0] + 1)] = block
    for z in range(1, 15):
        update = (1.0 / MID) * (inv_ref[z] * (b_ref[z] - first_ref[z]))
        x = x0_ref[z] + update
        u_ref[z] = update
        x_ref[z] = x
        put_nodes(v_ref, z, x, width)
    refs = (w_ref, v_ref, s_ref, carry_ref, b_ref, x_ref, u_ref, inv_ref, idle_ref)
    (p1, c1), (p2, c2) = chebyshev_factors()
    sweep(2, 13, refs, width, p1, c1)
    sweep(3, 12, refs, width, p2, c2)

    head = iota((8, width), 0) < 4

    def product(layer):
        return layer_product(wr_ref, v_ref, s_ref, layer, width)

    carry = product(3)[48:96]
    parts = []
    for z in range(8):
        both = product(4 + z)
        plane = both[0:48] + carry
        plane = plane[0:24] + shift_down(plane[24:48])
        carry = both[48:96]
        idle = own_part(idle_ref, 4 + z, 0, head)
        for d in range(3):
            x = own_part(x_ref, 4 + z, d, head)
            out_ref[d, z] = x
            parts.append(b_in[d, z] - plane[8 * d : 8 * d + 8] - idle * x)
    residual = jnp.concatenate(parts, axis=0).astype(BF16)
    sums = jnp.dot(rzy_ref[...], residual, preferred_element_type=F32)
    sums = jnp.dot(sums.astype(BF16), rx_ref[...], preferred_element_type=F32)
    rhs_ref[...] = sums.reshape(rhs_ref.shape)
    even = 1 - place[0]
    for out, up in ((q0_ref, even), (q1_ref, 1 - even)):
        out[0:9] = rhs_ref[pl.ds(6 * up, 9)].astype(BF16)
        out[9:12] = sc_ref[pl.ds(up, 3)].astype(BF16)


def pack_coarse_kernel(place, rhs_ref, sc_ref, r0_ref, r1_ref, full_ref, q0_ref, q1_ref):
    odd = place[0] == 1
    even_y = place[1] == 0
    head = iota(rhs_ref.shape[1:], 0) < 4
    kept = []

    def low(i):
        return jnp.where(odd, r0_ref[i].astype(F32), r1_ref[i].astype(F32))

    def high(i):
        return jnp.where(odd, r1_ref[i].astype(F32), r0_ref[i].astype(F32))

    for z in range(10):
        c = z - 3
        for d in range(4):
            value = jnp.zeros(rhs_ref.shape[1:], F32)
            if d < 3:
                if -2 <= c <= 0:
                    value = value + low(3 * (c + 2) + d)
                if 4 <= c <= 6:
                    value = value + high(3 * (c - 4) + d)
                if 0 <= c <= 4:
                    value = value + rhs_ref[3 * c + d]
            else:
                if c <= -1:
                    value = low(9 + c + 3)
                elif c >= 4:
                    value = high(9 + c - 4)
                else:
                    value = sc_ref[c]
            full_ref[4 * z + d] = value
            kept.append(value)
    for i in range(20):
        a, b = kept[2 * i], kept[2 * i + 1]
        up = jnp.where(head, flip(a), b)
        down = jnp.where(head, pltpu.roll(a, 5, 0), pltpu.roll(b, 1, 0))
        q0_ref[i] = jnp.where(even_y, up, down).astype(BF16)
        q1_ref[i] = jnp.where(even_y, down, up).astype(BF16)


def coarse_kernel(
    place, w_ref, wd_ref, bound_ref, py_ref, px_ref, full_ref, y0_ref, y1_ref, smooth_ref, out_hbm,
    v_ref, s_ref, carry_ref, b_ref, x_ref, u_ref, inv_ref, idle_ref, out_ref, sem,
):
    half = full_ref.shape[-1]
    width = 2 * half
    bound = bound_ref[0:1, 0:1]
    odd = place[1] == 1
    rows8 = iota((8, half), 0)
    for z in range(10):
        for d in range(4):
            i = 4 * z + d
            low = jnp.where(odd, y0_ref[i // 2].astype(F32), y1_ref[i // 2].astype(F32))
            high = jnp.where(odd, y1_ref[i // 2].astype(F32), y0_ref[i // 2].astype(F32))
            if i % 2:
                low = flip(low)
            high = pltpu.roll(high, 3 if i % 2 else 7, 0)
            first = (
                full_ref[i] + jnp.where(rows8 < 4, low, 0.0) + jnp.where(rows8 == 7, high, 0.0)
            )
            block = jnp.concatenate([first, jnp.where(rows8 < 3, high, 0.0)], axis=0)
            if d < 3:
                b_ref[z, ROWS * d : ROWS * (d + 1)] = block
            else:
                put_scale(s_ref, z, block)
    invert_diagonal(
        1, 9, wd_ref, s_ref, carry_ref, inv_ref, idle_ref, bound, half, place[2], place[3], 7, 7
    )

    def first_step(z, token):
        update = (1.0 / MID) * (inv_ref[z] * b_ref[z])
        u_ref[z] = update
        x_ref[z] = update
        put_nodes(v_ref, z, update, half)
        return token

    lax.fori_loop(1, 10, first_step, 0, unroll=True)
    refs = (w_ref, v_ref, s_ref, carry_ref, b_ref, x_ref, u_ref, inv_ref, idle_ref)
    (p1, c1), (p2, c2) = chebyshev_factors()
    sweep(2, 8, refs, half, p1, c1)
    sweep(3, 7, refs, half, p2, c2)

    coarse = jnp.concatenate([v_ref[3 + k, 0:BAND] for k in range(5)], axis=0)
    rows = jnp.dot(py_ref[...], coarse, preferred_element_type=F32)
    high, low = split(rows)
    wide = jnp.dot(jnp.concatenate([high, low], axis=0), px_ref[...], preferred_element_type=F32)
    wide = (wide[0:120] + wide[120:240]).reshape(5, 3, 8, width)
    copies = []
    for z in range(8):
        k = z // 2
        plane = wide[k] if z % 2 == 0 else 0.5 * (wide[k] + wide[k + 1])
        out_ref[z] = smooth_ref[:, z] + plane
        copies.append(pltpu.make_async_copy(out_ref.at[z], out_hbm.at[:, z], sem.at[z]))
        copies[-1].start()
    for copy in copies:
        copy.wait()


def swap(array, axis, offset):
    length = lax.axis_size(axis)
    pairs = []
    for i in range(offset, length - 1, 2):
        pairs += [(i, i + 1), (i + 1, i)]
    return lax.ppermute(array, axis, pairs)


def call(
    body, out_shape, n_in, scratch=(), name=None, place=True, space=pltpu.VMEM, out_space=pltpu.VMEM
):
    vmem = pl.BlockSpec(memory_space=out_space)
    single = not isinstance(out_shape, (tuple, list))
    lead = [pl.BlockSpec(memory_space=pltpu.SMEM)] if place else []
    return pl.pallas_call(
        body,
        out_shape=out_shape,
        in_specs=lead + [pl.BlockSpec(memory_space=space)] * n_in,
        out_specs=vmem if single else [vmem] * len(out_shape),
        scratch_shapes=list(scratch),
        compiler_params=pltpu.CompilerParams(vmem_limit_bytes=24 << 20),
        name=name,
    )


def body(applied_load, start_field, bone_mask, element_stiffness):
    width = applied_load.shape[-1]
    half = width // 2
    gz, gy = lax.axis_index("gz"), lax.axis_index("gy")
    place = jnp.stack(
        [
            gz % 2,
            gy % 2,
            (gz == lax.axis_size("gz") - 1).astype(jnp.int32),
            (gy == lax.axis_size("gy") - 1).astype(jnp.int32),
        ]
    ).astype(jnp.int32)
    shape = jax.ShapeDtypeStruct
    packet = shape((25, 8, width), BF16)
    arguments = (start_field, applied_load, bone_mask)
    q0, q1, token, start_field, applied_load, bone_mask = call(
        pack_z_kernel,
        [packet, packet, shape((8, 128), F32)] + [shape(a.shape, a.dtype) for a in arguments],
        3,
        [pltpu.SemaphoreType.DMA((7,))],
        name="pack_z",
        space=pltpu.HBM,
    )(place, *[pltpu.with_memory_space_constraint(a, pltpu.HBM) for a in arguments])
    r1 = swap(q1, "gz", 1)
    r0 = swap(q0, "gz", 0)
    w, wd, bound, wr, rzy, hzy, py, rx, px, pair = call(
        matrices_kernel,
        [
            shape((4 * BAND, 8 * BAND), BF16),
            shape((4 * BAND, 2 * ROWS), BF16),
            shape((8, 128), F32),
            shape((2 * BAND, 8 * BAND), BF16),
            shape((120, 192), BF16),
            shape((32, 64), BF16),
            shape((120, 240), BF16),
            shape((width, half), BF16),
            shape((half, width), BF16),
            shape((width, half), BF16),
        ],
        2,
        name="matrices",
        place=False,
    )(element_stiffness, token)
    packet = shape((32, 8, width), BF16)
    q0, q1 = call(pack_nodes_kernel, [packet, packet], 5, name="pack_nodes")(
        place, bound, start_field, bone_mask, r0, r1
    )
    y1 = swap(q1, "gy", 1)
    y0 = swap(q0, "gy", 0)
    packet = shape((21, 8, width), BF16)
    q0, q1 = call(pack_load_kernel, [packet, packet], 3, name="pack_load")(
        place, applied_load, r0, r1
    )
    yb1 = swap(q1, "gy", 1)
    yb0 = swap(q0, "gy", 0)
    plane16 = shape((16, BAND, width), F32)
    carry = pltpu.VMEM((2 * BAND, width), F32)
    shifted = pltpu.VMEM((16, 2 * BAND, width), BF16)
    full_plane = pltpu.VMEM((16, BAND, width), F32)
    x0, scales, inverse, idle, first, scale = call(
        fine_start_kernel,
        [
            plane16,
            shape((16, 2 * ROWS, width), BF16),
            plane16,
            shape((16, ROWS, width), F32),
            plane16,
            shape((4, 8, half), F32),
        ],
        11,
        [shifted, carry],
        name="fine_start",
    )(place, w, wd, bound, hzy, pair, start_field, bone_mask, r0, r1, y0, y1)
    packet = shape((12, 8, half), BF16)
    smoothed, rhs, q0, q1 = call(
        fine_kernel,
        [shape(start_field.shape, F32), shape((15, 8, half), F32), packet, packet],
        15,
        [shifted, carry, full_plane, full_plane, full_plane],
        name="fine",
    )(place, w, wr, rzy, rx, x0, scales, inverse, idle, first, scale, applied_load, r0, r1, yb0, yb1)
    r1 = swap(q1, "gz", 1)
    r0 = swap(q0, "gz", 0)
    packet = shape((20, 8, half), BF16)
    full, q0, q1 = call(
        pack_coarse_kernel,
        [shape((40, 8, half), F32), packet, packet],
        4,
        name="pack_coarse",
    )(place, rhs, scale, r0, r1)
    y1 = swap(q1, "gy", 1)
    y0 = swap(q0, "gy", 0)
    coarse_plane = pltpu.VMEM((11, BAND, half), F32)
    return call(
        coarse_kernel,
        shape(start_field.shape, F32),
        9,
        [
            pltpu.VMEM((11, 2 * BAND, half), BF16),
            pltpu.VMEM((11, 2 * ROWS, half), BF16),
            pltpu.VMEM((2 * BAND, half), F32),
            coarse_plane,
            coarse_plane,
            coarse_plane,
            coarse_plane,
            pltpu.VMEM((11, ROWS, half), F32),
            pltpu.VMEM((8, 3, 8, width), F32),
            pltpu.SemaphoreType.DMA((8,)),
        ],
        name="coarse",
        out_space=pltpu.HBM,
    )(place, w, wd, bound, py, px, full, y0, y1, smoothed)


def solution(mesh):
    in_specs = (P(None, "gz", "gy", None), P(None, "gz", "gy", None), P("gz", "gy", None), P())
    out_specs = P(None, "gz", "gy", None)
    return jax.shard_map(body, mesh=mesh, in_specs=in_specs, out_specs=out_specs, check_vma=False)
```

```python
import jax
import jax.numpy as jnp
from jax import lax
from jax.sharding import PartitionSpec as P
from jax.experimental import pallas as pl
from jax.experimental.pallas import tpu as pltpu

F32 = jnp.float32
BF16 = jnp.bfloat16
CHEB = 3
LOW = 0.1
MID = 0.5 * (1.0 + LOW)
HALF = 0.5 * (1.0 - LOW)
RATIO = (1.0 + LOW) / (1.0 - LOW)
ROWS = 16
BAND = 3 * ROWS
DEEP = 4


def iota(shape, dim):
    return lax.broadcasted_iota(jnp.int32, shape, dim)


def build_matrices(stiff):
    m = 4 * BAND
    row_m = iota((m, 24), 0)
    base_row = 12 * (row_m // (2 * BAND)) + 3 * ((row_m // BAND) % 2) + (row_m // ROWS) % 3
    col_e = iota((m, 24), 1)
    row_k = iota((24, m), 0)
    col_k = iota((24, m), 1)
    base_col = 6 * (col_k // (2 * BAND)) + 3 * ((col_k // BAND) % 2) + (col_k // ROWS) % 3
    mm = iota((m, m), 0)
    kk = iota((m, m), 1)
    gap = (mm % ROWS) - (kk % ROWS) + kk // (2 * BAND)
    blocks = []
    left = []
    for cy in range(2):
        pick = (col_e == base_row + 6 * cy).astype(BF16)
        left.append(jnp.dot(pick, stiff, preferred_element_type=F32).astype(BF16))
    for p in range(2):
        pick = (row_k == base_col + 12 * p).astype(BF16)
        block = jnp.zeros((m, m), F32)
        for cy in range(2):
            full = jnp.dot(left[cy], pick, preferred_element_type=F32)
            block = jnp.where(gap == cy, full, block)
        blocks.append(block.astype(BF16))
    md = iota((m, 2 * ROWS), 0)
    kd = iota((m, 2 * ROWS), 1)
    diag = jnp.zeros((m, 2 * ROWS), F32)
    for cy in range(2):
        own = jnp.sum(
            jnp.where(col_e == base_row + 6 * cy, left[cy].astype(F32), 0.0), axis=1, keepdims=True
        )
        diag = jnp.where((kd // ROWS == cy) & (kd % ROWS == md % ROWS), own, diag)
    return jnp.concatenate(blocks, axis=1), diag.astype(BF16)


def spectral_bound(stiff):
    wide = stiff.astype(F32)
    eye = iota((24, 24), 0) == iota((24, 24), 1)
    own = jnp.sum(jnp.where(eye, wide, 0.0), axis=1, keepdims=True)
    total = jnp.sum(jnp.abs(wide), axis=1, keepdims=True)
    return jnp.max(total / own, axis=0, keepdims=True)


def shift_up(values, width):
    rolled = pltpu.roll(values, width - 1, 1)
    return jnp.where(iota(values.shape, 1) == width - 1, 0.0, rolled)


def shift_down(values):
    rolled = pltpu.roll(values, 1, 1)
    return jnp.where(iota(values.shape, 1) == 0, 0.0, rolled)


def shifted_nodes(values, width):
    return jnp.concatenate([values.astype(BF16), shift_up(values, width).astype(BF16)], axis=0)


def scale_rows(scale):
    down = pltpu.roll(scale, 1, 0)
    down = jnp.where(iota(scale.shape, 0) == 0, 0.0, down)
    return jnp.concatenate([scale.astype(BF16), down.astype(BF16)], axis=0)


def layer_operator(w_ref, nodes, scales):
    def product(layer):
        scale = scales(layer)
        width = scale.shape[-1]
        parts = []
        for p in range(2):
            plane = nodes(layer + p).reshape(6, ROWS, width)
            for cy in range(2):
                masked = plane * scale[cy * ROWS : (cy + 1) * ROWS][None]
                parts.append(masked.reshape(2 * BAND, width))
        return jnp.dot(w_ref[...], jnp.concatenate(parts, axis=0), preferred_element_type=F32)

    return product


def diagonal_operator(wd_ref, scales):
    def product(layer):
        return jnp.dot(wd_ref[...], scales(layer), preferred_element_type=F32)

    return product


def planes_of(lo, hi, product, use, band=BAND):
    carry = product(lo - 1)[2 * band : 4 * band]
    for z in range(lo, hi + 1):
        both = product(z)
        plane = both[0 : 2 * band] + carry
        carry = both[2 * band : 4 * band]
        use(z, plane[0:band] + shift_down(plane[band : 2 * band]))


def inverter(inv_ref, idle_ref, bound, width, past_z, past_y, first, base=0):
    rows = iota((BAND, width), 0) % ROWS
    keep_y = jnp.where((rows >= first) & (past_y == 1), 0.0, 1.0)

    def use(z, diag):
        idle = (diag == 0.0).astype(F32)
        inverse = keep_y / ((diag + idle) * bound)
        if z >= first:
            inverse = inverse * jnp.where(past_z == 1, 0.0, 1.0)
        inv_ref[z - base] = inverse
        idle_ref[z - base] = idle[0:ROWS]

    return use


def tile3(values):
    return jnp.concatenate([values, values, values], axis=0)


def advance(plane, b, x, update, inverse, idle, factors):
    previous, current = factors
    new = current * (inverse * (b - plane - tile3(idle) * x))
    if previous is not None:
        new = previous * update + new
    return x + new, new


def chebyshev_factors():
    factors = [(None, 1.0 / MID)]
    rho = 1.0 / RATIO
    for _ in range(CHEB - 1):
        nxt = 1.0 / (2.0 * RATIO - rho)
        factors.append((nxt * rho, 2.0 * nxt / HALF))
        rho = nxt
    return factors


def weights(gap, where):
    value = jnp.where(gap == 0, 1.0, jnp.where(gap == 1, 0.5, 0.0))
    return jnp.where(where, value, 0.0)


def own_rows(w_ref):
    groups = [w_ref[ROWS * g : ROWS * (g + 1)].astype(F32)[4:12] for g in range(12)]
    return jnp.concatenate(groups, axis=0).astype(BF16)


def restrict_planes():
    out, src = iota((120, 192), 0), iota((120, 192), 1)
    gap_z = jnp.abs(src // 24 - 2 * (out // 24))
    gap_y = jnp.abs(src % 8 - 2 * (out % 8 - 3))
    same = (src // 8) % 3 == (out // 8) % 3
    return (weights(gap_z, same) * weights(gap_y, same)).astype(BF16)


def halve_planes():
    out, src = iota((32, 64), 0), iota((32, 64), 1)
    same = (src // 16 == out // 8) & ((src % 8) // 2 == out % 8 - 3)
    return same.astype(F32).astype(BF16)


def prolong_rows():
    out, src = iota((120, 240), 0), iota((120, 240), 1)
    gap = jnp.abs(out % 8 - 2 * (src % ROWS - 3))
    same = (out // 24 == src // BAND) & ((out // 8) % 3 == (src // ROWS) % 3)
    return weights(gap, same).astype(BF16)


def matrices_kernel(
    e_ref, token_ref, w_ref, wd_ref, bound_ref, wr_ref, rzy_ref, hzy_ref, py_ref, rx_ref, px_ref, pair_ref
):
    stiff = e_ref[...]
    w_ref[...], wd_ref[...] = build_matrices(stiff)
    bound_ref[...] = jnp.broadcast_to(spectral_bound(stiff), (8, 128))
    wr_ref[...] = own_rows(w_ref)
    rzy_ref[...] = restrict_planes()
    hzy_ref[...] = halve_planes()
    py_ref[...] = prolong_rows()
    fine, coarse = iota(rx_ref.shape, 0), iota(rx_ref.shape, 1)
    rx_ref[...] = weights(jnp.abs(fine - 2 * coarse), fine >= 0).astype(BF16)
    pair_ref[...] = (fine // 2 == coarse).astype(F32).astype(BF16)
    coarse, fine = iota(px_ref.shape, 0), iota(px_ref.shape, 1)
    px_ref[...] = weights(jnp.abs(fine - 2 * coarse), fine >= 0).astype(BF16)


def pack_z_kernel(
    place, x_hbm, b_hbm, m_hbm, e_hbm, q0_ref, q1_ref, x_ref, b_ref, m_ref, e_ref, sem
):
    even = 1 - place[0]
    pairs = [(m_hbm, m_ref), (e_hbm, e_ref)]
    for d in range(3):
        pairs += [(x_hbm.at[d], x_ref.at[d]), (b_hbm.at[d], b_ref.at[d])]
    copies = [pltpu.make_async_copy(src, dst, sem.at[i]) for i, (src, dst) in enumerate(pairs)]
    for copy in copies:
        copy.start()
    for copy in copies:
        copy.wait()
    for out, up in ((q0_ref, even), (q1_ref, 1 - even)):
        for d in range(3):
            out[4 * d : 4 * d + 4] = x_ref[d, pl.ds(4 * up, 4)].astype(BF16)
            out[12 + 3 * d : 15 + 3 * d] = b_ref[d, pl.ds(5 * up, 3)].astype(BF16)
        out[21:25] = m_ref[pl.ds(4 * up, 4)].astype(F32).astype(BF16)


def own_planes(x_ref, b_ref, m_ref):
    def at(kind, d, w):
        if kind == "m":
            return m_ref[w - 4].astype(F32)
        return (x_ref if kind == "x" else b_ref)[d, w - 4]

    return at


def borrowed_planes(place, r0_ref, r1_ref):
    odd = place[0] == 1

    def at(kind, d, w):
        low = w < 4
        if kind == "x":
            i = 4 * d + w % 4
        elif kind == "b":
            i = 12 + 3 * d + (w - 1 if low else w - 12)
        else:
            i = 21 + w % 4
        first, second = (r0_ref, r1_ref) if low else (r1_ref, r0_ref)
        return jnp.where(odd, first[i].astype(F32), second[i].astype(F32))

    return at


def flip(values):
    return pltpu.roll(values, 4, 0)


def tiles_of(pairs, load_pairs):
    return (
        [("x", d, pair) for d in range(3) for pair in pairs]
        + [("b", d, pair) for d in range(3) for pair in load_pairs]
        + [("m", 0, pair) for pair in pairs]
    )


OWN_PAIRS = ((4, 5), (6, 7), (8, 9), (10, 11))
OWN_TILES = tiles_of(OWN_PAIRS, OWN_PAIRS)
FAR_TILES = tiles_of(((0, 1), (2, 3), (12, 13), (14, 15)), ((1, 2), (3, 12), (13, 14)))


def pack_rows(place, at, tiles, q0_ref, q1_ref):
    even = place[1] == 0
    for index, (kind, d, (first, second)) in enumerate(tiles):
        a, b = at(kind, d, first), at(kind, d, second)
        head = iota(a.shape, 0) < 4
        up = jnp.where(head, flip(a), b)
        down = jnp.where(head, a, flip(b))
        q0_ref[index] = jnp.where(even, up, down).astype(BF16)
        q1_ref[index] = jnp.where(even, down, up).astype(BF16)


def pack_own_kernel(place, x_ref, b_ref, m_ref, q0_ref, q1_ref, token_ref):
    pack_rows(place, own_planes(x_ref, b_ref, m_ref), OWN_TILES, q0_ref, q1_ref)
    token_ref[...] = jnp.zeros(token_ref.shape, F32)


def pack_far_kernel(place, after_ref, r0_ref, r1_ref, q0_ref, q1_ref):
    pack_rows(place, borrowed_planes(place, r0_ref, r1_ref), FAR_TILES, q0_ref, q1_ref)


def unpack_rows(place, at, tiles, y0_ref, y1_ref, width, use):
    odd = place[1] == 1
    head = iota((8, width), 0) < 4
    for index, (kind, d, pair) in enumerate(tiles):
        low = jnp.where(odd, y0_ref[index].astype(F32), y1_ref[index].astype(F32))
        high = jnp.where(odd, y1_ref[index].astype(F32), y0_ref[index].astype(F32))
        for k, w in enumerate(pair):
            own = flip(at(kind, d, w))
            below = low if k == 0 else flip(low)
            above = flip(high) if k == 0 else high
            block = jnp.concatenate(
                [jnp.where(head, below, own), jnp.where(head, own, above)], axis=0
            )
            use(kind, d, w, block)


def split(values):
    high = values.astype(BF16)
    return high, (values - high.astype(F32)).astype(BF16)


def fine_own_kernel(
    place, w_ref, wd_ref, bound_ref, hzy_ref, pair_ref, x_in, b_in, m_in, y0_ref, y1_ref,
    v0_ref, v1_ref, v2_ref, v3_ref, s_ref, b_ref, x_ref, u_ref, inv_ref, idle_ref, sc_ref,
):
    width = x_in.shape[-1]

    def keep(kind, d, w, block):
        if kind == "m":
            s_ref[w - 4] = scale_rows(block)
        else:
            (x_ref if kind == "x" else b_ref)[w - 4, ROWS * d : ROWS * (d + 1)] = block

    unpack_rows(
        place, own_planes(x_in, b_in, m_in), OWN_TILES, y0_ref, y1_ref, width, keep
    )
    for z in range(8):
        v0_ref[z] = shifted_nodes(x_ref[z], width)

    def scales(layer):
        return s_ref[layer - 4]

    planes_of(
        5, 11, diagonal_operator(wd_ref, scales),
        inverter(inv_ref, idle_ref, bound_ref[0:1, 0:1], width, place[2], place[3], 12, 4),
    )
    levels = (v0_ref, v1_ref, v2_ref, v3_ref)
    for level, factors in enumerate(chebyshev_factors()):
        source, target = levels[level], levels[level + 1]

        def use(w, plane):
            z = w - 4
            update = None if level == 0 else u_ref[z]
            x_ref[z], u_ref[z] = advance(
                plane, b_ref[z], x_ref[z], update, inv_ref[z], idle_ref[z], factors
            )
            target[z] = shifted_nodes(x_ref[z], width)

        planes_of(
            5 + level, 10 - level,
            layer_operator(w_ref, lambda w: source[w - 4], scales), use,
        )
    counts = jnp.dot(
        hzy_ref[...], m_in[...].astype(F32).astype(BF16).reshape(64, width), preferred_element_type=F32
    )
    counts = jnp.dot(counts.astype(BF16), pair_ref[...], preferred_element_type=F32)
    sc_ref[...] = (0.25 * counts).reshape(sc_ref.shape)


def own_part(values, d, head):
    a = values[ROWS * d : ROWS * d + 8]
    b = values[ROWS * d + 8 : ROWS * d + 16]
    return flip(jnp.where(head, b, a))


def fine_rest_kernel(
    place, w_ref, wd_ref, bound_ref, wr_ref, rzy_ref, rx_ref,
    v0_in, v1_in, v2_in, v3_in, s_in, b_mid, x_in, u_in, inv_in, idle_in, sc_ref,
    b_in, r0_ref, r1_ref, y0_ref, y1_ref,
    out_ref, rhs_ref, q0_ref, q1_ref,
    v0_ref, v1_ref, v2_ref, v3_ref, s_ref, b_ref, x_ref, u_ref, inv_ref, idle_ref,
):
    width = b_in.shape[-1]

    def either(mid, far, lo, hi):
        return lambda w: mid[w - 4] if lo <= w <= hi else far[w]

    def keep(kind, d, w, block):
        if kind == "m":
            s_ref[w] = scale_rows(block)
        else:
            (x_ref if kind == "x" else b_ref)[w, ROWS * d : ROWS * (d + 1)] = block

    unpack_rows(
        place, borrowed_planes(place, r0_ref, r1_ref), FAR_TILES, y0_ref, y1_ref, width, keep
    )
    for w in (0, 1, 2, 3, 12, 13, 14, 15):
        v0_ref[w] = shifted_nodes(x_ref[w], width)
    scales = either(s_in, s_ref, 4, 11)
    invert = inverter(inv_ref, idle_ref, bound_ref[0:1, 0:1], width, place[2], place[3], 12)
    planes_of(1, 4, diagonal_operator(wd_ref, scales), invert)
    planes_of(12, 14, diagonal_operator(wd_ref, scales), invert)
    inverse, idles = either(inv_in, inv_ref, 5, 11), either(idle_in, idle_ref, 5, 11)
    loads = either(b_mid, b_ref, 4, 11)
    state = {w: (x_ref, u_ref, w) for w in range(16)}
    state.update({w: (x_in, u_in, w - 4) for w in range(4, 12)})
    near = (v0_in, v1_in, v2_in, v3_in)
    far = (v0_ref, v1_ref, v2_ref, v3_ref)
    for level, factors in enumerate(chebyshev_factors()):
        target = far[level + 1]

        def use(w, plane):
            xs, us, z = state[w]
            update = None if level == 0 else us[z]
            x_ref[w], u_ref[w] = advance(
                plane, loads(w), xs[z], update, inverse(w), idles(w), factors
            )
            state[w] = (x_ref, u_ref, w)
            target[w] = shifted_nodes(x_ref[w], width)

        product = layer_operator(
            w_ref, either(near[level], far[level], 4 + level, 11 - level), scales
        )
        planes_of(1 + level, 4 + level, product, use)
        planes_of(11 - level, 14 - level, product, use)

    head = iota((8, width), 0) < 4
    parts = []

    def use(w, plane):
        idle = own_part(idles(w), 0, head)
        xs, _, z = state[w]
        final = xs[z]
        for d in range(3):
            x = own_part(final, d, head)
            out_ref[d, w - 4] = x
            parts.append(b_in[d, w - 4] - plane[8 * d : 8 * d + 8] - idle * x)

    planes_of(4, 11, layer_operator(wr_ref, either(near[3], far[3], 7, 8), scales), use, 24)
    residual = jnp.concatenate(parts, axis=0).astype(BF16)
    sums = jnp.dot(rzy_ref[...], residual, preferred_element_type=F32)
    sums = jnp.dot(sums.astype(BF16), rx_ref[...], preferred_element_type=F32)
    rhs_ref[...] = sums.reshape(rhs_ref.shape)
    even = 1 - place[0]
    for out, up in ((q0_ref, even), (q1_ref, 1 - even)):
        out[0:9] = rhs_ref[pl.ds(6 * up, 9)].astype(BF16)
        out[9:12] = sc_ref[pl.ds(up, 3)].astype(BF16)


def pack_coarse_kernel(place, rhs_ref, sc_ref, r0_ref, r1_ref, full_ref, q0_ref, q1_ref):
    odd = place[0] == 1
    even_y = place[1] == 0
    head = iota(rhs_ref.shape[1:], 0) < 4
    kept = []

    def low(i):
        return jnp.where(odd, r0_ref[i].astype(F32), r1_ref[i].astype(F32))

    def high(i):
        return jnp.where(odd, r1_ref[i].astype(F32), r0_ref[i].astype(F32))

    for z in range(10):
        c = z - 3
        for d in range(4):
            value = jnp.zeros(rhs_ref.shape[1:], F32)
            if d < 3:
                if -2 <= c <= 0:
                    value = value + low(3 * (c + 2) + d)
                if 4 <= c <= 6:
                    value = value + high(3 * (c - 4) + d)
                if 0 <= c <= 4:
                    value = value + rhs_ref[3 * c + d]
            else:
                if c <= -1:
                    value = low(9 + c + 3)
                elif c >= 4:
                    value = high(9 + c - 4)
                else:
                    value = sc_ref[c]
            full_ref[4 * z + d] = value
            kept.append(value)
    for i in range(20):
        a, b = kept[2 * i], kept[2 * i + 1]
        up = jnp.where(head, flip(a), b)
        down = jnp.where(head, pltpu.roll(a, 5, 0), pltpu.roll(b, 1, 0))
        q0_ref[i] = jnp.where(even_y, up, down).astype(BF16)
        q1_ref[i] = jnp.where(even_y, down, up).astype(BF16)


def coarse_kernel(
    place, w_ref, wd_ref, bound_ref, py_ref, px_ref, full_ref, y0_ref, y1_ref, smooth_ref, out_hbm,
    v_ref, s_ref, b_ref, x_ref, u_ref, inv_ref, idle_ref, out_ref, sem,
):
    half = full_ref.shape[-1]
    width = 2 * half
    bound = bound_ref[0:1, 0:1]
    odd = place[1] == 1
    rows8 = iota((8, half), 0)
    for z in range(10):
        for d in range(4):
            i = 4 * z + d
            low = jnp.where(odd, y0_ref[i // 2].astype(F32), y1_ref[i // 2].astype(F32))
            high = jnp.where(odd, y1_ref[i // 2].astype(F32), y0_ref[i // 2].astype(F32))
            if i % 2:
                low = flip(low)
            high = pltpu.roll(high, 3 if i % 2 else 7, 0)
            first = (
                full_ref[i] + jnp.where(rows8 < 4, low, 0.0) + jnp.where(rows8 == 7, high, 0.0)
            )
            block = jnp.concatenate([first, jnp.where(rows8 < 3, high, 0.0)], axis=0)
            if d < 3:
                b_ref[z, ROWS * d : ROWS * (d + 1)] = block
            else:
                s_ref[z] = scale_rows(block)
    def scales(layer):
        return s_ref[layer]

    planes_of(
        1, 9, diagonal_operator(wd_ref, scales),
        inverter(inv_ref, idle_ref, bound, half, place[2], place[3], 7),
    )
    factors = chebyshev_factors()
    for z in range(1, 10):
        update = factors[0][1] * (inv_ref[z] * b_ref[z])
        u_ref[z] = update
        x_ref[z] = update
        v_ref[z] = shifted_nodes(update, half)
    product = layer_operator(w_ref, lambda z: v_ref[z], scales)
    for level in (1, 2):

        def use(z, plane):
            x_ref[z], u_ref[z] = advance(
                plane, b_ref[z], x_ref[z], u_ref[z], inv_ref[z], idle_ref[z], factors[level]
            )
            v_ref[z] = shifted_nodes(x_ref[z], half)

        planes_of(1 + level, 9 - level if level == 1 else 7, product, use)

    coarse = jnp.concatenate([v_ref[3 + k, 0:BAND] for k in range(5)], axis=0)
    rows = jnp.dot(py_ref[...], coarse, preferred_element_type=F32)
    high, low = split(rows)
    wide = jnp.dot(jnp.concatenate([high, low], axis=0), px_ref[...], preferred_element_type=F32)
    wide = (wide[0:120] + wide[120:240]).reshape(5, 3, 8, width)
    copies = []
    for z in range(8):
        k = z // 2
        plane = wide[k] if z % 2 == 0 else 0.5 * (wide[k] + wide[k + 1])
        out_ref[z] = smooth_ref[:, z] + plane
        copies.append(pltpu.make_async_copy(out_ref.at[z], out_hbm.at[:, z], sem.at[z]))
        copies[-1].start()
    for copy in copies:
        copy.wait()


def swap(array, axis, offset):
    length = lax.axis_size(axis)
    pairs = []
    for i in range(offset, length - 1, 2):
        pairs += [(i, i + 1), (i + 1, i)]
    return lax.ppermute(array, axis, pairs)


def whereabouts():
    gz, gy = lax.axis_index("gz"), lax.axis_index("gy")
    return (
        lax.rem(gz, 2),
        lax.rem(gy, 2),
        (gz == lax.axis_size("gz") - 1).astype(jnp.int32),
        (gy == lax.axis_size("gy") - 1).astype(jnp.int32),
    )


def call(
    body, out_shape, n_in, scratch=(), name=None, place=True, space=pltpu.VMEM, out_space=pltpu.VMEM
):
    vmem = pl.BlockSpec(memory_space=out_space)
    single = not isinstance(out_shape, (tuple, list))
    return pl.pallas_call(
        (lambda *refs: body(whereabouts(), *refs)) if place else body,
        out_shape=out_shape,
        in_specs=[pl.BlockSpec(memory_space=space)] * n_in,
        out_specs=vmem if single else [vmem] * len(out_shape),
        scratch_shapes=list(scratch),
        compiler_params=pltpu.CompilerParams(vmem_limit_bytes=24 << 20),
        name=name,
    )


def body(applied_load, start_field, bone_mask, element_stiffness):
    width = applied_load.shape[-1]
    half = width // 2
    shape = jax.ShapeDtypeStruct
    packet = shape((25, 8, width), BF16)
    arguments = (start_field, applied_load, bone_mask, element_stiffness)
    q0, q1, start_field, applied_load, bone_mask, stiff = call(
        pack_z_kernel,
        [packet, packet] + [shape(a.shape, a.dtype) for a in arguments],
        4,
        [pltpu.SemaphoreType.DMA((8,))],
        name="pack_z",
        space=pltpu.HBM,
    )(*[pltpu.with_memory_space_constraint(a, pltpu.HBM) for a in arguments])
    r1 = swap(q1, "gz", 1)
    r0 = swap(q0, "gz", 0)
    packet = shape((len(OWN_TILES), 8, width), BF16)
    q0, q1, token = call(
        pack_own_kernel, [packet, packet, shape((8, 128), F32)], 3, name="pack_own"
    )(start_field, applied_load, bone_mask)
    yn1 = swap(q1, "gy", 1)
    yn0 = swap(q0, "gy", 0)
    w, wd, bound, wr, rzy, hzy, py, rx, px, pair = call(
        matrices_kernel,
        [
            shape((4 * BAND, 8 * BAND), BF16),
            shape((4 * BAND, 2 * ROWS), BF16),
            shape((8, 128), F32),
            shape((2 * BAND, 8 * BAND), BF16),
            shape((120, 192), BF16),
            shape((32, 64), BF16),
            shape((120, 240), BF16),
            shape((width, half), BF16),
            shape((half, width), BF16),
            shape((width, half), BF16),
        ],
        2,
        name="matrices",
        place=False,
    )(stiff, token)

    packet = shape((len(FAR_TILES), 8, width), BF16)
    q0, q1 = call(pack_far_kernel, [packet, packet], 3, name="pack_far")(bound, r0, r1)
    yf1 = swap(q1, "gy", 1)
    yf0 = swap(q0, "gy", 0)
    def field(count, rows, dtype):
        return (count, rows, width), dtype

    kinds = [(2 * BAND, BF16)] * 4 + [(2 * ROWS, BF16)] + [(BAND, F32)] * 4 + [(ROWS, F32)]
    *middle, scale = call(
        fine_own_kernel,
        [shape(*field(8, *kind)) for kind in kinds] + [shape((4, 8, half), F32)],
        10,
        name="fine_own",
    )(w, wd, bound, hzy, pair, start_field, applied_load, bone_mask, yn0, yn1)
    packet = shape((12, 8, half), BF16)
    smoothed, rhs, q0, q1 = call(
        fine_rest_kernel,
        [shape(start_field.shape, F32), shape((15, 8, half), F32), packet, packet],
        22,
        [pltpu.VMEM(*field(16, *kind)) for kind in kinds],
        name="fine_rest",
    )(w, wd, bound, wr, rzy, rx, *middle, scale, applied_load, r0, r1, yf0, yf1)
    r1 = swap(q1, "gz", 1)
    r0 = swap(q0, "gz", 0)
    packet = shape((20, 8, half), BF16)
    full, q0, q1 = call(
        pack_coarse_kernel,
        [shape((40, 8, half), F32), packet, packet],
        4,
        name="pack_coarse",
    )(rhs, scale, r0, r1)
    y1 = swap(q1, "gy", 1)
    y0 = swap(q0, "gy", 0)
    coarse_plane = pltpu.VMEM((11, BAND, half), F32)
    return call(
        coarse_kernel,
        shape(start_field.shape, F32),
        9,
        [
            pltpu.VMEM((11, 2 * BAND, half), BF16),
            pltpu.VMEM((11, 2 * ROWS, half), BF16),
            coarse_plane,
            coarse_plane,
            coarse_plane,
            coarse_plane,
            pltpu.VMEM((11, ROWS, half), F32),
            pltpu.VMEM((8, 3, 8, width), F32),
            pltpu.SemaphoreType.DMA((8,)),
        ],
        name="coarse",
        out_space=pltpu.HBM,
    )(w, wd, bound, py, px, full, y0, y1, smoothed)


def solution(mesh):
    in_specs = (P(None, "gz", "gy", None), P(None, "gz", "gy", None), P("gz", "gy", None), P())
    out_specs = P(None, "gz", "gy", None)
    return jax.shard_map(body, mesh=mesh, in_specs=in_specs, out_specs=out_specs, check_vma=False)
```

```python
import jax
import jax.numpy as jnp
from jax import lax
from jax.sharding import PartitionSpec as P
from jax.experimental import pallas as pl
from jax.experimental.pallas import tpu as pltpu

F32 = jnp.float32
BF16 = jnp.bfloat16
CHEB = 3
LOW = 0.1
MID = 0.5 * (1.0 + LOW)
HALF = 0.5 * (1.0 - LOW)
RATIO = (1.0 + LOW) / (1.0 - LOW)
ROWS = 16
BAND = 3 * ROWS
DEEP = 4


def iota(shape, dim):
    return lax.broadcasted_iota(jnp.int32, shape, dim)


def build_matrices(stiff):
    m = 4 * BAND
    row_m = iota((m, 24), 0)
    base_row = 12 * (row_m // (2 * BAND)) + 3 * ((row_m // BAND) % 2) + (row_m // ROWS) % 3
    col_e = iota((m, 24), 1)
    row_k = iota((24, m), 0)
    col_k = iota((24, m), 1)
    base_col = 6 * (col_k // (2 * BAND)) + 3 * ((col_k // BAND) % 2) + (col_k // ROWS) % 3
    mm = iota((m, m), 0)
    kk = iota((m, m), 1)
    gap = (mm % ROWS) - (kk % ROWS) + kk // (2 * BAND)
    blocks = []
    left = []
    for cy in range(2):
        pick = (col_e == base_row + 6 * cy).astype(BF16)
        left.append(jnp.dot(pick, stiff, preferred_element_type=F32).astype(BF16))
    for p in range(2):
        pick = (row_k == base_col + 12 * p).astype(BF16)
        block = jnp.zeros((m, m), F32)
        for cy in range(2):
            full = jnp.dot(left[cy], pick, preferred_element_type=F32)
            block = jnp.where(gap == cy, full, block)
        blocks.append(block.astype(BF16))
    md = iota((m, 2 * ROWS), 0)
    kd = iota((m, 2 * ROWS), 1)
    diag = jnp.zeros((m, 2 * ROWS), F32)
    for cy in range(2):
        own = jnp.sum(
            jnp.where(col_e == base_row + 6 * cy, left[cy].astype(F32), 0.0), axis=1, keepdims=True
        )
        diag = jnp.where((kd // ROWS == cy) & (kd % ROWS == md % ROWS), own, diag)
    return jnp.concatenate(blocks, axis=1), diag.astype(BF16)


def spectral_bound(stiff):
    wide = stiff.astype(F32)
    eye = iota((24, 24), 0) == iota((24, 24), 1)
    own = jnp.sum(jnp.where(eye, wide, 0.0), axis=1, keepdims=True)
    total = jnp.sum(jnp.abs(wide), axis=1, keepdims=True)
    return jnp.max(total / own, axis=0, keepdims=True)


def shift_up(values, width):
    rolled = pltpu.roll(values, width - 1, 1)
    return jnp.where(iota(values.shape, 1) == width - 1, 0.0, rolled)


def shift_down(values):
    rolled = pltpu.roll(values, 1, 1)
    return jnp.where(iota(values.shape, 1) == 0, 0.0, rolled)


def shifted_nodes(values, width):
    return jnp.concatenate([values.astype(BF16), shift_up(values, width).astype(BF16)], axis=0)


def scale_rows(scale):
    down = pltpu.roll(scale, 1, 0)
    down = jnp.where(iota(scale.shape, 0) == 0, 0.0, down)
    return jnp.concatenate([scale.astype(BF16), down.astype(BF16)], axis=0)


def half_of(matrix_ref, half):
    if half is None:
        return matrix_ref[...]
    rows = matrix_ref.shape[0] // 2
    return matrix_ref[half * rows : (half + 1) * rows]


def layer_operator(w_ref, nodes, scales):
    def product(layer, half=None):
        scale = scales(layer)
        width = scale.shape[-1]
        parts = []
        for p in range(2):
            plane = nodes(layer + p).reshape(6, ROWS, width)
            for cy in range(2):
                masked = plane * scale[cy * ROWS : (cy + 1) * ROWS][None]
                parts.append(masked.reshape(2 * BAND, width))
        matrix = half_of(w_ref, half)
        return jnp.dot(matrix, jnp.concatenate(parts, axis=0), preferred_element_type=F32)

    return product


def diagonal_operator(wd_ref, scales):
    def product(layer, half=None):
        return jnp.dot(half_of(wd_ref, half), scales(layer), preferred_element_type=F32)

    return product


def planes_of(lo, hi, product, use, band=BAND, below=None, above=None):
    carry = product(lo - 1, 1) if below is None else below
    for z in range(lo, hi + 1):
        if z < hi:
            both = product(z)
            part, rest = both[0 : 2 * band], both[2 * band : 4 * band]
        else:
            part, rest = product(z, 0) if above is None else above, None
        plane = part + carry
        carry = rest
        use(z, plane[0:band] + shift_down(plane[band : 2 * band]))


def inverter(inv_ref, idle_ref, bound, width, past_z, past_y, first, base=0):
    rows = iota((BAND, width), 0) % ROWS
    keep_y = jnp.where((rows >= first) & (past_y == 1), 0.0, 1.0)

    def use(z, diag):
        idle = (diag == 0.0).astype(F32)
        inverse = keep_y / ((diag + idle) * bound)
        if z >= first:
            inverse = inverse * jnp.where(past_z == 1, 0.0, 1.0)
        inv_ref[z - base] = inverse
        idle_ref[z - base] = idle[0:ROWS]

    return use


def tile3(values):
    return jnp.concatenate([values, values, values], axis=0)


def advance(plane, b, x, update, inverse, idle, factors):
    previous, current = factors
    new = current * (inverse * (b - plane - tile3(idle) * x))
    if previous is not None:
        new = previous * update + new
    return x + new, new


def chebyshev_factors():
    factors = [(None, 1.0 / MID)]
    rho = 1.0 / RATIO
    for _ in range(CHEB - 1):
        nxt = 1.0 / (2.0 * RATIO - rho)
        factors.append((nxt * rho, 2.0 * nxt / HALF))
        rho = nxt
    return factors


def weights(gap, where):
    value = jnp.where(gap == 0, 1.0, jnp.where(gap == 1, 0.5, 0.0))
    return jnp.where(where, value, 0.0)


def own_rows(w_ref):
    groups = [w_ref[ROWS * g : ROWS * (g + 1)].astype(F32)[4:12] for g in range(12)]
    return jnp.concatenate(groups, axis=0).astype(BF16)


def restrict_planes():
    out, src = iota((120, 192), 0), iota((120, 192), 1)
    gap_z = jnp.abs(src // 24 - 2 * (out // 24))
    gap_y = jnp.abs(src % 8 - 2 * (out % 8 - 3))
    same = (src // 8) % 3 == (out // 8) % 3
    return (weights(gap_z, same) * weights(gap_y, same)).astype(BF16)


def halve_planes():
    out, src = iota((32, 64), 0), iota((32, 64), 1)
    same = (src // 16 == out // 8) & ((src % 8) // 2 == out % 8 - 3)
    return same.astype(F32).astype(BF16)


def prolong_rows():
    out, src = iota((120, 240), 0), iota((120, 240), 1)
    gap = jnp.abs(out % 8 - 2 * (src % ROWS - 3))
    same = (out // 24 == src // BAND) & ((out // 8) % 3 == (src // ROWS) % 3)
    return weights(gap, same).astype(BF16)


def matrices_kernel(
    e_ref, token_ref, w_ref, wd_ref, bound_ref, wr_ref, rzy_ref, hzy_ref, py_ref, rx_ref, px_ref, pair_ref
):
    stiff = e_ref[...]
    w_ref[...], wd_ref[...] = build_matrices(stiff)
    bound_ref[...] = jnp.broadcast_to(spectral_bound(stiff), (8, 128))
    wr_ref[...] = own_rows(w_ref)
    rzy_ref[...] = restrict_planes()
    hzy_ref[...] = halve_planes()
    py_ref[...] = prolong_rows()
    fine, coarse = iota(rx_ref.shape, 0), iota(rx_ref.shape, 1)
    rx_ref[...] = weights(jnp.abs(fine - 2 * coarse), fine >= 0).astype(BF16)
    pair_ref[...] = (fine // 2 == coarse).astype(F32).astype(BF16)
    coarse, fine = iota(px_ref.shape, 0), iota(px_ref.shape, 1)
    px_ref[...] = weights(jnp.abs(fine - 2 * coarse), fine >= 0).astype(BF16)


def pack_z_kernel(
    place, x_hbm, b_hbm, m_hbm, e_hbm, q0_ref, q1_ref, x_ref, b_ref, m_ref, e_ref, sem
):
    even = 1 - place[0]
    pairs = [(m_hbm, m_ref), (e_hbm, e_ref)]
    for d in range(3):
        pairs += [(x_hbm.at[d], x_ref.at[d]), (b_hbm.at[d], b_ref.at[d])]
    copies = [pltpu.make_async_copy(src, dst, sem.at[i]) for i, (src, dst) in enumerate(pairs)]
    for copy in copies:
        copy.start()
    for copy in copies:
        copy.wait()
    for out, up in ((q0_ref, even), (q1_ref, 1 - even)):
        for d in range(3):
            out[4 * d : 4 * d + 4] = x_ref[d, pl.ds(4 * up, 4)].astype(BF16)
            out[12 + 3 * d : 15 + 3 * d] = b_ref[d, pl.ds(5 * up, 3)].astype(BF16)
        out[21:25] = m_ref[pl.ds(4 * up, 4)].astype(F32).astype(BF16)


def own_planes(x_ref, b_ref, m_ref):
    def at(kind, d, w):
        if kind == "m":
            return m_ref[w - 4].astype(F32)
        return (x_ref if kind == "x" else b_ref)[d, w - 4]

    return at


def borrowed_planes(place, r0_ref, r1_ref):
    odd = place[0] == 1

    def at(kind, d, w):
        low = w < 4
        if kind == "x":
            i = 4 * d + w % 4
        elif kind == "b":
            i = 12 + 3 * d + (w - 1 if low else w - 12)
        else:
            i = 21 + w % 4
        first, second = (r0_ref, r1_ref) if low else (r1_ref, r0_ref)
        return jnp.where(odd, first[i].astype(F32), second[i].astype(F32))

    return at


def flip(values):
    return pltpu.roll(values, 4, 0)


def tiles_of(pairs, load_pairs):
    return (
        [("x", d, pair) for d in range(3) for pair in pairs]
        + [("b", d, pair) for d in range(3) for pair in load_pairs]
        + [("m", 0, pair) for pair in pairs]
    )


OWN_PAIRS = ((4, 5), (6, 7), (8, 9), (10, 11))
OWN_TILES = tiles_of(OWN_PAIRS, OWN_PAIRS)
FAR_TILES = tiles_of(((0, 1), (2, 3), (12, 13), (14, 15)), ((1, 2), (3, 12), (13, 14)))


def pack_rows(place, at, tiles, q0_ref, q1_ref):
    even = place[1] == 0
    for index, (kind, d, (first, second)) in enumerate(tiles):
        a, b = at(kind, d, first), at(kind, d, second)
        head = iota(a.shape, 0) < 4
        up = jnp.where(head, flip(a), b)
        down = jnp.where(head, a, flip(b))
        q0_ref[index] = jnp.where(even, up, down).astype(BF16)
        q1_ref[index] = jnp.where(even, down, up).astype(BF16)


def pack_own_kernel(place, x_ref, b_ref, m_ref, q0_ref, q1_ref, token_ref):
    pack_rows(place, own_planes(x_ref, b_ref, m_ref), OWN_TILES, q0_ref, q1_ref)
    token_ref[...] = jnp.zeros(token_ref.shape, F32)


def pack_far_kernel(place, after_ref, r0_ref, r1_ref, q0_ref, q1_ref):
    pack_rows(place, borrowed_planes(place, r0_ref, r1_ref), FAR_TILES, q0_ref, q1_ref)


def unpack_rows(place, at, tiles, y0_ref, y1_ref, width, use):
    odd = place[1] == 1
    head = iota((8, width), 0) < 4
    for index, (kind, d, pair) in enumerate(tiles):
        low = jnp.where(odd, y0_ref[index].astype(F32), y1_ref[index].astype(F32))
        high = jnp.where(odd, y1_ref[index].astype(F32), y0_ref[index].astype(F32))
        for k, w in enumerate(pair):
            own = flip(at(kind, d, w))
            below = low if k == 0 else flip(low)
            above = flip(high) if k == 0 else high
            block = jnp.concatenate(
                [jnp.where(head, below, own), jnp.where(head, own, above)], axis=0
            )
            use(kind, d, w, block)


def split(values):
    high = values.astype(BF16)
    return high, (values - high.astype(F32)).astype(BF16)


def fine_own_kernel(
    place, w_ref, wd_ref, bound_ref, hzy_ref, pair_ref, x_in, b_in, m_in, y0_ref, y1_ref,
    v0_ref, v1_ref, v2_ref, v3_ref, s_ref, b_ref, x_ref, u_ref, inv_ref, idle_ref, seam_ref, sc_ref,
):
    width = x_in.shape[-1]

    def keep(kind, d, w, block):
        if kind == "m":
            s_ref[w - 4] = scale_rows(block)
        else:
            (x_ref if kind == "x" else b_ref)[w - 4, ROWS * d : ROWS * (d + 1)] = block

    unpack_rows(
        place, own_planes(x_in, b_in, m_in), OWN_TILES, y0_ref, y1_ref, width, keep
    )
    for z in range(8):
        v0_ref[z] = shifted_nodes(x_ref[z], width)

    def scales(layer):
        return s_ref[layer - 4]

    planes_of(
        5, 11, diagonal_operator(wd_ref, scales),
        inverter(inv_ref, idle_ref, bound_ref[0:1, 0:1], width, place[2], place[3], 12, 4),
    )
    levels = (v0_ref, v1_ref, v2_ref, v3_ref)
    for level, factors in enumerate(chebyshev_factors()):
        source, target = levels[level], levels[level + 1]

        def use(w, plane):
            z = w - 4
            update = None if level == 0 else u_ref[z]
            x_ref[z], u_ref[z] = advance(
                plane, b_ref[z], x_ref[z], update, inv_ref[z], idle_ref[z], factors
            )
            target[z] = shifted_nodes(x_ref[z], width)

        lo, hi = 5 + level, 10 - level
        product = layer_operator(w_ref, lambda w: source[w - 4], scales)
        first, last = product(lo - 1), product(hi)
        seam_ref[2 * level] = first[0 : 2 * BAND]
        seam_ref[2 * level + 1] = last[2 * BAND : 4 * BAND]
        planes_of(
            lo, hi, product, use, below=first[2 * BAND : 4 * BAND], above=last[0 : 2 * BAND]
        )
    counts = jnp.dot(
        hzy_ref[...], m_in[...].astype(F32).astype(BF16).reshape(64, width), preferred_element_type=F32
    )
    counts = jnp.dot(counts.astype(BF16), pair_ref[...], preferred_element_type=F32)
    sc_ref[...] = (0.25 * counts).reshape(sc_ref.shape)


def own_part(values, d, head):
    a = values[ROWS * d : ROWS * d + 8]
    b = values[ROWS * d + 8 : ROWS * d + 16]
    return flip(jnp.where(head, b, a))


def fine_rest_kernel(
    place, w_ref, wd_ref, bound_ref, wr_ref, rzy_ref, rx_ref,
    v0_in, v1_in, v2_in, v3_in, s_in, b_mid, x_in, u_in, inv_in, idle_in, seam_ref, sc_ref,
    b_in, r0_ref, r1_ref, y0_ref, y1_ref,
    out_ref, rhs_ref, q0_ref, q1_ref,
    v0_ref, v1_ref, v2_ref, v3_ref, s_ref, b_ref, x_ref, u_ref, inv_ref, idle_ref,
):
    width = b_in.shape[-1]

    def either(mid, far, lo, hi):
        return lambda w: mid[w - 4] if lo <= w <= hi else far[w]

    def keep(kind, d, w, block):
        if kind == "m":
            s_ref[w] = scale_rows(block)
        else:
            (x_ref if kind == "x" else b_ref)[w, ROWS * d : ROWS * (d + 1)] = block

    unpack_rows(
        place, borrowed_planes(place, r0_ref, r1_ref), FAR_TILES, y0_ref, y1_ref, width, keep
    )
    for w in (0, 1, 2, 3, 12, 13, 14, 15):
        v0_ref[w] = shifted_nodes(x_ref[w], width)
    scales = either(s_in, s_ref, 4, 11)
    invert = inverter(inv_ref, idle_ref, bound_ref[0:1, 0:1], width, place[2], place[3], 12)
    planes_of(1, 4, diagonal_operator(wd_ref, scales), invert)
    planes_of(12, 14, diagonal_operator(wd_ref, scales), invert)
    inverse, idles = either(inv_in, inv_ref, 5, 11), either(idle_in, idle_ref, 5, 11)
    loads = either(b_mid, b_ref, 4, 11)
    state = {w: (x_ref, u_ref, w) for w in range(16)}
    state.update({w: (x_in, u_in, w - 4) for w in range(4, 12)})
    near = (v0_in, v1_in, v2_in, v3_in)
    far = (v0_ref, v1_ref, v2_ref, v3_ref)
    for level, factors in enumerate(chebyshev_factors()):
        target = far[level + 1]

        def use(w, plane):
            xs, us, z = state[w]
            update = None if level == 0 else us[z]
            x_ref[w], u_ref[w] = advance(
                plane, loads(w), xs[z], update, inverse(w), idles(w), factors
            )
            state[w] = (x_ref, u_ref, w)
            target[w] = shifted_nodes(x_ref[w], width)

        product = layer_operator(
            w_ref, either(near[level], far[level], 4 + level, 11 - level), scales
        )
        planes_of(1 + level, 4 + level, product, use, above=seam_ref[2 * level])
        planes_of(11 - level, 14 - level, product, use, below=seam_ref[2 * level + 1])

    head = iota((8, width), 0) < 4
    parts = []

    def use(w, plane):
        idle = own_part(idles(w), 0, head)
        xs, _, z = state[w]
        final = xs[z]
        for d in range(3):
            x = own_part(final, d, head)
            out_ref[d, w - 4] = x
            parts.append(b_in[d, w - 4] - plane[8 * d : 8 * d + 8] - idle * x)

    planes_of(4, 11, layer_operator(wr_ref, either(near[3], far[3], 7, 8), scales), use, 24)
    residual = jnp.concatenate(parts, axis=0).astype(BF16)
    sums = jnp.dot(rzy_ref[...], residual, preferred_element_type=F32)
    sums = jnp.dot(sums.astype(BF16), rx_ref[...], preferred_element_type=F32)
    rhs_ref[...] = sums.reshape(rhs_ref.shape)
    even = 1 - place[0]
    for out, up in ((q0_ref, even), (q1_ref, 1 - even)):
        out[0:9] = rhs_ref[pl.ds(6 * up, 9)].astype(BF16)
        out[9:12] = sc_ref[pl.ds(up, 3)].astype(BF16)


def pack_coarse_kernel(place, rhs_ref, sc_ref, r0_ref, r1_ref, full_ref, q0_ref, q1_ref):
    odd = place[0] == 1
    even_y = place[1] == 0
    head = iota(rhs_ref.shape[1:], 0) < 4
    kept = []

    def low(i):
        return jnp.where(odd, r0_ref[i].astype(F32), r1_ref[i].astype(F32))

    def high(i):
        return jnp.where(odd, r1_ref[i].astype(F32), r0_ref[i].astype(F32))

    for z in range(10):
        c = z - 3
        for d in range(4):
            value = jnp.zeros(rhs_ref.shape[1:], F32)
            if d < 3:
                if -2 <= c <= 0:
                    value = value + low(3 * (c + 2) + d)
                if 4 <= c <= 6:
                    value = value + high(3 * (c - 4) + d)
                if 0 <= c <= 4:
                    value = value + rhs_ref[3 * c + d]
            else:
                if c <= -1:
                    value = low(9 + c + 3)
                elif c >= 4:
                    value = high(9 + c - 4)
                else:
                    value = sc_ref[c]
            full_ref[4 * z + d] = value
            kept.append(value)
    for i in range(20):
        a, b = kept[2 * i], kept[2 * i + 1]
        up = jnp.where(head, flip(a), b)
        down = jnp.where(head, pltpu.roll(a, 5, 0), pltpu.roll(b, 1, 0))
        q0_ref[i] = jnp.where(even_y, up, down).astype(BF16)
        q1_ref[i] = jnp.where(even_y, down, up).astype(BF16)


def coarse_kernel(
    place, w_ref, wd_ref, bound_ref, py_ref, px_ref, full_ref, y0_ref, y1_ref, smooth_ref, out_hbm,
    v_ref, s_ref, b_ref, x_ref, u_ref, inv_ref, idle_ref, out_ref, sem,
):
    half = full_ref.shape[-1]
    width = 2 * half
    bound = bound_ref[0:1, 0:1]
    odd = place[1] == 1
    rows8 = iota((8, half), 0)
    for z in range(10):
        for d in range(4):
            i = 4 * z + d
            low = jnp.where(odd, y0_ref[i // 2].astype(F32), y1_ref[i // 2].astype(F32))
            high = jnp.where(odd, y1_ref[i // 2].astype(F32), y0_ref[i // 2].astype(F32))
            if i % 2:
                low = flip(low)
            high = pltpu.roll(high, 3 if i % 2 else 7, 0)
            first = (
                full_ref[i] + jnp.where(rows8 < 4, low, 0.0) + jnp.where(rows8 == 7, high, 0.0)
            )
            block = jnp.concatenate([first, jnp.where(rows8 < 3, high, 0.0)], axis=0)
            if d < 3:
                b_ref[z, ROWS * d : ROWS * (d + 1)] = block
            else:
                s_ref[z] = scale_rows(block)
    def scales(layer):
        return s_ref[layer]

    planes_of(
        1, 9, diagonal_operator(wd_ref, scales),
        inverter(inv_ref, idle_ref, bound, half, place[2], place[3], 7),
    )
    factors = chebyshev_factors()
    for z in range(1, 10):
        update = factors[0][1] * (inv_ref[z] * b_ref[z])
        u_ref[z] = update
        x_ref[z] = update
        v_ref[z] = shifted_nodes(update, half)
    product = layer_operator(w_ref, lambda z: v_ref[z], scales)
    for level in (1, 2):

        def use(z, plane):
            x_ref[z], u_ref[z] = advance(
                plane, b_ref[z], x_ref[z], u_ref[z], inv_ref[z], idle_ref[z], factors[level]
            )
            v_ref[z] = shifted_nodes(x_ref[z], half)

        planes_of(1 + level, 9 - level if level == 1 else 7, product, use)

    coarse = jnp.concatenate([v_ref[3 + k, 0:BAND] for k in range(5)], axis=0)
    rows = jnp.dot(py_ref[...], coarse, preferred_element_type=F32)
    high, low = split(rows)
    wide = jnp.dot(jnp.concatenate([high, low], axis=0), px_ref[...], preferred_element_type=F32)
    wide = (wide[0:120] + wide[120:240]).reshape(5, 3, 8, width)
    copies = []
    for z in range(8):
        k = z // 2
        plane = wide[k] if z % 2 == 0 else 0.5 * (wide[k] + wide[k + 1])
        out_ref[z] = smooth_ref[:, z] + plane
        copies.append(pltpu.make_async_copy(out_ref.at[z], out_hbm.at[:, z], sem.at[z]))
        copies[-1].start()
    for copy in copies:
        copy.wait()


def swap(array, axis, offset):
    length = lax.axis_size(axis)
    pairs = []
    for i in range(offset, length - 1, 2):
        pairs += [(i, i + 1), (i + 1, i)]
    return lax.ppermute(array, axis, pairs)


def whereabouts():
    gz, gy = lax.axis_index("gz"), lax.axis_index("gy")
    return (
        lax.rem(gz, 2),
        lax.rem(gy, 2),
        (gz == lax.axis_size("gz") - 1).astype(jnp.int32),
        (gy == lax.axis_size("gy") - 1).astype(jnp.int32),
    )


def call(
    body, out_shape, n_in, scratch=(), name=None, place=True, space=pltpu.VMEM, out_space=pltpu.VMEM
):
    vmem = pl.BlockSpec(memory_space=out_space)
    single = not isinstance(out_shape, (tuple, list))
    return pl.pallas_call(
        (lambda *refs: body(whereabouts(), *refs)) if place else body,
        out_shape=out_shape,
        in_specs=[pl.BlockSpec(memory_space=space)] * n_in,
        out_specs=vmem if single else [vmem] * len(out_shape),
        scratch_shapes=list(scratch),
        compiler_params=pltpu.CompilerParams(vmem_limit_bytes=24 << 20),
        name=name,
    )


def body(applied_load, start_field, bone_mask, element_stiffness):
    width = applied_load.shape[-1]
    half = width // 2
    shape = jax.ShapeDtypeStruct
    packet = shape((25, 8, width), BF16)
    arguments = (start_field, applied_load, bone_mask, element_stiffness)
    q0, q1, start_field, applied_load, bone_mask, stiff = call(
        pack_z_kernel,
        [packet, packet] + [shape(a.shape, a.dtype) for a in arguments],
        4,
        [pltpu.SemaphoreType.DMA((8,))],
        name="pack_z",
        space=pltpu.HBM,
    )(*[pltpu.with_memory_space_constraint(a, pltpu.HBM) for a in arguments])
    r1 = swap(q1, "gz", 1)
    r0 = swap(q0, "gz", 0)
    packet = shape((len(OWN_TILES), 8, width), BF16)
    q0, q1, token = call(
        pack_own_kernel, [packet, packet, shape((8, 128), F32)], 3, name="pack_own"
    )(start_field, applied_load, bone_mask)
    yn1 = swap(q1, "gy", 1)
    yn0 = swap(q0, "gy", 0)
    w, wd, bound, wr, rzy, hzy, py, rx, px, pair = call(
        matrices_kernel,
        [
            shape((4 * BAND, 8 * BAND), BF16),
            shape((4 * BAND, 2 * ROWS), BF16),
            shape((8, 128), F32),
            shape((2 * BAND, 8 * BAND), BF16),
            shape((120, 192), BF16),
            shape((32, 64), BF16),
            shape((120, 240), BF16),
            shape((width, half), BF16),
            shape((half, width), BF16),
            shape((width, half), BF16),
        ],
        2,
        name="matrices",
        place=False,
    )(stiff, token)

    packet = shape((len(FAR_TILES), 8, width), BF16)
    q0, q1 = call(pack_far_kernel, [packet, packet], 3, name="pack_far")(bound, r0, r1)
    yf1 = swap(q1, "gy", 1)
    yf0 = swap(q0, "gy", 0)
    def field(count, rows, dtype):
        return (count, rows, width), dtype

    kinds = [(2 * BAND, BF16)] * 4 + [(2 * ROWS, BF16)] + [(BAND, F32)] * 4 + [(ROWS, F32)]
    *middle, scale = call(
        fine_own_kernel,
        [shape(*field(8, *kind)) for kind in kinds]
        + [shape(*field(6, 2 * BAND, F32)), shape((4, 8, half), F32)],
        10,
        name="fine_own",
    )(w, wd, bound, hzy, pair, start_field, applied_load, bone_mask, yn0, yn1)
    packet = shape((12, 8, half), BF16)
    smoothed, rhs, q0, q1 = call(
        fine_rest_kernel,
        [shape(start_field.shape, F32), shape((15, 8, half), F32), packet, packet],
        23,
        [pltpu.VMEM(*field(16, *kind)) for kind in kinds],
        name="fine_rest",
    )(w, wd, bound, wr, rzy, rx, *middle, scale, applied_load, r0, r1, yf0, yf1)
    r1 = swap(q1, "gz", 1)
    r0 = swap(q0, "gz", 0)
    packet = shape((20, 8, half), BF16)
    full, q0, q1 = call(
        pack_coarse_kernel,
        [shape((40, 8, half), F32), packet, packet],
        4,
        name="pack_coarse",
    )(rhs, scale, r0, r1)
    y1 = swap(q1, "gy", 1)
    y0 = swap(q0, "gy", 0)
    coarse_plane = pltpu.VMEM((11, BAND, half), F32)
    return call(
        coarse_kernel,
        shape(start_field.shape, F32),
        9,
        [
            pltpu.VMEM((11, 2 * BAND, half), BF16),
            pltpu.VMEM((11, 2 * ROWS, half), BF16),
            coarse_plane,
            coarse_plane,
            coarse_plane,
            coarse_plane,
            pltpu.VMEM((11, ROWS, half), F32),
            pltpu.VMEM((8, 3, 8, width), F32),
            pltpu.SemaphoreType.DMA((8,)),
        ],
        name="coarse",
        out_space=pltpu.HBM,
    )(w, wd, bound, py, px, full, y0, y1, smoothed)


def solution(mesh):
    in_specs = (P(None, "gz", "gy", None), P(None, "gz", "gy", None), P("gz", "gy", None), P())
    out_specs = P(None, "gz", "gy", None)
    return jax.shard_map(body, mesh=mesh, in_specs=in_specs, out_specs=out_specs, check_vma=False)
```

```python
import jax
import jax.numpy as jnp
from jax import lax
from jax.sharding import PartitionSpec as P
from jax.experimental import pallas as pl
from jax.experimental.pallas import tpu as pltpu

F32 = jnp.float32
BF16 = jnp.bfloat16
CHEB = 3
LOW = 0.1
MID = 0.5 * (1.0 + LOW)
HALF = 0.5 * (1.0 - LOW)
RATIO = (1.0 + LOW) / (1.0 - LOW)
ROWS = 16
BAND = 3 * ROWS
DEEP = 4


def iota(shape, dim):
    return lax.broadcasted_iota(jnp.int32, shape, dim)


def build_matrices(stiff):
    m = 4 * BAND
    row_m = iota((m, 24), 0)
    base_row = 12 * (row_m // (2 * BAND)) + 3 * ((row_m // BAND) % 2) + (row_m // ROWS) % 3
    col_e = iota((m, 24), 1)
    row_k = iota((24, m), 0)
    col_k = iota((24, m), 1)
    base_col = 6 * (col_k // (2 * BAND)) + 3 * ((col_k // BAND) % 2) + (col_k // ROWS) % 3
    mm = iota((m, m), 0)
    kk = iota((m, m), 1)
    gap = (mm % ROWS) - (kk % ROWS) + kk // (2 * BAND)
    blocks = []
    left = []
    for cy in range(2):
        pick = (col_e == base_row + 6 * cy).astype(BF16)
        left.append(jnp.dot(pick, stiff, preferred_element_type=F32).astype(BF16))
    for p in range(2):
        pick = (row_k == base_col + 12 * p).astype(BF16)
        block = jnp.zeros((m, m), F32)
        for cy in range(2):
            full = jnp.dot(left[cy], pick, preferred_element_type=F32)
            block = jnp.where(gap == cy, full, block)
        blocks.append(block.astype(BF16))
    md = iota((m, 2 * ROWS), 0)
    kd = iota((m, 2 * ROWS), 1)
    diag = jnp.zeros((m, 2 * ROWS), F32)
    for cy in range(2):
        own = jnp.sum(
            jnp.where(col_e == base_row + 6 * cy, left[cy].astype(F32), 0.0), axis=1, keepdims=True
        )
        diag = jnp.where((kd // ROWS == cy) & (kd % ROWS == md % ROWS), own, diag)
    return jnp.concatenate(blocks, axis=1), diag.astype(BF16)


def spectral_bound(stiff):
    wide = stiff.astype(F32)
    eye = iota((24, 24), 0) == iota((24, 24), 1)
    own = jnp.sum(jnp.where(eye, wide, 0.0), axis=1, keepdims=True)
    total = jnp.sum(jnp.abs(wide), axis=1, keepdims=True)
    return jnp.max(total / own, axis=0, keepdims=True)


def shift_up(values, width):
    rolled = pltpu.roll(values, width - 1, 1)
    return jnp.where(iota(values.shape, 1) == width - 1, 0.0, rolled)


def shift_down(values):
    rolled = pltpu.roll(values, 1, 1)
    return jnp.where(iota(values.shape, 1) == 0, 0.0, rolled)


def shifted_nodes(values, width):
    return jnp.concatenate([values.astype(BF16), shift_up(values, width).astype(BF16)], axis=0)


def scale_rows(scale):
    down = pltpu.roll(scale, 1, 0)
    down = jnp.where(iota(scale.shape, 0) == 0, 0.0, down)
    return jnp.concatenate([scale.astype(BF16), down.astype(BF16)], axis=0)


def half_of(matrix_ref, half):
    if half is None:
        return matrix_ref[...]
    rows = matrix_ref.shape[0] // 2
    return matrix_ref[half * rows : (half + 1) * rows]


def layer_operator(w_ref, nodes, scales):
    def product(layer, half=None):
        scale = scales(layer)
        width = scale.shape[-1]
        parts = []
        for p in range(2):
            plane = nodes(layer + p).reshape(6, ROWS, width)
            for cy in range(2):
                masked = plane * scale[cy * ROWS : (cy + 1) * ROWS][None]
                parts.append(masked.reshape(2 * BAND, width))
        matrix = half_of(w_ref, half)
        return jnp.dot(matrix, jnp.concatenate(parts, axis=0), preferred_element_type=F32)

    return product


def diagonal_operator(wd_ref, scales):
    def product(layer, half=None):
        return jnp.dot(half_of(wd_ref, half), scales(layer), preferred_element_type=F32)

    return product


def plane_steps(lo, hi, product, use, band=BAND, below=None, above=None):
    carry = product(lo - 1, 1) if below is None else below
    for z in range(lo, hi + 1):
        if z < hi:
            both = product(z)
            part, rest = both[0 : 2 * band], both[2 * band : 4 * band]
        else:
            part, rest = product(z, 0) if above is None else above, None
        plane = part + carry
        carry = rest
        use(z, plane[0:band] + shift_down(plane[band : 2 * band]))
        yield


def planes_of(*args, **options):
    for _ in plane_steps(*args, **options):
        pass


def inverter(inv_ref, idle_ref, bound, width, past_z, past_y, first, base=0):
    rows = iota((BAND, width), 0) % ROWS
    keep_y = jnp.where((rows >= first) & (past_y == 1), 0.0, 1.0)

    def use(z, diag):
        idle = (diag == 0.0).astype(F32)
        inverse = keep_y / ((diag + idle) * bound)
        if z >= first:
            inverse = inverse * jnp.where(past_z == 1, 0.0, 1.0)
        inv_ref[z - base] = inverse
        idle_ref[z - base] = idle[0:ROWS]

    return use


def tile3(values):
    return jnp.concatenate([values, values, values], axis=0)


def advance(plane, b, x, update, inverse, idle, factors):
    previous, current = factors
    new = current * (inverse * (b - plane - tile3(idle) * x))
    if previous is not None:
        new = previous * update + new
    return x + new, new


def chebyshev_factors():
    factors = [(None, 1.0 / MID)]
    rho = 1.0 / RATIO
    for _ in range(CHEB - 1):
        nxt = 1.0 / (2.0 * RATIO - rho)
        factors.append((nxt * rho, 2.0 * nxt / HALF))
        rho = nxt
    return factors


def weights(gap, where):
    value = jnp.where(gap == 0, 1.0, jnp.where(gap == 1, 0.5, 0.0))
    return jnp.where(where, value, 0.0)


def own_rows(w_ref):
    groups = [w_ref[ROWS * g : ROWS * (g + 1)].astype(F32)[4:12] for g in range(12)]
    return jnp.concatenate(groups, axis=0).astype(BF16)


def restrict_planes():
    out, src = iota((120, 192), 0), iota((120, 192), 1)
    gap_z = jnp.abs(src // 24 - 2 * (out // 24))
    gap_y = jnp.abs(src % 8 - 2 * (out % 8 - 3))
    same = (src // 8) % 3 == (out // 8) % 3
    return (weights(gap_z, same) * weights(gap_y, same)).astype(BF16)


def halve_planes():
    out, src = iota((32, 64), 0), iota((32, 64), 1)
    same = (src // 16 == out // 8) & ((src % 8) // 2 == out % 8 - 3)
    return same.astype(F32).astype(BF16)


def prolong_rows():
    out, src = iota((120, 240), 0), iota((120, 240), 1)
    gap = jnp.abs(out % 8 - 2 * (src % ROWS - 3))
    same = (out // 24 == src // BAND) & ((out // 8) % 3 == (src // ROWS) % 3)
    return weights(gap, same).astype(BF16)


def matrices_kernel(
    e_ref, token_ref, w_ref, wd_ref, bound_ref, wr_ref, rzy_ref, hzy_ref, py_ref, rx_ref, px_ref, pair_ref
):
    stiff = e_ref[...]
    w_ref[...], wd_ref[...] = build_matrices(stiff)
    bound_ref[...] = jnp.broadcast_to(spectral_bound(stiff), (8, 128))
    wr_ref[...] = own_rows(w_ref)
    rzy_ref[...] = restrict_planes()
    hzy_ref[...] = halve_planes()
    py_ref[...] = prolong_rows()
    fine, coarse = iota(rx_ref.shape, 0), iota(rx_ref.shape, 1)
    rx_ref[...] = weights(jnp.abs(fine - 2 * coarse), fine >= 0).astype(BF16)
    pair_ref[...] = (fine // 2 == coarse).astype(F32).astype(BF16)
    coarse, fine = iota(px_ref.shape, 0), iota(px_ref.shape, 1)
    px_ref[...] = weights(jnp.abs(fine - 2 * coarse), fine >= 0).astype(BF16)


def pack_z_kernel(
    place, x_hbm, b_hbm, m_hbm, e_hbm, q0_ref, q1_ref, x_ref, b_ref, m_ref, e_ref, sem
):
    even = 1 - place[0]
    pairs = [(m_hbm, m_ref), (e_hbm, e_ref)]
    for d in range(3):
        pairs += [(x_hbm.at[d], x_ref.at[d]), (b_hbm.at[d], b_ref.at[d])]
    copies = [pltpu.make_async_copy(src, dst, sem.at[i]) for i, (src, dst) in enumerate(pairs)]
    for copy in copies:
        copy.start()
    for copy in copies:
        copy.wait()
    for out, up in ((q0_ref, even), (q1_ref, 1 - even)):
        for d in range(3):
            out[4 * d : 4 * d + 4] = x_ref[d, pl.ds(4 * up, 4)].astype(BF16)
            out[12 + 3 * d : 15 + 3 * d] = b_ref[d, pl.ds(5 * up, 3)].astype(BF16)
        out[21:25] = m_ref[pl.ds(4 * up, 4)].astype(F32).astype(BF16)


def own_planes(x_ref, b_ref, m_ref):
    def at(kind, d, w):
        if kind == "m":
            return m_ref[w - 4].astype(F32)
        return (x_ref if kind == "x" else b_ref)[d, w - 4]

    return at


def borrowed_planes(place, r0_ref, r1_ref):
    odd = place[0] == 1

    def at(kind, d, w):
        low = w < 4
        if kind == "x":
            i = 4 * d + w % 4
        elif kind == "b":
            i = 12 + 3 * d + (w - 1 if low else w - 12)
        else:
            i = 21 + w % 4
        first, second = (r0_ref, r1_ref) if low else (r1_ref, r0_ref)
        return jnp.where(odd, first[i].astype(F32), second[i].astype(F32))

    return at


def flip(values):
    return pltpu.roll(values, 4, 0)


def tiles_of(pairs, load_pairs):
    return (
        [("x", d, pair) for d in range(3) for pair in pairs]
        + [("b", d, pair) for d in range(3) for pair in load_pairs]
        + [("m", 0, pair) for pair in pairs]
    )


OWN_PAIRS = ((4, 5), (6, 7), (8, 9), (10, 11))
OWN_TILES = tiles_of(OWN_PAIRS, OWN_PAIRS)
FAR_TILES = tiles_of(((0, 1), (2, 3), (12, 13), (14, 15)), ((1, 2), (3, 12), (13, 14)))


def pack_rows(place, at, tiles, q0_ref, q1_ref):
    even = place[1] == 0
    for index, (kind, d, (first, second)) in enumerate(tiles):
        a, b = at(kind, d, first), at(kind, d, second)
        head = iota(a.shape, 0) < 4
        up = jnp.where(head, flip(a), b)
        down = jnp.where(head, a, flip(b))
        q0_ref[index] = jnp.where(even, up, down).astype(BF16)
        q1_ref[index] = jnp.where(even, down, up).astype(BF16)


def pack_own_kernel(place, x_ref, b_ref, m_ref, q0_ref, q1_ref, token_ref):
    pack_rows(place, own_planes(x_ref, b_ref, m_ref), OWN_TILES, q0_ref, q1_ref)
    token_ref[...] = jnp.zeros(token_ref.shape, F32)


def pack_far_kernel(place, after_ref, r1_ref, r0_ref, q0_ref, q1_ref):
    pack_rows(place, borrowed_planes(place, r0_ref, r1_ref), FAR_TILES, q0_ref, q1_ref)


def unpack_rows(place, at, tiles, y0_ref, y1_ref, width, use):
    odd = place[1] == 1
    head = iota((8, width), 0) < 4
    for index, (kind, d, pair) in enumerate(tiles):
        low = jnp.where(odd, y0_ref[index].astype(F32), y1_ref[index].astype(F32))
        high = jnp.where(odd, y1_ref[index].astype(F32), y0_ref[index].astype(F32))
        for k, w in enumerate(pair):
            own = flip(at(kind, d, w))
            below = low if k == 0 else flip(low)
            above = flip(high) if k == 0 else high
            block = jnp.concatenate(
                [jnp.where(head, below, own), jnp.where(head, own, above)], axis=0
            )
            use(kind, d, w, block)


def fine_own_kernel(
    place, w_ref, wd_ref, bound_ref, hzy_ref, pair_ref, x_in, b_in, m_in, y0_ref, y1_ref,
    v0_ref, v1_ref, v2_ref, v3_ref, s_ref, b_ref, x_ref, u_ref, inv_ref, idle_ref, seam_ref, sc_ref,
):
    width = x_in.shape[-1]

    def keep(kind, d, w, block):
        if kind == "m":
            s_ref[w - 4] = scale_rows(block)
        else:
            (x_ref if kind == "x" else b_ref)[w - 4, ROWS * d : ROWS * (d + 1)] = block

    unpack_rows(
        place, own_planes(x_in, b_in, m_in), OWN_TILES, y0_ref, y1_ref, width, keep
    )
    for z in range(8):
        v0_ref[z] = shifted_nodes(x_ref[z], width)

    def scales(layer):
        return s_ref[layer - 4]

    planes_of(
        5, 11, diagonal_operator(wd_ref, scales),
        inverter(inv_ref, idle_ref, bound_ref[0:1, 0:1], width, place[2], place[3], 12, 4),
    )
    levels = (v0_ref, v1_ref, v2_ref, v3_ref)
    for level, factors in enumerate(chebyshev_factors()):
        source, target = levels[level], levels[level + 1]

        def use(w, plane):
            z = w - 4
            update = None if level == 0 else u_ref[z]
            x_ref[z], u_ref[z] = advance(
                plane, b_ref[z], x_ref[z], update, inv_ref[z], idle_ref[z], factors
            )
            target[z] = shifted_nodes(x_ref[z], width)

        lo, hi = 5 + level, 10 - level
        product = layer_operator(w_ref, lambda w: source[w - 4], scales)
        first, last = product(lo - 1), product(hi)
        seam_ref[2 * level] = first[0 : 2 * BAND]
        seam_ref[2 * level + 1] = last[2 * BAND : 4 * BAND]
        planes_of(
            lo, hi, product, use, below=first[2 * BAND : 4 * BAND], above=last[0 : 2 * BAND]
        )
    counts = jnp.dot(
        hzy_ref[...], m_in[...].astype(F32).astype(BF16).reshape(64, width), preferred_element_type=F32
    )
    counts = jnp.dot(counts.astype(BF16), pair_ref[...], preferred_element_type=F32)
    sc_ref[...] = (0.25 * counts).reshape(sc_ref.shape)


def own_part(values, d, head):
    a = values[ROWS * d : ROWS * d + 8]
    b = values[ROWS * d + 8 : ROWS * d + 16]
    return flip(jnp.where(head, b, a))


def fine_rest_kernel(
    place, w_ref, wd_ref, bound_ref, wr_ref, rzy_ref, rx_ref,
    v0_in, v1_in, v2_in, v3_in, s_in, b_mid, x_in, u_in, inv_in, idle_in, seam_ref, sc_ref,
    b_in, r1_ref, r0_ref, y1_ref, y0_ref,
    out_ref, rhs_ref, q0_ref, q1_ref,
    v0_ref, v1_ref, v2_ref, v3_ref, s_ref, b_ref, x_ref, u_ref, inv_ref, idle_ref,
):
    width = b_in.shape[-1]

    def either(mid, far, lo, hi):
        return lambda w: mid[w - 4] if lo <= w <= hi else far[w]

    def keep(kind, d, w, block):
        if kind == "m":
            s_ref[w] = scale_rows(block)
        else:
            (x_ref if kind == "x" else b_ref)[w, ROWS * d : ROWS * (d + 1)] = block

    unpack_rows(
        place, borrowed_planes(place, r0_ref, r1_ref), FAR_TILES, y0_ref, y1_ref, width, keep
    )
    for w in (0, 1, 2, 3, 12, 13, 14, 15):
        v0_ref[w] = shifted_nodes(x_ref[w], width)
    scales = either(s_in, s_ref, 4, 11)
    invert = inverter(inv_ref, idle_ref, bound_ref[0:1, 0:1], width, place[2], place[3], 12)
    planes_of(1, 4, diagonal_operator(wd_ref, scales), invert)
    planes_of(12, 14, diagonal_operator(wd_ref, scales), invert)
    inverse, idles = either(inv_in, inv_ref, 5, 11), either(idle_in, idle_ref, 5, 11)
    loads = either(b_mid, b_ref, 4, 11)
    state = {w: (x_ref, u_ref, w) for w in range(16)}
    state.update({w: (x_in, u_in, w - 4) for w in range(4, 12)})
    near = (v0_in, v1_in, v2_in, v3_in)
    far = (v0_ref, v1_ref, v2_ref, v3_ref)
    all_factors = chebyshev_factors()

    def run(level, lo, hi, **seam):
        target = far[level + 1]

        def use(w, plane):
            xs, us, z = state[w]
            update = None if level == 0 else us[z]
            x_ref[w], u_ref[w] = advance(
                plane, loads(w), xs[z], update, inverse(w), idles(w), all_factors[level]
            )
            state[w] = (x_ref, u_ref, w)
            target[w] = shifted_nodes(x_ref[w], width)

        nodes = either(near[level], far[level], 4 + level, 11 - level)
        return plane_steps(lo, hi, layer_operator(w_ref, nodes, scales), use, **seam)

    low = [run(k, 1 + k, 4 + k, above=seam_ref[2 * k]) for k in range(CHEB)]
    high = [run(k, 11 - k, 14 - k, below=seam_ref[2 * k + 1]) for k in range(CHEB)]
    for k in range(CHEB):
        for _ in low[k]:
            pass
        for _ in high[k]:
            pass

    head = iota((8, width), 0) < 4
    parts = []

    def use(w, plane):
        idle = own_part(idles(w), 0, head)
        xs, _, z = state[w]
        final = xs[z]
        for d in range(3):
            x = own_part(final, d, head)
            out_ref[d, w - 4] = x
            parts.append(b_in[d, w - 4] - plane[8 * d : 8 * d + 8] - idle * x)

    planes_of(4, 11, layer_operator(wr_ref, either(near[3], far[3], 7, 8), scales), use, 24)
    residual = jnp.concatenate(parts, axis=0).astype(BF16)
    sums = jnp.dot(rzy_ref[...], residual, preferred_element_type=F32)
    sums = jnp.dot(sums.astype(BF16), rx_ref[...], preferred_element_type=F32)
    rhs_ref[...] = sums.reshape(rhs_ref.shape)
    even = 1 - place[0]
    for out, up in ((q0_ref, even), (q1_ref, 1 - even)):
        out[0:9] = rhs_ref[pl.ds(6 * up, 9)].astype(BF16)
        out[9:12] = sc_ref[pl.ds(up, 3)].astype(BF16)


def pack_coarse_kernel(place, rhs_ref, sc_ref, r1_ref, r0_ref, full_ref, q0_ref, q1_ref):
    odd = place[0] == 1
    even_y = place[1] == 0
    head = iota(rhs_ref.shape[1:], 0) < 4
    kept = []

    def low(i):
        return jnp.where(odd, r0_ref[i].astype(F32), r1_ref[i].astype(F32))

    def high(i):
        return jnp.where(odd, r1_ref[i].astype(F32), r0_ref[i].astype(F32))

    for z in range(10):
        c = z - 3
        for d in range(4):
            value = jnp.zeros(rhs_ref.shape[1:], F32)
            if d < 3:
                if -2 <= c <= 0:
                    value = value + low(3 * (c + 2) + d)
                if 4 <= c <= 6:
                    value = value + high(3 * (c - 4) + d)
                if 0 <= c <= 4:
                    value = value + rhs_ref[3 * c + d]
            else:
                if c <= -1:
                    value = low(9 + c + 3)
                elif c >= 4:
                    value = high(9 + c - 4)
                else:
                    value = sc_ref[c]
            full_ref[4 * z + d] = value
            kept.append(value)
    for i in range(20):
        a, b = kept[2 * i], kept[2 * i + 1]
        up = jnp.where(head, flip(a), b)
        down = jnp.where(head, pltpu.roll(a, 5, 0), pltpu.roll(b, 1, 0))
        q0_ref[i] = jnp.where(even_y, up, down).astype(BF16)
        q1_ref[i] = jnp.where(even_y, down, up).astype(BF16)


def coarse_kernel(
    place, w_ref, wd_ref, bound_ref, py_ref, px_ref, full_ref, y1_ref, y0_ref, smooth_ref, out_hbm,
    v_ref, v1_ref, v2_ref, s_ref, b_ref, x_ref, u_ref, inv_ref, idle_ref, out_ref, sem,
):
    half = full_ref.shape[-1]
    width = 2 * half
    bound = bound_ref[0:1, 0:1]
    odd = place[1] == 1
    rows8 = iota((8, half), 0)
    for z in range(10):
        for d in range(4):
            i = 4 * z + d
            low = jnp.where(odd, y0_ref[i // 2].astype(F32), y1_ref[i // 2].astype(F32))
            high = jnp.where(odd, y1_ref[i // 2].astype(F32), y0_ref[i // 2].astype(F32))
            if i % 2:
                low = flip(low)
            high = pltpu.roll(high, 3 if i % 2 else 7, 0)
            first = (
                full_ref[i] + jnp.where(rows8 < 4, low, 0.0) + jnp.where(rows8 == 7, high, 0.0)
            )
            block = jnp.concatenate([first, jnp.where(rows8 < 3, high, 0.0)], axis=0)
            if d < 3:
                b_ref[z, ROWS * d : ROWS * (d + 1)] = block
            else:
                s_ref[z] = scale_rows(block)
    def scales(layer):
        return s_ref[layer]

    factors = chebyshev_factors()
    levels = (v_ref, v1_ref, v2_ref)
    invert = inverter(inv_ref, idle_ref, bound, half, place[2], place[3], 7)

    def start(z, diag):
        invert(z, diag)
        update = factors[0][1] * (inv_ref[z] * b_ref[z])
        u_ref[z] = update
        x_ref[z] = update
        v_ref[z] = shifted_nodes(update, half)

    def run(level, lo, hi):
        def use(z, plane):
            x_ref[z], u_ref[z] = advance(
                plane, b_ref[z], x_ref[z], u_ref[z], inv_ref[z], idle_ref[z], factors[level]
            )
            levels[level][z] = shifted_nodes(x_ref[z], half)

        nodes = levels[level - 1]
        return plane_steps(lo, hi, layer_operator(w_ref, lambda z: nodes[z], scales), use)

    steps = (
        plane_steps(1, 9, diagonal_operator(wd_ref, scales), start), run(1, 2, 8), run(2, 3, 7)
    )
    for k in (0,) * 9 + (1,) * 7 + (2,) * 5:
        next(steps[k])

    coarse = jnp.concatenate([v2_ref[3 + k, 0:BAND] for k in range(5)], axis=0)
    rows = jnp.dot(py_ref[...], coarse, preferred_element_type=F32)
    wide = jnp.dot(rows.astype(BF16), px_ref[...], preferred_element_type=F32)
    wide = wide.reshape(5, 3, 8, width)
    copies = []
    for z in range(8):
        k = z // 2
        plane = wide[k] if z % 2 == 0 else 0.5 * (wide[k] + wide[k + 1])
        out_ref[z] = smooth_ref[:, z] + plane
        copies.append(pltpu.make_async_copy(out_ref.at[z], out_hbm.at[:, z], sem.at[z]))
        copies[-1].start()
    for copy in copies:
        copy.wait()


def swap(array, axis, offset):
    length = lax.axis_size(axis)
    pairs = []
    for i in range(offset, length - 1, 2):
        pairs += [(i, i + 1), (i + 1, i)]
    return lax.ppermute(array, axis, pairs)


def whereabouts():
    gz, gy = lax.axis_index("gz"), lax.axis_index("gy")
    return (
        lax.rem(gz, 2),
        lax.rem(gy, 2),
        (gz == lax.axis_size("gz") - 1).astype(jnp.int32),
        (gy == lax.axis_size("gy") - 1).astype(jnp.int32),
    )


def call(
    body, out_shape, n_in, scratch=(), name=None, place=True, space=pltpu.VMEM, out_space=pltpu.VMEM
):
    vmem = pl.BlockSpec(memory_space=out_space)
    single = not isinstance(out_shape, (tuple, list))
    return pl.pallas_call(
        (lambda *refs: body(whereabouts(), *refs)) if place else body,
        out_shape=out_shape,
        in_specs=[pl.BlockSpec(memory_space=space)] * n_in,
        out_specs=vmem if single else [vmem] * len(out_shape),
        scratch_shapes=list(scratch),
        compiler_params=pltpu.CompilerParams(vmem_limit_bytes=24 << 20),
        name=name,
    )


def body(applied_load, start_field, bone_mask, element_stiffness):
    width = applied_load.shape[-1]
    half = width // 2
    shape = jax.ShapeDtypeStruct
    packet = shape((25, 8, width), BF16)
    arguments = (start_field, applied_load, bone_mask, element_stiffness)
    q0, q1, start_field, applied_load, bone_mask, stiff = call(
        pack_z_kernel,
        [packet, packet] + [shape(a.shape, a.dtype) for a in arguments],
        4,
        [pltpu.SemaphoreType.DMA((8,))],
        name="pack_z",
        space=pltpu.HBM,
    )(*[pltpu.with_memory_space_constraint(a, pltpu.HBM) for a in arguments])
    r1 = swap(q1, "gz", 1)
    r0 = swap(q0, "gz", 0)
    packet = shape((len(OWN_TILES), 8, width), BF16)
    q0, q1, token = call(
        pack_own_kernel, [packet, packet, shape((8, 128), F32)], 3, name="pack_own"
    )(start_field, applied_load, bone_mask)
    yn1 = swap(q1, "gy", 1)
    yn0 = swap(q0, "gy", 0)
    w, wd, bound, wr, rzy, hzy, py, rx, px, pair = call(
        matrices_kernel,
        [
            shape((4 * BAND, 8 * BAND), BF16),
            shape((4 * BAND, 2 * ROWS), BF16),
            shape((8, 128), F32),
            shape((2 * BAND, 8 * BAND), BF16),
            shape((120, 192), BF16),
            shape((32, 64), BF16),
            shape((120, 240), BF16),
            shape((width, half), BF16),
            shape((half, width), BF16),
            shape((width, half), BF16),
        ],
        2,
        name="matrices",
        place=False,
    )(stiff, token)

    packet = shape((len(FAR_TILES), 8, width), BF16)
    q0, q1 = call(pack_far_kernel, [packet, packet], 3, name="pack_far")(bound, r1, r0)
    yf1 = swap(q1, "gy", 1)
    yf0 = swap(q0, "gy", 0)
    def field(count, rows, dtype):
        return (count, rows, width), dtype

    kinds = [(2 * BAND, BF16)] * 4 + [(2 * ROWS, BF16)] + [(BAND, F32)] * 4 + [(ROWS, F32)]
    *middle, scale = call(
        fine_own_kernel,
        [shape(*field(8, *kind)) for kind in kinds]
        + [shape(*field(6, 2 * BAND, F32)), shape((4, 8, half), F32)],
        10,
        name="fine_own",
    )(w, wd, bound, hzy, pair, start_field, applied_load, bone_mask, yn0, yn1)
    packet = shape((12, 8, half), BF16)
    smoothed, rhs, q0, q1 = call(
        fine_rest_kernel,
        [shape(start_field.shape, F32), shape((15, 8, half), F32), packet, packet],
        23,
        [pltpu.VMEM(*field(16, *kind)) for kind in kinds],
        name="fine_rest",
    )(w, wd, bound, wr, rzy, rx, *middle, scale, applied_load, r1, r0, yf1, yf0)
    r1 = swap(q1, "gz", 1)
    r0 = swap(q0, "gz", 0)
    packet = shape((20, 8, half), BF16)
    full, q0, q1 = call(
        pack_coarse_kernel,
        [shape((40, 8, half), F32), packet, packet],
        4,
        name="pack_coarse",
    )(rhs, scale, r1, r0)
    y1 = swap(q1, "gy", 1)
    y0 = swap(q0, "gy", 0)
    coarse_plane = pltpu.VMEM((11, BAND, half), F32)
    return call(
        coarse_kernel,
        shape(start_field.shape, F32),
        9,
        [
            pltpu.VMEM((11, 2 * BAND, half), BF16),
            pltpu.VMEM((11, 2 * BAND, half), BF16),
            pltpu.VMEM((11, 2 * BAND, half), BF16),
            pltpu.VMEM((11, 2 * ROWS, half), BF16),
            coarse_plane,
            coarse_plane,
            coarse_plane,
            coarse_plane,
            pltpu.VMEM((11, ROWS, half), F32),
            pltpu.VMEM((8, 3, 8, width), F32),
            pltpu.SemaphoreType.DMA((8,)),
        ],
        name="coarse",
        out_space=pltpu.HBM,
    )(w, wd, bound, py, px, full, y1, y0, smoothed)


def solution(mesh):
    in_specs = (P(None, "gz", "gy", None), P(None, "gz", "gy", None), P("gz", "gy", None), P())
    out_specs = P(None, "gz", "gy", None)
    return jax.shard_map(body, mesh=mesh, in_specs=in_specs, out_specs=out_specs, check_vma=False)
```

```python
import jax
import jax.numpy as jnp
from jax import lax
from jax.sharding import PartitionSpec as P
from jax.experimental import pallas as pl
from jax.experimental.pallas import tpu as pltpu

F32 = jnp.float32
BF16 = jnp.bfloat16
CHEB = 3
LOW = 0.1
MID = 0.5 * (1.0 + LOW)
HALF = 0.5 * (1.0 - LOW)
RATIO = (1.0 + LOW) / (1.0 - LOW)
ROWS = 16
BAND = 3 * ROWS
DEEP = 4


def iota(shape, dim):
    return lax.broadcasted_iota(jnp.int32, shape, dim)


def build_matrices(stiff):
    m = 4 * BAND
    row_m = iota((m, 24), 0)
    base_row = 12 * (row_m // (2 * BAND)) + 3 * ((row_m // BAND) % 2) + (row_m // ROWS) % 3
    col_e = iota((m, 24), 1)
    row_k = iota((24, m), 0)
    col_k = iota((24, m), 1)
    base_col = 6 * (col_k // (2 * BAND)) + 3 * ((col_k // BAND) % 2) + (col_k // ROWS) % 3
    mm = iota((m, m), 0)
    kk = iota((m, m), 1)
    gap = (mm % ROWS) - (kk % ROWS) + kk // (2 * BAND)
    blocks = []
    left = []
    for cy in range(2):
        pick = (col_e == base_row + 6 * cy).astype(BF16)
        left.append(jnp.dot(pick, stiff, preferred_element_type=F32).astype(BF16))
    for p in range(2):
        pick = (row_k == base_col + 12 * p).astype(BF16)
        block = jnp.zeros((m, m), F32)
        for cy in range(2):
            full = jnp.dot(left[cy], pick, preferred_element_type=F32)
            block = jnp.where(gap == cy, full, block)
        blocks.append(block.astype(BF16))
    md = iota((m, 2 * ROWS), 0)
    kd = iota((m, 2 * ROWS), 1)
    diag = jnp.zeros((m, 2 * ROWS), F32)
    for cy in range(2):
        own = jnp.sum(
            jnp.where(col_e == base_row + 6 * cy, left[cy].astype(F32), 0.0), axis=1, keepdims=True
        )
        diag = jnp.where((kd // ROWS == cy) & (kd % ROWS == md % ROWS), own, diag)
    return jnp.concatenate(blocks, axis=1), diag.astype(BF16)


def spectral_bound(stiff):
    wide = stiff.astype(F32)
    eye = iota((24, 24), 0) == iota((24, 24), 1)
    own = jnp.sum(jnp.where(eye, wide, 0.0), axis=1, keepdims=True)
    total = jnp.sum(jnp.abs(wide), axis=1, keepdims=True)
    return jnp.max(total / own, axis=0, keepdims=True)


def shift_up(values, width):
    rolled = pltpu.roll(values, width - 1, 1)
    return jnp.where(iota(values.shape, 1) == width - 1, 0.0, rolled)


def shift_down(values):
    rolled = pltpu.roll(values, 1, 1)
    return jnp.where(iota(values.shape, 1) == 0, 0.0, rolled)


def shifted_nodes(values, width):
    return jnp.concatenate([values.astype(BF16), shift_up(values, width).astype(BF16)], axis=0)


def scale_rows(scale):
    down = pltpu.roll(scale, 1, 0)
    down = jnp.where(iota(scale.shape, 0) == 0, 0.0, down)
    return jnp.concatenate([scale.astype(BF16), down.astype(BF16)], axis=0)


def half_of(matrix_ref, half):
    if half is None:
        return matrix_ref[...]
    rows = matrix_ref.shape[0] // 2
    return matrix_ref[half * rows : (half + 1) * rows]


def layer_operator(w_ref, nodes, scales):
    def product(layer, half=None):
        scale = scales(layer)
        width = scale.shape[-1]
        parts = []
        for p in range(2):
            plane = nodes(layer + p).reshape(6, ROWS, width)
            for cy in range(2):
                masked = plane * scale[cy * ROWS : (cy + 1) * ROWS][None]
                parts.append(masked.reshape(2 * BAND, width))
        matrix = half_of(w_ref, half)
        return jnp.dot(matrix, jnp.concatenate(parts, axis=0), preferred_element_type=F32)

    return product


def diagonal_operator(wd_ref, scales):
    def product(layer, half=None):
        return jnp.dot(half_of(wd_ref, half), scales(layer), preferred_element_type=F32)

    return product


def plane_steps(lo, hi, product, use, band=BAND, below=None, above=None):
    carry = product(lo - 1, 1) if below is None else below
    for z in range(lo, hi + 1):
        if z < hi:
            both = product(z)
            part, rest = both[0 : 2 * band], both[2 * band : 4 * band]
        else:
            part, rest = product(z, 0) if above is None else above, None
        plane = part + carry
        carry = rest
        use(z, plane[0:band] + shift_down(plane[band : 2 * band]))
        yield


def planes_of(*args, **options):
    for _ in plane_steps(*args, **options):
        pass


def inverter(inv_ref, idle_ref, bound, width, past_z, past_y, first, base=0):
    rows = iota((BAND, width), 0) % ROWS
    keep_y = jnp.where((rows >= first) & (past_y == 1), 0.0, 1.0)

    def use(z, diag):
        idle = (diag == 0.0).astype(F32)
        inverse = keep_y / ((diag + idle) * bound)
        if z >= first:
            inverse = inverse * jnp.where(past_z == 1, 0.0, 1.0)
        inv_ref[z - base] = inverse
        idle_ref[z - base] = idle[0:ROWS]

    return use


def tile3(values):
    return jnp.concatenate([values, values, values], axis=0)


def advance(plane, b, x, update, inverse, idle, factors):
    previous, current = factors
    new = current * (inverse * (b - plane - tile3(idle) * x))
    if previous is not None:
        new = previous * update + new
    return x + new, new


def chebyshev_factors():
    factors = [(None, 1.0 / MID)]
    rho = 1.0 / RATIO
    for _ in range(CHEB - 1):
        nxt = 1.0 / (2.0 * RATIO - rho)
        factors.append((nxt * rho, 2.0 * nxt / HALF))
        rho = nxt
    return factors


def weights(gap, where):
    value = jnp.where(gap == 0, 1.0, jnp.where(gap == 1, 0.5, 0.0))
    return jnp.where(where, value, 0.0)


def own_rows(w_ref):
    groups = [w_ref[ROWS * g : ROWS * (g + 1)].astype(F32)[4:12] for g in range(12)]
    return jnp.concatenate(groups, axis=0).astype(BF16)


def restrict_planes():
    out, src = iota((120, 192), 0), iota((120, 192), 1)
    gap_z = jnp.abs(src // 24 - 2 * (out // 24))
    gap_y = jnp.abs(src % 8 - 2 * (out % 8 - 3))
    same = (src // 8) % 3 == (out // 8) % 3
    return (weights(gap_z, same) * weights(gap_y, same)).astype(BF16)


def halve_planes():
    out, src = iota((32, 64), 0), iota((32, 64), 1)
    same = (src // 16 == out // 8) & ((src % 8) // 2 == out % 8 - 3)
    return same.astype(F32).astype(BF16)


def prolong_rows():
    out, src = iota((120, 240), 0), iota((120, 240), 1)
    gap = jnp.abs(out % 8 - 2 * (src % ROWS - 3))
    same = (out // 24 == src // BAND) & ((out // 8) % 3 == (src // ROWS) % 3)
    return weights(gap, same).astype(BF16)


def matrices_kernel(
    e_ref, token_ref, w_ref, wd_ref, bound_ref, wr_ref, rzy_ref, hzy_ref, py_ref, rx_ref, px_ref, pair_ref
):
    stiff = e_ref[...]
    w_ref[...], wd_ref[...] = build_matrices(stiff)
    bound_ref[...] = jnp.broadcast_to(spectral_bound(stiff), (8, 128))
    wr_ref[...] = own_rows(w_ref)
    rzy_ref[...] = restrict_planes()
    hzy_ref[...] = halve_planes()
    py_ref[...] = prolong_rows()
    fine, coarse = iota(rx_ref.shape, 0), iota(rx_ref.shape, 1)
    rx_ref[...] = weights(jnp.abs(fine - 2 * coarse), fine >= 0).astype(BF16)
    pair_ref[...] = (fine // 2 == coarse).astype(F32).astype(BF16)
    coarse, fine = iota(px_ref.shape, 0), iota(px_ref.shape, 1)
    px_ref[...] = weights(jnp.abs(fine - 2 * coarse), fine >= 0).astype(BF16)


def pack_z_kernel(
    place, x_hbm, b_hbm, m_hbm, e_hbm, q0_ref, q1_ref, x_ref, b_ref, m_ref, e_ref, sem
):
    even = 1 - place[0]
    pairs = []
    for d in range(3):
        pairs += [(x_hbm.at[d], x_ref.at[d])]
    for d in range(3):
        pairs += [(b_hbm.at[d], b_ref.at[d])]
    pairs += [(m_hbm, m_ref), (e_hbm, e_ref)]
    copies = [pltpu.make_async_copy(src, dst, sem.at[i]) for i, (src, dst) in enumerate(pairs)]
    for copy in copies:
        copy.start()
    outs = ((q0_ref, even), (q1_ref, 1 - even))
    for d in range(3):
        copies[d].wait()
        for out, up in outs:
            out[4 * d : 4 * d + 4] = x_ref[d, pl.ds(4 * up, 4)].astype(BF16)
    for d in range(3):
        copies[3 + d].wait()
        for out, up in outs:
            out[12 + 3 * d : 15 + 3 * d] = b_ref[d, pl.ds(5 * up, 3)].astype(BF16)
    copies[6].wait()
    for out, up in outs:
        out[21:25] = m_ref[pl.ds(4 * up, 4)].astype(F32).astype(BF16)
    copies[7].wait()


def own_planes(x_ref, b_ref, m_ref):
    def at(kind, d, w):
        if kind == "m":
            return m_ref[w - 4].astype(F32)
        return (x_ref if kind == "x" else b_ref)[d, w - 4]

    return at


def borrowed_planes(place, r0_ref, r1_ref):
    odd = place[0] == 1

    def at(kind, d, w):
        low = w < 4
        if kind == "x":
            i = 4 * d + w % 4
        elif kind == "b":
            i = 12 + 3 * d + (w - 1 if low else w - 12)
        else:
            i = 21 + w % 4
        first, second = (r0_ref, r1_ref) if low else (r1_ref, r0_ref)
        return jnp.where(odd, first[i].astype(F32), second[i].astype(F32))

    return at


def flip(values):
    return pltpu.roll(values, 4, 0)


def tiles_of(pairs, load_pairs):
    return (
        [("x", d, pair) for d in range(3) for pair in pairs]
        + [("b", d, pair) for d in range(3) for pair in load_pairs]
        + [("m", 0, pair) for pair in pairs]
    )


OWN_PAIRS = ((4, 5), (6, 7), (8, 9), (10, 11))
OWN_TILES = tiles_of(OWN_PAIRS, OWN_PAIRS)
FAR_TILES = tiles_of(((0, 1), (2, 3), (12, 13), (14, 15)), ((1, 2), (3, 12), (13, 14)))


def pack_rows(place, at, tiles, q0_ref, q1_ref):
    even = place[1] == 0
    for index, (kind, d, (first, second)) in enumerate(tiles):
        a, b = at(kind, d, first), at(kind, d, second)
        head = iota(a.shape, 0) < 4
        up = jnp.where(head, flip(a), b)
        down = jnp.where(head, a, flip(b))
        q0_ref[index] = jnp.where(even, up, down).astype(BF16)
        q1_ref[index] = jnp.where(even, down, up).astype(BF16)


def pack_own_kernel(place, x_ref, b_ref, m_ref, q0_ref, q1_ref, token_ref):
    pack_rows(place, own_planes(x_ref, b_ref, m_ref), OWN_TILES, q0_ref, q1_ref)
    token_ref[...] = jnp.zeros(token_ref.shape, F32)


def pack_far_kernel(place, after_ref, r1_ref, r0_ref, q0_ref, q1_ref):
    pack_rows(place, borrowed_planes(place, r0_ref, r1_ref), FAR_TILES, q0_ref, q1_ref)


def unpack_rows(place, at, tiles, y0_ref, y1_ref, width, use):
    odd = place[1] == 1
    head = iota((8, width), 0) < 4
    for index, (kind, d, pair) in enumerate(tiles):
        low = jnp.where(odd, y0_ref[index].astype(F32), y1_ref[index].astype(F32))
        high = jnp.where(odd, y1_ref[index].astype(F32), y0_ref[index].astype(F32))
        for k, w in enumerate(pair):
            own = flip(at(kind, d, w))
            below = low if k == 0 else flip(low)
            above = flip(high) if k == 0 else high
            block = jnp.concatenate(
                [jnp.where(head, below, own), jnp.where(head, own, above)], axis=0
            )
            use(kind, d, w, block)


def fine_own_kernel(
    place, w_ref, wd_ref, bound_ref, hzy_ref, pair_ref, x_in, b_in, m_in, y0_ref, y1_ref,
    v0_ref, v1_ref, v2_ref, v3_ref, s_ref, b_ref, x_ref, u_ref, inv_ref, idle_ref, seam_ref, sc_ref,
):
    width = x_in.shape[-1]

    def keep(kind, d, w, block):
        if kind == "m":
            s_ref[w - 4] = scale_rows(block)
        else:
            (x_ref if kind == "x" else b_ref)[w - 4, ROWS * d : ROWS * (d + 1)] = block

    unpack_rows(
        place, own_planes(x_in, b_in, m_in), OWN_TILES, y0_ref, y1_ref, width, keep
    )
    for z in range(8):
        v0_ref[z] = shifted_nodes(x_ref[z], width)

    def scales(layer):
        return s_ref[layer - 4]

    planes_of(
        5, 11, diagonal_operator(wd_ref, scales),
        inverter(inv_ref, idle_ref, bound_ref[0:1, 0:1], width, place[2], place[3], 12, 4),
    )
    levels = (v0_ref, v1_ref, v2_ref, v3_ref)
    for level, factors in enumerate(chebyshev_factors()):
        source, target = levels[level], levels[level + 1]

        def use(w, plane):
            z = w - 4
            update = None if level == 0 else u_ref[z]
            x_ref[z], u_ref[z] = advance(
                plane, b_ref[z], x_ref[z], update, inv_ref[z], idle_ref[z], factors
            )
            target[z] = shifted_nodes(x_ref[z], width)

        lo, hi = 5 + level, 10 - level
        product = layer_operator(w_ref, lambda w: source[w - 4], scales)
        first, last = product(lo - 1), product(hi)
        seam_ref[2 * level] = first[0 : 2 * BAND]
        seam_ref[2 * level + 1] = last[2 * BAND : 4 * BAND]
        planes_of(
            lo, hi, product, use, below=first[2 * BAND : 4 * BAND], above=last[0 : 2 * BAND]
        )
    counts = jnp.dot(
        hzy_ref[...], m_in[...].astype(F32).astype(BF16).reshape(64, width), preferred_element_type=F32
    )
    counts = jnp.dot(counts.astype(BF16), pair_ref[...], preferred_element_type=F32)
    sc_ref[...] = (0.25 * counts).reshape(sc_ref.shape)


def own_part(values, d, head):
    a = values[ROWS * d : ROWS * d + 8]
    b = values[ROWS * d + 8 : ROWS * d + 16]
    return flip(jnp.where(head, b, a))


def fine_rest_kernel(
    place, w_ref, wd_ref, bound_ref, wr_ref, rzy_ref, rx_ref,
    v0_in, v1_in, v2_in, v3_in, s_in, b_mid, x_in, u_in, inv_in, idle_in, seam_ref, sc_ref,
    b_in, r1_ref, r0_ref, y1_ref, y0_ref,
    out_ref, rhs_ref, q0_ref, q1_ref,
    v0_ref, v1_ref, v2_ref, v3_ref, s_ref, b_ref, x_ref, u_ref, inv_ref, idle_ref,
):
    width = b_in.shape[-1]

    def either(mid, far, lo, hi):
        return lambda w: mid[w - 4] if lo <= w <= hi else far[w]

    def keep(kind, d, w, block):
        if kind == "m":
            s_ref[w] = scale_rows(block)
        else:
            (x_ref if kind == "x" else b_ref)[w, ROWS * d : ROWS * (d + 1)] = block

    unpack_rows(
        place, borrowed_planes(place, r0_ref, r1_ref), FAR_TILES, y0_ref, y1_ref, width, keep
    )
    for w in (0, 1, 2, 3, 12, 13, 14, 15):
        v0_ref[w] = shifted_nodes(x_ref[w], width)
    scales = either(s_in, s_ref, 4, 11)
    invert = inverter(inv_ref, idle_ref, bound_ref[0:1, 0:1], width, place[2], place[3], 12)
    planes_of(1, 4, diagonal_operator(wd_ref, scales), invert)
    planes_of(12, 14, diagonal_operator(wd_ref, scales), invert)
    inverse, idles = either(inv_in, inv_ref, 5, 11), either(idle_in, idle_ref, 5, 11)
    loads = either(b_mid, b_ref, 4, 11)
    state = {w: (x_ref, u_ref, w) for w in range(16)}
    state.update({w: (x_in, u_in, w - 4) for w in range(4, 12)})
    near = (v0_in, v1_in, v2_in, v3_in)
    far = (v0_ref, v1_ref, v2_ref, v3_ref)
    all_factors = chebyshev_factors()

    def run(level, lo, hi, **seam):
        target = far[level + 1]

        def use(w, plane):
            xs, us, z = state[w]
            update = None if level == 0 else us[z]
            x_ref[w], u_ref[w] = advance(
                plane, loads(w), xs[z], update, inverse(w), idles(w), all_factors[level]
            )
            state[w] = (x_ref, u_ref, w)
            target[w] = shifted_nodes(x_ref[w], width)

        nodes = either(near[level], far[level], 4 + level, 11 - level)
        return plane_steps(lo, hi, layer_operator(w_ref, nodes, scales), use, **seam)

    low = [run(k, 1 + k, 4 + k, above=seam_ref[2 * k]) for k in range(CHEB)]
    high = [run(k, 11 - k, 14 - k, below=seam_ref[2 * k + 1]) for k in range(CHEB)]
    for k in range(CHEB):
        for _ in low[k]:
            pass
        for _ in high[k]:
            pass

    head = iota((8, width), 0) < 4
    parts = []

    def use(w, plane):
        idle = own_part(idles(w), 0, head)
        xs, _, z = state[w]
        final = xs[z]
        for d in range(3):
            x = own_part(final, d, head)
            out_ref[d, w - 4] = x
            parts.append(b_in[d, w - 4] - plane[8 * d : 8 * d + 8] - idle * x)

    planes_of(4, 11, layer_operator(wr_ref, either(near[3], far[3], 7, 8), scales), use, 24)
    residual = jnp.concatenate(parts, axis=0).astype(BF16)
    sums = jnp.dot(rzy_ref[...], residual, preferred_element_type=F32)
    sums = jnp.dot(sums.astype(BF16), rx_ref[...], preferred_element_type=F32)
    rhs_ref[...] = sums.reshape(rhs_ref.shape)
    even = 1 - place[0]
    for out, up in ((q0_ref, even), (q1_ref, 1 - even)):
        out[0:9] = rhs_ref[pl.ds(6 * up, 9)].astype(BF16)
        out[9:12] = sc_ref[pl.ds(up, 3)].astype(BF16)


def pack_coarse_kernel(place, rhs_ref, sc_ref, r1_ref, r0_ref, full_ref, q0_ref, q1_ref):
    odd = place[0] == 1
    even_y = place[1] == 0
    head = iota(rhs_ref.shape[1:], 0) < 4
    kept = []

    def low(i):
        return jnp.where(odd, r0_ref[i].astype(F32), r1_ref[i].astype(F32))

    def high(i):
        return jnp.where(odd, r1_ref[i].astype(F32), r0_ref[i].astype(F32))

    for z in range(10):
        c = z - 3
        for d in range(4):
            value = jnp.zeros(rhs_ref.shape[1:], F32)
            if d < 3:
                if -2 <= c <= 0:
                    value = value + low(3 * (c + 2) + d)
                if 4 <= c <= 6:
                    value = value + high(3 * (c - 4) + d)
                if 0 <= c <= 4:
                    value = value + rhs_ref[3 * c + d]
            else:
                if c <= -1:
                    value = low(9 + c + 3)
                elif c >= 4:
                    value = high(9 + c - 4)
                else:
                    value = sc_ref[c]
            full_ref[4 * z + d] = value
            kept.append(value)
    for i in range(20):
        a, b = kept[2 * i], kept[2 * i + 1]
        up = jnp.where(head, flip(a), b)
        down = jnp.where(head, pltpu.roll(a, 5, 0), pltpu.roll(b, 1, 0))
        q0_ref[i] = jnp.where(even_y, up, down).astype(BF16)
        q1_ref[i] = jnp.where(even_y, down, up).astype(BF16)


def coarse_kernel(
    place, w_ref, wd_ref, bound_ref, py_ref, px_ref, full_ref, y1_ref, y0_ref, smooth_ref, out_hbm,
    v_ref, v1_ref, v2_ref, s_ref, b_ref, x_ref, u_ref, inv_ref, idle_ref, out_ref, sem,
):
    half = full_ref.shape[-1]
    width = 2 * half
    bound = bound_ref[0:1, 0:1]
    odd = place[1] == 1
    rows8 = iota((8, half), 0)
    for z in range(10):
        for d in range(4):
            i = 4 * z + d
            low = jnp.where(odd, y0_ref[i // 2].astype(F32), y1_ref[i // 2].astype(F32))
            high = jnp.where(odd, y1_ref[i // 2].astype(F32), y0_ref[i // 2].astype(F32))
            if i % 2:
                low = flip(low)
            high = pltpu.roll(high, 3 if i % 2 else 7, 0)
            first = (
                full_ref[i] + jnp.where(rows8 < 4, low, 0.0) + jnp.where(rows8 == 7, high, 0.0)
            )
            block = jnp.concatenate([first, jnp.where(rows8 < 3, high, 0.0)], axis=0)
            if d < 3:
                b_ref[z, ROWS * d : ROWS * (d + 1)] = block
            else:
                s_ref[z] = scale_rows(block)
    def scales(layer):
        return s_ref[layer]

    factors = chebyshev_factors()
    levels = (v_ref, v1_ref, v2_ref)
    invert = inverter(inv_ref, idle_ref, bound, half, place[2], place[3], 7)

    def start(z, diag):
        invert(z, diag)
        update = factors[0][1] * (inv_ref[z] * b_ref[z])
        u_ref[z] = update
        x_ref[z] = update
        v_ref[z] = shifted_nodes(update, half)

    def run(level, lo, hi):
        def use(z, plane):
            x_ref[z], u_ref[z] = advance(
                plane, b_ref[z], x_ref[z], u_ref[z], inv_ref[z], idle_ref[z], factors[level]
            )
            levels[level][z] = shifted_nodes(x_ref[z], half)

        nodes = levels[level - 1]
        return plane_steps(lo, hi, layer_operator(w_ref, lambda z: nodes[z], scales), use)

    steps = (
        plane_steps(1, 9, diagonal_operator(wd_ref, scales), start), run(1, 2, 8), run(2, 3, 7)
    )
    for k in (0,) * 9 + (1,) * 7 + (2,) * 5:
        next(steps[k])

    coarse = jnp.concatenate([v2_ref[3 + k, 0:BAND] for k in range(5)], axis=0)
    rows = jnp.dot(py_ref[...], coarse, preferred_element_type=F32)
    wide = jnp.dot(rows.astype(BF16), px_ref[...], preferred_element_type=F32)
    wide = wide.reshape(5, 3, 8, width)
    copies = []
    for z in range(8):
        k = z // 2
        plane = wide[k] if z % 2 == 0 else 0.5 * (wide[k] + wide[k + 1])
        out_ref[z] = smooth_ref[:, z] + plane
        copies.append(pltpu.make_async_copy(out_ref.at[z], out_hbm.at[:, z], sem.at[z]))
        copies[-1].start()
    for copy in copies:
        copy.wait()


def swap(array, axis, offset):
    length = lax.axis_size(axis)
    pairs = []
    for i in range(offset, length - 1, 2):
        pairs += [(i, i + 1), (i + 1, i)]
    return lax.ppermute(array, axis, pairs)


def whereabouts():
    gz, gy = lax.axis_index("gz"), lax.axis_index("gy")
    return (
        lax.rem(gz, 2),
        lax.rem(gy, 2),
        (gz == lax.axis_size("gz") - 1).astype(jnp.int32),
        (gy == lax.axis_size("gy") - 1).astype(jnp.int32),
    )


def call(
    body, out_shape, n_in, scratch=(), name=None, place=True, space=pltpu.VMEM, out_space=pltpu.VMEM
):
    vmem = pl.BlockSpec(memory_space=out_space)
    single = not isinstance(out_shape, (tuple, list))
    return pl.pallas_call(
        (lambda *refs: body(whereabouts(), *refs)) if place else body,
        out_shape=out_shape,
        in_specs=[pl.BlockSpec(memory_space=space)] * n_in,
        out_specs=vmem if single else [vmem] * len(out_shape),
        scratch_shapes=list(scratch),
        compiler_params=pltpu.CompilerParams(vmem_limit_bytes=24 << 20),
        name=name,
    )


def body(applied_load, start_field, bone_mask, element_stiffness):
    width = applied_load.shape[-1]
    half = width // 2
    shape = jax.ShapeDtypeStruct
    packet = shape((25, 8, width), BF16)
    arguments = (start_field, applied_load, bone_mask, element_stiffness)
    q0, q1, start_field, applied_load, bone_mask, stiff = call(
        pack_z_kernel,
        [packet, packet] + [shape(a.shape, a.dtype) for a in arguments],
        4,
        [pltpu.SemaphoreType.DMA((8,))],
        name="pack_z",
        space=pltpu.HBM,
    )(*[pltpu.with_memory_space_constraint(a, pltpu.HBM) for a in arguments])
    r1 = swap(q1, "gz", 1)
    r0 = swap(q0, "gz", 0)
    packet = shape((len(OWN_TILES), 8, width), BF16)
    q0, q1, token = call(
        pack_own_kernel, [packet, packet, shape((8, 128), F32)], 3, name="pack_own"
    )(start_field, applied_load, bone_mask)
    yn1 = swap(q1, "gy", 1)
    yn0 = swap(q0, "gy", 0)
    w, wd, bound, wr, rzy, hzy, py, rx, px, pair = call(
        matrices_kernel,
        [
            shape((4 * BAND, 8 * BAND), BF16),
            shape((4 * BAND, 2 * ROWS), BF16),
            shape((8, 128), F32),
            shape((2 * BAND, 8 * BAND), BF16),
            shape((120, 192), BF16),
            shape((32, 64), BF16),
            shape((120, 240), BF16),
            shape((width, half), BF16),
            shape((half, width), BF16),
            shape((width, half), BF16),
        ],
        2,
        name="matrices",
        place=False,
    )(stiff, token)

    packet = shape((len(FAR_TILES), 8, width), BF16)
    q0, q1 = call(pack_far_kernel, [packet, packet], 3, name="pack_far")(bound, r1, r0)
    yf1 = swap(q1, "gy", 1)
    yf0 = swap(q0, "gy", 0)
    def field(count, rows, dtype):
        return (count, rows, width), dtype

    kinds = [(2 * BAND, BF16)] * 4 + [(2 * ROWS, BF16)] + [(BAND, F32)] * 4 + [(ROWS, F32)]
    *middle, scale = call(
        fine_own_kernel,
        [shape(*field(8, *kind)) for kind in kinds]
        + [shape(*field(6, 2 * BAND, F32)), shape((4, 8, half), F32)],
        10,
        name="fine_own",
    )(w, wd, bound, hzy, pair, start_field, applied_load, bone_mask, yn0, yn1)
    packet = shape((12, 8, half), BF16)
    smoothed, rhs, q0, q1 = call(
        fine_rest_kernel,
        [shape(start_field.shape, F32), shape((15, 8, half), F32), packet, packet],
        23,
        [pltpu.VMEM(*field(16, *kind)) for kind in kinds],
        name="fine_rest",
    )(w, wd, bound, wr, rzy, rx, *middle, scale, applied_load, r1, r0, yf1, yf0)
    r1 = swap(q1, "gz", 1)
    r0 = swap(q0, "gz", 0)
    packet = shape((20, 8, half), BF16)
    full, q0, q1 = call(
        pack_coarse_kernel,
        [shape((40, 8, half), F32), packet, packet],
        4,
        name="pack_coarse",
    )(rhs, scale, r1, r0)
    y1 = swap(q1, "gy", 1)
    y0 = swap(q0, "gy", 0)
    coarse_plane = pltpu.VMEM((11, BAND, half), F32)
    return call(
        coarse_kernel,
        shape(start_field.shape, F32),
        9,
        [
            pltpu.VMEM((11, 2 * BAND, half), BF16),
            pltpu.VMEM((11, 2 * BAND, half), BF16),
            pltpu.VMEM((11, 2 * BAND, half), BF16),
            pltpu.VMEM((11, 2 * ROWS, half), BF16),
            coarse_plane,
            coarse_plane,
            coarse_plane,
            coarse_plane,
            pltpu.VMEM((11, ROWS, half), F32),
            pltpu.VMEM((8, 3, 8, width), F32),
            pltpu.SemaphoreType.DMA((8,)),
        ],
        name="coarse",
        out_space=pltpu.HBM,
    )(w, wd, bound, py, px, full, y1, y0, smoothed)


def solution(mesh):
    in_specs = (P(None, "gz", "gy", None), P(None, "gz", "gy", None), P("gz", "gy", None), P())
    out_specs = P(None, "gz", "gy", None)
    return jax.shard_map(body, mesh=mesh, in_specs=in_specs, out_specs=out_specs, check_vma=False)
```

```python
import jax
import jax.numpy as jnp
from jax import lax
from jax.sharding import PartitionSpec as P
from jax.experimental import pallas as pl
from jax.experimental.pallas import tpu as pltpu

F32 = jnp.float32
BF16 = jnp.bfloat16
CHEB = 3
LOW = 0.1
MID = 0.5 * (1.0 + LOW)
HALF = 0.5 * (1.0 - LOW)
RATIO = (1.0 + LOW) / (1.0 - LOW)
ROWS = 16
BAND = 3 * ROWS
DEEP = 4


def iota(shape, dim):
    return lax.broadcasted_iota(jnp.int32, shape, dim)


def build_matrices(stiff):
    m = 4 * BAND
    row_m = iota((m, 24), 0)
    base_row = 12 * (row_m // (2 * BAND)) + 3 * ((row_m // BAND) % 2) + (row_m // ROWS) % 3
    col_e = iota((m, 24), 1)
    row_k = iota((24, m), 0)
    col_k = iota((24, m), 1)
    base_col = 6 * (col_k // (2 * BAND)) + 3 * ((col_k // BAND) % 2) + (col_k // ROWS) % 3
    mm = iota((m, m), 0)
    kk = iota((m, m), 1)
    gap = (mm % ROWS) - (kk % ROWS) + kk // (2 * BAND)
    blocks = []
    left = []
    for cy in range(2):
        pick = (col_e == base_row + 6 * cy).astype(BF16)
        left.append(jnp.dot(pick, stiff, preferred_element_type=F32).astype(BF16))
    for p in range(2):
        pick = (row_k == base_col + 12 * p).astype(BF16)
        block = jnp.zeros((m, m), F32)
        for cy in range(2):
            full = jnp.dot(left[cy], pick, preferred_element_type=F32)
            block = jnp.where(gap == cy, full, block)
        blocks.append(block.astype(BF16))
    md = iota((m, 2 * ROWS), 0)
    kd = iota((m, 2 * ROWS), 1)
    diag = jnp.zeros((m, 2 * ROWS), F32)
    for cy in range(2):
        own = jnp.sum(
            jnp.where(col_e == base_row + 6 * cy, left[cy].astype(F32), 0.0), axis=1, keepdims=True
        )
        diag = jnp.where((kd // ROWS == cy) & (kd % ROWS == md % ROWS), own, diag)
    return jnp.concatenate(blocks, axis=1), diag.astype(BF16)


def spectral_bound(stiff):
    wide = stiff.astype(F32)
    eye = iota((24, 24), 0) == iota((24, 24), 1)
    own = jnp.sum(jnp.where(eye, wide, 0.0), axis=1, keepdims=True)
    total = jnp.sum(jnp.abs(wide), axis=1, keepdims=True)
    return jnp.max(total / own, axis=0, keepdims=True)


def shift_up(values, width):
    rolled = pltpu.roll(values, width - 1, 1)
    return jnp.where(iota(values.shape, 1) == width - 1, 0.0, rolled)


def shift_down(values):
    rolled = pltpu.roll(values, 1, 1)
    return jnp.where(iota(values.shape, 1) == 0, 0.0, rolled)


def shifted_nodes(values, width):
    return jnp.concatenate([values.astype(BF16), shift_up(values, width).astype(BF16)], axis=0)


def scale_rows(scale):
    down = pltpu.roll(scale, 1, 0)
    down = jnp.where(iota(scale.shape, 0) == 0, 0.0, down)
    return jnp.concatenate([scale.astype(BF16), down.astype(BF16)], axis=0)


def half_of(matrix_ref, half):
    if half is None:
        return matrix_ref[...]
    rows = matrix_ref.shape[0] // 2
    return matrix_ref[half * rows : (half + 1) * rows]


def layer_operator(w_ref, nodes, scales):
    def product(layer, half=None):
        scale = scales(layer)
        width = scale.shape[-1]
        parts = []
        for p in range(2):
            plane = nodes(layer + p).reshape(6, ROWS, width)
            for cy in range(2):
                masked = plane * scale[cy * ROWS : (cy + 1) * ROWS][None]
                parts.append(masked.reshape(2 * BAND, width))
        matrix = half_of(w_ref, half)
        return jnp.dot(matrix, jnp.concatenate(parts, axis=0), preferred_element_type=F32)

    return product


def diagonal_operator(wd_ref, scales):
    def product(layer, half=None):
        return jnp.dot(half_of(wd_ref, half), scales(layer), preferred_element_type=F32)

    return product


def plane_steps(lo, hi, product, use, band=BAND, below=None, above=None):
    carry = product(lo - 1, 1) if below is None else below
    for z in range(lo, hi + 1):
        if z < hi:
            both = product(z)
            part, rest = both[0 : 2 * band], both[2 * band : 4 * band]
        else:
            part, rest = product(z, 0) if above is None else above, None
        plane = part + carry
        carry = rest
        use(z, plane[0:band] + shift_down(plane[band : 2 * band]))
        yield


def planes_of(*args, **options):
    for _ in plane_steps(*args, **options):
        pass


def inverter(inv_ref, idle_ref, bound, width, past_z, past_y, first, base=0):
    rows = iota((BAND, width), 0) % ROWS
    keep_y = jnp.where((rows >= first) & (past_y == 1), 0.0, 1.0)

    def use(z, diag):
        idle = (diag == 0.0).astype(F32)
        inverse = keep_y / ((diag + idle) * bound)
        if z >= first:
            inverse = inverse * jnp.where(past_z == 1, 0.0, 1.0)
        inv_ref[z - base] = inverse
        idle_ref[z - base] = idle[0:ROWS]

    return use


def tile3(values):
    return jnp.concatenate([values, values, values], axis=0)


def advance(plane, b, x, update, inverse, idle, factors):
    previous, current = factors
    new = current * (inverse * (b - plane - tile3(idle) * x))
    if previous is not None:
        new = previous * update + new
    return x + new, new


def chebyshev_factors():
    factors = [(None, 1.0 / MID)]
    rho = 1.0 / RATIO
    for _ in range(CHEB - 1):
        nxt = 1.0 / (2.0 * RATIO - rho)
        factors.append((nxt * rho, 2.0 * nxt / HALF))
        rho = nxt
    return factors


def weights(gap, where):
    value = jnp.where(gap == 0, 1.0, jnp.where(gap == 1, 0.5, 0.0))
    return jnp.where(where, value, 0.0)


def own_rows(w_ref):
    groups = [w_ref[ROWS * g : ROWS * (g + 1)].astype(F32)[4:12] for g in range(12)]
    return jnp.concatenate(groups, axis=0).astype(BF16)


def restrict_planes():
    out, src = iota((120, 192), 0), iota((120, 192), 1)
    gap_z = jnp.abs(src // 24 - 2 * (out // 24))
    gap_y = jnp.abs(src % 8 - 2 * (out % 8 - 3))
    same = (src // 8) % 3 == (out // 8) % 3
    return (weights(gap_z, same) * weights(gap_y, same)).astype(BF16)


def halve_planes():
    out, src = iota((32, 64), 0), iota((32, 64), 1)
    same = (src // 16 == out // 8) & ((src % 8) // 2 == out % 8 - 3)
    return same.astype(F32).astype(BF16)


def prolong_rows():
    out, src = iota((120, 240), 0), iota((120, 240), 1)
    gap = jnp.abs(out % 8 - 2 * (src % ROWS - 3))
    same = (out // 24 == src // BAND) & ((out // 8) % 3 == (src // ROWS) % 3)
    return weights(gap, same).astype(BF16)


def matrices_kernel(
    e_ref, token_ref, w_ref, wd_ref, bound_ref, wr_ref, rzy_ref, hzy_ref, py_ref, rx_ref, px_ref, pair_ref
):
    stiff = e_ref[...]
    w_ref[...], wd_ref[...] = build_matrices(stiff)
    bound_ref[...] = jnp.broadcast_to(spectral_bound(stiff), (8, 128))
    wr_ref[...] = own_rows(w_ref)
    rzy_ref[...] = restrict_planes()
    hzy_ref[...] = halve_planes()
    py_ref[...] = prolong_rows()
    fine, coarse = iota(rx_ref.shape, 0), iota(rx_ref.shape, 1)
    rx_ref[...] = weights(jnp.abs(fine - 2 * coarse), fine >= 0).astype(BF16)
    pair_ref[...] = (fine // 2 == coarse).astype(F32).astype(BF16)
    coarse, fine = iota(px_ref.shape, 0), iota(px_ref.shape, 1)
    px_ref[...] = weights(jnp.abs(fine - 2 * coarse), fine >= 0).astype(BF16)


def pack_z_kernel(
    place, x_hbm, b_hbm, m_hbm, e_hbm, q0_ref, q1_ref, x_ref, b_ref, m_ref, e_ref, sem
):
    even = 1 - place[0]
    pairs = []
    for d in range(3):
        pairs += [(x_hbm.at[d], x_ref.at[d])]
    for d in range(3):
        pairs += [(b_hbm.at[d], b_ref.at[d])]
    pairs += [(m_hbm, m_ref), (e_hbm, e_ref)]
    copies = [pltpu.make_async_copy(src, dst, sem.at[i]) for i, (src, dst) in enumerate(pairs)]
    for copy in copies:
        copy.start()
    outs = ((q0_ref, even), (q1_ref, 1 - even))
    for d in range(3):
        copies[d].wait()
        for out, up in outs:
            out[4 * d : 4 * d + 4] = x_ref[d, pl.ds(4 * up, 4)].astype(BF16)
    for d in range(3):
        copies[3 + d].wait()
        for out, up in outs:
            out[12 + 3 * d : 15 + 3 * d] = b_ref[d, pl.ds(5 * up, 3)].astype(BF16)
    copies[6].wait()
    for out, up in outs:
        out[21:25] = m_ref[pl.ds(4 * up, 4)].astype(F32).astype(BF16)
    copies[7].wait()


def own_planes(x_ref, b_ref, m_ref):
    def at(kind, d, w):
        if kind == "m":
            return m_ref[w - 4].astype(F32)
        return (x_ref if kind == "x" else b_ref)[d, w - 4]

    return at


def borrowed_planes(place, r0_ref, r1_ref):
    odd = place[0] == 1

    def at(kind, d, w):
        low = w < 4
        if kind == "x":
            i = 4 * d + w % 4
        elif kind == "b":
            i = 12 + 3 * d + (w - 1 if low else w - 12)
        else:
            i = 21 + w % 4
        first, second = (r0_ref, r1_ref) if low else (r1_ref, r0_ref)
        return jnp.where(odd, first[i].astype(F32), second[i].astype(F32))

    return at


def flip(values):
    return pltpu.roll(values, 4, 0)


def tiles_of(pairs, load_pairs):
    return (
        [("x", d, pair) for d in range(3) for pair in pairs]
        + [("b", d, pair) for d in range(3) for pair in load_pairs]
        + [("m", 0, pair) for pair in pairs]
    )


OWN_PAIRS = ((4, 5), (6, 7), (8, 9), (10, 11))
OWN_TILES = tiles_of(OWN_PAIRS, OWN_PAIRS)
FAR_TILES = tiles_of(((0, 1), (2, 3), (12, 13), (14, 15)), ((1, 2), (3, 12), (13, 14)))


def pack_rows(place, at, tiles, q0_ref, q1_ref):
    even = place[1] == 0
    for index, (kind, d, (first, second)) in enumerate(tiles):
        a, b = at(kind, d, first), at(kind, d, second)
        head = iota(a.shape, 0) < 4
        up = jnp.where(head, flip(a), b)
        down = jnp.where(head, a, flip(b))
        q0_ref[index] = jnp.where(even, up, down).astype(BF16)
        q1_ref[index] = jnp.where(even, down, up).astype(BF16)


def pack_own_kernel(place, x_ref, b_ref, m_ref, q0_ref, q1_ref, token_ref):
    pack_rows(place, own_planes(x_ref, b_ref, m_ref), OWN_TILES, q0_ref, q1_ref)
    token_ref[...] = jnp.zeros(token_ref.shape, F32)


def pack_far_kernel(place, after_ref, r1_ref, r0_ref, q0_ref, q1_ref):
    pack_rows(place, borrowed_planes(place, r0_ref, r1_ref), FAR_TILES, q0_ref, q1_ref)


def unpack_rows(place, at, tiles, y0_ref, y1_ref, width, use):
    odd = place[1] == 1
    head = iota((8, width), 0) < 4
    for index, (kind, d, pair) in enumerate(tiles):
        low = jnp.where(odd, y0_ref[index].astype(F32), y1_ref[index].astype(F32))
        high = jnp.where(odd, y1_ref[index].astype(F32), y0_ref[index].astype(F32))
        for k, w in enumerate(pair):
            own = flip(at(kind, d, w))
            below = low if k == 0 else flip(low)
            above = flip(high) if k == 0 else high
            block = jnp.concatenate(
                [jnp.where(head, below, own), jnp.where(head, own, above)], axis=0
            )
            use(kind, d, w, block)


def fine_own_kernel(
    place, w_ref, wd_ref, bound_ref, hzy_ref, pair_ref, x_in, b_in, m_in, y1_ref, y0_ref,
    v0_ref, v1_ref, v2_ref, v3_ref, s_ref, b_ref, x_ref, u_ref, inv_ref, idle_ref, seam_ref, sc_ref,
):
    width = x_in.shape[-1]

    def keep(kind, d, w, block):
        if kind == "m":
            s_ref[w - 4] = scale_rows(block)
        else:
            (x_ref if kind == "x" else b_ref)[w - 4, ROWS * d : ROWS * (d + 1)] = block

    unpack_rows(
        place, own_planes(x_in, b_in, m_in), OWN_TILES, y0_ref, y1_ref, width, keep
    )
    for z in range(8):
        v0_ref[z] = shifted_nodes(x_ref[z], width)

    def scales(layer):
        return s_ref[layer - 4]

    planes_of(
        5, 11, diagonal_operator(wd_ref, scales),
        inverter(inv_ref, idle_ref, bound_ref[0:1, 0:1], width, place[2], place[3], 12, 4),
    )
    levels = (v0_ref, v1_ref, v2_ref, v3_ref)
    for level, factors in enumerate(chebyshev_factors()):
        source, target = levels[level], levels[level + 1]

        def use(w, plane):
            z = w - 4
            update = None if level == 0 else u_ref[z]
            x_ref[z], u_ref[z] = advance(
                plane, b_ref[z], x_ref[z], update, inv_ref[z], idle_ref[z], factors
            )
            target[z] = shifted_nodes(x_ref[z], width)

        lo, hi = 5 + level, 10 - level
        product = layer_operator(w_ref, lambda w: source[w - 4], scales)
        first, last = product(lo - 1), product(hi)
        seam_ref[2 * level] = first[0 : 2 * BAND]
        seam_ref[2 * level + 1] = last[2 * BAND : 4 * BAND]
        planes_of(
            lo, hi, product, use, below=first[2 * BAND : 4 * BAND], above=last[0 : 2 * BAND]
        )
    counts = jnp.dot(
        hzy_ref[...], m_in[...].astype(F32).astype(BF16).reshape(64, width), preferred_element_type=F32
    )
    counts = jnp.dot(counts.astype(BF16), pair_ref[...], preferred_element_type=F32)
    sc_ref[...] = (0.25 * counts).reshape(sc_ref.shape)


def own_part(values, d, head):
    a = values[ROWS * d : ROWS * d + 8]
    b = values[ROWS * d + 8 : ROWS * d + 16]
    return flip(jnp.where(head, b, a))


def fine_rest_kernel(
    place, w_ref, wd_ref, bound_ref, wr_ref, rzy_ref, rx_ref,
    v0_in, v1_in, v2_in, v3_in, s_in, b_mid, x_in, u_in, inv_in, idle_in, seam_ref, sc_ref,
    b_in, r1_ref, r0_ref, y1_ref, y0_ref,
    out_ref, rhs_ref, q0_ref, q1_ref,
    v0_ref, v1_ref, v2_ref, v3_ref, s_ref, b_ref, x_ref, u_ref, inv_ref, idle_ref,
):
    width = b_in.shape[-1]

    def either(mid, far, lo, hi):
        return lambda w: mid[w - 4] if lo <= w <= hi else far[w]

    def keep(kind, d, w, block):
        if kind == "m":
            s_ref[w] = scale_rows(block)
        else:
            (x_ref if kind == "x" else b_ref)[w, ROWS * d : ROWS * (d + 1)] = block

    unpack_rows(
        place, borrowed_planes(place, r0_ref, r1_ref), FAR_TILES, y0_ref, y1_ref, width, keep
    )
    for w in (0, 1, 2, 3, 12, 13, 14, 15):
        v0_ref[w] = shifted_nodes(x_ref[w], width)
    scales = either(s_in, s_ref, 4, 11)
    invert = inverter(inv_ref, idle_ref, bound_ref[0:1, 0:1], width, place[2], place[3], 12)
    planes_of(1, 4, diagonal_operator(wd_ref, scales), invert)
    planes_of(12, 14, diagonal_operator(wd_ref, scales), invert)
    inverse, idles = either(inv_in, inv_ref, 5, 11), either(idle_in, idle_ref, 5, 11)
    loads = either(b_mid, b_ref, 4, 11)
    state = {w: (x_ref, u_ref, w) for w in range(16)}
    state.update({w: (x_in, u_in, w - 4) for w in range(4, 12)})
    near = (v0_in, v1_in, v2_in, v3_in)
    far = (v0_ref, v1_ref, v2_ref, v3_ref)
    all_factors = chebyshev_factors()

    def run(level, lo, hi, **seam):
        target = far[level + 1]

        def use(w, plane):
            xs, us, z = state[w]
            update = None if level == 0 else us[z]
            x_ref[w], u_ref[w] = advance(
                plane, loads(w), xs[z], update, inverse(w), idles(w), all_factors[level]
            )
            state[w] = (x_ref, u_ref, w)
            target[w] = shifted_nodes(x_ref[w], width)

        nodes = either(near[level], far[level], 4 + level, 11 - level)
        return plane_steps(lo, hi, layer_operator(w_ref, nodes, scales), use, **seam)

    low = [run(k, 1 + k, 4 + k, above=seam_ref[2 * k]) for k in range(CHEB)]
    high = [run(k, 11 - k, 14 - k, below=seam_ref[2 * k + 1]) for k in range(CHEB)]
    for k in range(CHEB):
        for _ in low[k]:
            pass
        for _ in high[k]:
            pass

    head = iota((8, width), 0) < 4
    parts = []

    def use(w, plane):
        idle = own_part(idles(w), 0, head)
        xs, _, z = state[w]
        final = xs[z]
        for d in range(3):
            x = own_part(final, d, head)
            out_ref[d, w - 4] = x
            parts.append(b_in[d, w - 4] - plane[8 * d : 8 * d + 8] - idle * x)

    planes_of(4, 11, layer_operator(wr_ref, either(near[3], far[3], 7, 8), scales), use, 24)
    residual = jnp.concatenate(parts, axis=0).astype(BF16)
    sums = jnp.dot(rzy_ref[...], residual, preferred_element_type=F32)
    sums = jnp.dot(sums.astype(BF16), rx_ref[...], preferred_element_type=F32)
    rhs_ref[...] = sums.reshape(rhs_ref.shape)
    even = 1 - place[0]
    for out, up in ((q0_ref, even), (q1_ref, 1 - even)):
        out[0:9] = rhs_ref[pl.ds(6 * up, 9)].astype(BF16)
        out[9:12] = sc_ref[pl.ds(up, 3)].astype(BF16)


def pack_coarse_kernel(place, rhs_ref, sc_ref, r1_ref, r0_ref, full_ref, q0_ref, q1_ref):
    odd = place[0] == 1
    even_y = place[1] == 0
    head = iota(rhs_ref.shape[1:], 0) < 4
    kept = []

    def low(i):
        return jnp.where(odd, r0_ref[i].astype(F32), r1_ref[i].astype(F32))

    def high(i):
        return jnp.where(odd, r1_ref[i].astype(F32), r0_ref[i].astype(F32))

    for z in range(10):
        c = z - 3
        for d in range(4):
            value = jnp.zeros(rhs_ref.shape[1:], F32)
            if d < 3:
                if -2 <= c <= 0:
                    value = value + low(3 * (c + 2) + d)
                if 4 <= c <= 6:
                    value = value + high(3 * (c - 4) + d)
                if 0 <= c <= 4:
                    value = value + rhs_ref[3 * c + d]
            else:
                if c <= -1:
                    value = low(9 + c + 3)
                elif c >= 4:
                    value = high(9 + c - 4)
                else:
                    value = sc_ref[c]
            full_ref[4 * z + d] = value
            kept.append(value)
    for i in range(20):
        a, b = kept[2 * i], kept[2 * i + 1]
        up = jnp.where(head, flip(a), b)
        down = jnp.where(head, pltpu.roll(a, 5, 0), pltpu.roll(b, 1, 0))
        q0_ref[i] = jnp.where(even_y, up, down).astype(BF16)
        q1_ref[i] = jnp.where(even_y, down, up).astype(BF16)


def coarse_kernel(
    place, w_ref, wd_ref, bound_ref, py_ref, px_ref, full_ref, y1_ref, y0_ref, smooth_ref, out_hbm,
    v_ref, v1_ref, v2_ref, s_ref, b_ref, x_ref, u_ref, inv_ref, idle_ref, out_ref, sem,
):
    half = full_ref.shape[-1]
    width = 2 * half
    bound = bound_ref[0:1, 0:1]
    odd = place[1] == 1
    rows8 = iota((8, half), 0)
    for z in range(10):
        for d in range(4):
            i = 4 * z + d
            low = jnp.where(odd, y0_ref[i // 2].astype(F32), y1_ref[i // 2].astype(F32))
            high = jnp.where(odd, y1_ref[i // 2].astype(F32), y0_ref[i // 2].astype(F32))
            if i % 2:
                low = flip(low)
            high = pltpu.roll(high, 3 if i % 2 else 7, 0)
            first = (
                full_ref[i] + jnp.where(rows8 < 4, low, 0.0) + jnp.where(rows8 == 7, high, 0.0)
            )
            block = jnp.concatenate([first, jnp.where(rows8 < 3, high, 0.0)], axis=0)
            if d < 3:
                b_ref[z, ROWS * d : ROWS * (d + 1)] = block
            else:
                s_ref[z] = scale_rows(block)
    def scales(layer):
        return s_ref[layer]

    factors = chebyshev_factors()
    levels = (v_ref, v1_ref, v2_ref)
    invert = inverter(inv_ref, idle_ref, bound, half, place[2], place[3], 7)

    def start(z, diag):
        invert(z, diag)
        update = factors[0][1] * (inv_ref[z] * b_ref[z])
        u_ref[z] = update
        x_ref[z] = update
        v_ref[z] = shifted_nodes(update, half)

    def run(level, lo, hi):
        def use(z, plane):
            x_ref[z], u_ref[z] = advance(
                plane, b_ref[z], x_ref[z], u_ref[z], inv_ref[z], idle_ref[z], factors[level]
            )
            levels[level][z] = shifted_nodes(x_ref[z], half)

        nodes = levels[level - 1]
        return plane_steps(lo, hi, layer_operator(w_ref, lambda z: nodes[z], scales), use)

    steps = (
        plane_steps(1, 9, diagonal_operator(wd_ref, scales), start), run(1, 2, 8), run(2, 3, 7)
    )
    for k in (0,) * 9 + (1,) * 7 + (2,) * 5:
        next(steps[k])

    coarse = jnp.concatenate([v2_ref[3 + k, 0:BAND] for k in range(5)], axis=0)
    rows = jnp.dot(py_ref[...], coarse, preferred_element_type=F32)
    wide = jnp.dot(rows.astype(BF16), px_ref[...], preferred_element_type=F32)
    wide = wide.reshape(5, 3, 8, width)
    copies = []
    for z in range(8):
        k = z // 2
        plane = wide[k] if z % 2 == 0 else 0.5 * (wide[k] + wide[k + 1])
        out_ref[z] = smooth_ref[:, z] + plane
        copies.append(pltpu.make_async_copy(out_ref.at[z], out_hbm.at[:, z], sem.at[z]))
        copies[-1].start()
    for copy in copies:
        copy.wait()


def swap(array, axis, offset):
    length = lax.axis_size(axis)
    pairs = []
    for i in range(offset, length - 1, 2):
        pairs += [(i, i + 1), (i + 1, i)]
    return lax.ppermute(array, axis, pairs)


def whereabouts():
    gz, gy = lax.axis_index("gz"), lax.axis_index("gy")
    return (
        lax.rem(gz, 2),
        lax.rem(gy, 2),
        (gz == lax.axis_size("gz") - 1).astype(jnp.int32),
        (gy == lax.axis_size("gy") - 1).astype(jnp.int32),
    )


def call(
    body, out_shape, n_in, scratch=(), name=None, place=True, space=pltpu.VMEM, out_space=pltpu.VMEM
):
    vmem = pl.BlockSpec(memory_space=out_space)
    single = not isinstance(out_shape, (tuple, list))
    return pl.pallas_call(
        (lambda *refs: body(whereabouts(), *refs)) if place else body,
        out_shape=out_shape,
        in_specs=[pl.BlockSpec(memory_space=space)] * n_in,
        out_specs=vmem if single else [vmem] * len(out_shape),
        scratch_shapes=list(scratch),
        compiler_params=pltpu.CompilerParams(vmem_limit_bytes=24 << 20),
        name=name,
    )


def body(applied_load, start_field, bone_mask, element_stiffness):
    width = applied_load.shape[-1]
    half = width // 2
    shape = jax.ShapeDtypeStruct
    packet = shape((25, 8, width), BF16)
    arguments = (start_field, applied_load, bone_mask, element_stiffness)
    q0, q1, start_field, applied_load, bone_mask, stiff = call(
        pack_z_kernel,
        [packet, packet] + [shape(a.shape, a.dtype) for a in arguments],
        4,
        [pltpu.SemaphoreType.DMA((8,))],
        name="pack_z",
        space=pltpu.HBM,
    )(*[pltpu.with_memory_space_constraint(a, pltpu.HBM) for a in arguments])
    r1 = swap(q1, "gz", 1)
    r0 = swap(q0, "gz", 0)
    packet = shape((len(OWN_TILES), 8, width), BF16)
    q0, q1, token = call(
        pack_own_kernel, [packet, packet, shape((8, 128), F32)], 3, name="pack_own"
    )(start_field, applied_load, bone_mask)
    yn1 = swap(q1, "gy", 1)
    yn0 = swap(q0, "gy", 0)
    w, wd, bound, wr, rzy, hzy, py, rx, px, pair = call(
        matrices_kernel,
        [
            shape((4 * BAND, 8 * BAND), BF16),
            shape((4 * BAND, 2 * ROWS), BF16),
            shape((8, 128), F32),
            shape((2 * BAND, 8 * BAND), BF16),
            shape((120, 192), BF16),
            shape((32, 64), BF16),
            shape((120, 240), BF16),
            shape((width, half), BF16),
            shape((half, width), BF16),
            shape((width, half), BF16),
        ],
        2,
        name="matrices",
        place=False,
    )(stiff, token)

    packet = shape((len(FAR_TILES), 8, width), BF16)
    q0, q1 = call(pack_far_kernel, [packet, packet], 3, name="pack_far")(bound, r1, r0)
    yf1 = swap(q1, "gy", 1)
    yf0 = swap(q0, "gy", 0)
    def field(count, rows, dtype):
        return (count, rows, width), dtype

    kinds = [(2 * BAND, BF16)] * 4 + [(2 * ROWS, BF16)] + [(BAND, F32)] * 4 + [(ROWS, F32)]
    *middle, scale = call(
        fine_own_kernel,
        [shape(*field(8, *kind)) for kind in kinds]
        + [shape(*field(6, 2 * BAND, F32)), shape((4, 8, half), F32)],
        10,
        name="fine_own",
    )(w, wd, bound, hzy, pair, start_field, applied_load, bone_mask, yn1, yn0)
    packet = shape((12, 8, half), BF16)
    smoothed, rhs, q0, q1 = call(
        fine_rest_kernel,
        [shape(start_field.shape, F32), shape((15, 8, half), F32), packet, packet],
        23,
        [pltpu.VMEM(*field(16, *kind)) for kind in kinds],
        name="fine_rest",
    )(w, wd, bound, wr, rzy, rx, *middle, scale, applied_load, r1, r0, yf1, yf0)
    r1 = swap(q1, "gz", 1)
    r0 = swap(q0, "gz", 0)
    packet = shape((20, 8, half), BF16)
    full, q0, q1 = call(
        pack_coarse_kernel,
        [shape((40, 8, half), F32), packet, packet],
        4,
        name="pack_coarse",
    )(rhs, scale, r1, r0)
    y1 = swap(q1, "gy", 1)
    y0 = swap(q0, "gy", 0)
    coarse_plane = pltpu.VMEM((11, BAND, half), F32)
    return call(
        coarse_kernel,
        shape(start_field.shape, F32),
        9,
        [
            pltpu.VMEM((11, 2 * BAND, half), BF16),
            pltpu.VMEM((11, 2 * BAND, half), BF16),
            pltpu.VMEM((11, 2 * BAND, half), BF16),
            pltpu.VMEM((11, 2 * ROWS, half), BF16),
            coarse_plane,
            coarse_plane,
            coarse_plane,
            coarse_plane,
            pltpu.VMEM((11, ROWS, half), F32),
            pltpu.VMEM((8, 3, 8, width), F32),
            pltpu.SemaphoreType.DMA((8,)),
        ],
        name="coarse",
        out_space=pltpu.HBM,
    )(w, wd, bound, py, px, full, y1, y0, smoothed)


def solution(mesh):
    in_specs = (P(None, "gz", "gy", None), P(None, "gz", "gy", None), P("gz", "gy", None), P())
    out_specs = P(None, "gz", "gy", None)
    return jax.shard_map(body, mesh=mesh, in_specs=in_specs, out_specs=out_specs, check_vma=False)
```
